32 devices in a mesh: groups: 2 (over x), tiles: 16 (over z, y, core).
Axes of the slice: x: 2, y: 2, z: 4, core: 2. Of those that a mesh axis runs over, the one named last changes fastest.
Arguments:
- features: bfloat16 [128, 8, 16, 256], P(('groups', 'tiles')), parts along dimension 0, may hold values from -6 to 6
- weight_one: bfloat16 [6912, 256], P('tiles'), may hold values from -0.078125 to 0.078125
- weight_two: bfloat16 [6912, 256], P('tiles'), may hold values from -0.078125 to 0.078125
- cotangent: bfloat16 [128, 8, 16, 256], P(('groups', 'tiles')), parts along dimension 0, may hold values from -6 to 6
- block_mask: int32 [32, 2, 4], P('groups'), parts along dimension 0, may hold values 0 or 1
Outputs:
- features_out: bfloat16 [128, 8, 16, 256], P(('groups', 'tiles')), parts along dimension 0
- grad_w1: float32 [13824, 256], P(('groups', 'tiles')), parts along dimension 0
- grad_w2: float32 [13824, 256], P(('groups', 'tiles')), parts along dimension 0
The draws below stay inside these ranges and needn't reach their ends.
There are 2 independent parts, one for each index of `groups`. The reference program is written for one: setup_inputs(seed, part) draws one part's arguments, and reference() takes and returns one part's arrays. A program takes and returns all parts, laid end to end along the dimension named above; an argument that names none is the same for every part. Nothing has to cross between parts.
All inputs are finite; a program needn't handle non-finite values.
Results may differ from the reference program's by a relative error of at most 0.0049.
Values may be sent and summed in bfloat16 or wider, within the bound.
No kernel may reach another device: no remote copies, remote signals or barrier semaphores. Data moves between devices by JAX's collectives and lax.ppermute only.
A program may use at most 128 MiB of HBM per device.

```python
import math
import jax
import jax.numpy as jnp
from jax import lax

C = 256
B = 4
GY = 2
GZ = 4
VX = 64
VY = 8
VZ = 16
N_TILES = 16


def set_ends(drawn, rng, low, top_value):
    longest = drawn.shape.index(max(drawn.shape))
    spots = []
    for shift in (0, 1):
        where = [jax.random.randint(jax.random.fold_in(rng, axis), (), 0, length) for axis, length in enumerate(drawn.shape)]
        where[longest] = (where[longest] + shift) % drawn.shape[longest]
        spots.append(tuple(where))
    return drawn.at[spots[0]].set(low).at[spots[1]].set(top_value)


def steps_of(own_key, dims, split, least, largest):
    level = 1.0
    for dim, shards_of in split:
        steps = jax.random.uniform(jax.random.fold_in(jax.random.fold_in(own_key, 6), dim), (shards_of,), jnp.float32, least / len(split), largest / len(split))
        level = level * jnp.repeat(jnp.exp(steps), dims[dim] // shards_of).reshape((-1,) + (1,) * (len(dims) - 1 - dim))
    return level


def centred(key, dims, scale, most, split=(), kind=jnp.bfloat16):
    drawn = jax.random.normal(key, dims, jnp.float32) * scale
    if len(split) > 0:
        drawn = steps_of(key, dims, split, -0.22, 0.18) * drawn
    return jnp.clip(drawn, min=-most, max=most).astype(kind)


def setup_inputs(seed: int = 0, part: int = 0) -> dict:
    keys = jax.random.split(jax.random.key(seed), 6)
    part_splits = jax.random.split(jax.random.fold_in(keys[5], part), 6)
    return {
        "features": centred(part_splits[0], (VX, VY, VZ, C), 1.0, 6.0, ((0, 16),)),
        "weight_one": centred(keys[1], (27 * C, C), (27 * C) ** -0.5, 0.078125, ((0, 16),)),
        "weight_two": centred(keys[2], (27 * C, C), (27 * C) ** -0.5, 0.078125, ((0, 16),)),
        "cotangent": centred(part_splits[3], (VX, VY, VZ, C), 1.0, 6.0, ((0, 16),)),
        "block_mask": set_ends((jax.random.randint(part_splits[4], (N_TILES, GY, GZ), 0, 5) < 3).astype(jnp.int32), jax.random.fold_in(part_splits[4], 1), 0, 1),
    }


def tap_columns(padded, flipped):
    extent = [padded.shape[d] - 2 for d in range(3)]
    taps = []
    for a in range(3):
        for b in range(3):
            for c in range(3):
                start_x = 2 - a if flipped else a
                start_y = 2 - b if flipped else b
                start_z = 2 - c if flipped else c
                taps.append(padded[start_x:start_x + extent[0], start_y:start_y + extent[1], start_z:start_z + extent[2]])
    stacked = jnp.stack(taps, axis=3)
    return stacked.reshape(extent[0] * extent[1] * extent[2], 27 * padded.shape[3])

def expand_mask(cells, edge):
    planes, rows_y, rows_z = cells.shape
    values = cells.astype(jnp.float32)
    values = jnp.broadcast_to(values[:, None, :, None, :, None], (planes, edge, rows_y, edge, rows_z, edge))
    return values.reshape(planes * edge, rows_y * edge, rows_z * edge, 1)

def silu_slope(values):
    logistic = jax.nn.sigmoid(values)
    return logistic * (1.0 + values * (1.0 - logistic))

def reference(features, weight_one, weight_two, cotangent, block_mask):
    voxel_mask = expand_mask(block_mask, B)
    slabs = jnp.arange(N_TILES, dtype=jnp.int32)
    weight_back = jnp.swapaxes(weight_two.reshape(27, C, C), 1, 2).reshape(27 * C, C)

    def padded_of(field):
        return jnp.pad(field, ((1, 1), (1, 1), (1, 1), (0, 0)))

    def slab_cols(padded, slab, flipped):
        piece = lax.dynamic_slice_in_dim(padded, (slab * B).astype(jnp.int32), B + 2, 0)
        return tap_columns(piece, flipped)

    def convolve(field, weight, flipped):
        padded = padded_of(field)

        def one_slab(slab):
            return jnp.dot(slab_cols(padded, slab, flipped), weight, preferred_element_type=jnp.float32)
        return lax.map(one_slab, slabs).reshape(VX, VY, VZ, C)
    inputs = (features * voxel_mask).astype(jnp.bfloat16)
    pre_one = convolve(inputs, weight_one, False)
    act = (jax.nn.silu(pre_one) * voxel_mask).astype(jnp.bfloat16)
    features_out = (convolve(act, weight_two, False) * voxel_mask).astype(jnp.bfloat16)
    cot = (cotangent * voxel_mask).astype(jnp.bfloat16)
    back = convolve(cot, weight_back, True)
    delta = (back * silu_slope(pre_one) * voxel_mask).astype(jnp.bfloat16)
    act_pad = padded_of(act)
    in_pad = padded_of(inputs)

    def accumulate(carry, slab):
        grad_one, grad_two = carry
        rows_cot = lax.dynamic_slice_in_dim(cot, (slab * B).astype(jnp.int32), B, 0).reshape(-1, C)
        rows_delta = lax.dynamic_slice_in_dim(delta, (slab * B).astype(jnp.int32), B, 0).reshape(-1, C)
        grad_two = grad_two + lax.dot_general(slab_cols(act_pad, slab, False), rows_cot, (((0,), (0,)), ((), ())), preferred_element_type=jnp.float32)
        grad_one = grad_one + lax.dot_general(slab_cols(in_pad, slab, False), rows_delta, (((0,), (0,)), ((), ())), preferred_element_type=jnp.float32)
        return ((grad_one, grad_two), None)
    zeros_init = jnp.zeros((27 * C, C), jnp.float32)
    (grad_one, grad_two), unused_out = lax.scan(accumulate, (zeros_init, zeros_init), slabs)
    loss_scale = 1.0 / math.sqrt(VX * VY * VZ)
    return (features_out, grad_one * loss_scale, grad_two * loss_scale)
```

```python
import functools
import math

import jax
import jax.numpy as jnp
from jax import lax
from jax.experimental import pallas as pl
from jax.experimental.pallas import tpu as pltpu
from jax.sharding import PartitionSpec as P

B = 4
RING = (0, 2, 4, 6, 7, 5, 3, 1)
BF = jnp.bfloat16
F32 = jnp.float32


def with_halo(block, axis, width):
    count = lax.axis_size(axis)
    forward = [(i, i + 1) for i in range(count - 1)]
    backward = [(target, source) for source, target in forward]
    low = lax.ppermute(block[-width:], axis, forward)
    high = lax.ppermute(block[:width], axis, backward)
    return low, high


def tap_columns(padded, flipped):
    extent = [padded.shape[d] - 2 for d in range(3)]
    taps = []
    for a in range(3):
        for b in range(3):
            for c in range(3):
                x, y, z = (2 - a, 2 - b, 2 - c) if flipped else (a, b, c)
                taps.append(padded[x : x + extent[0], y : y + extent[1], z : z + extent[2]])
    stacked = jnp.stack(taps, axis=3)
    return stacked.reshape(extent[0] * extent[1] * extent[2], 27 * padded.shape[3])


def expand_mask(cells, edge):
    planes, rows_y, rows_z = cells.shape
    values = jnp.broadcast_to(
        cells.astype(F32)[:, None, :, None, :, None], (planes, edge, rows_y, edge, rows_z, edge)
    )
    return values.reshape(planes * edge, rows_y * edge, rows_z * edge, 1)


def silu_slope(values):
    logistic = jax.nn.sigmoid(values)
    return logistic * (1.0 + values * (1.0 - logistic))


def near_cells_of(block_mask):
    padded_cells = jnp.pad(block_mask, ((1, 1), (0, 0), (0, 0)))
    return lax.dynamic_slice_in_dim(padded_cells, lax.axis_index("tiles"), 3, 0)


def on_any(features, weight_one, weight_two, cotangent, block_mask):
    depth, width_y, width_z, channels = features.shape
    loss_scale = 1.0 / math.sqrt(lax.axis_size("tiles") * depth * width_y * width_z)
    own_mask = expand_mask(near_cells_of(block_mask), B)[depth : 2 * depth]
    own_flat = own_mask.reshape(-1, 1)

    def cube(field):
        low, high = with_halo(field, "tiles", 1)
        field = jnp.concatenate([low, field, high], axis=0)
        return jnp.pad(field, ((0, 0), (1, 1), (1, 1), (0, 0)))

    def grad_piece(columns_in, rows_in):
        product = lax.dot_general(
            columns_in, rows_in, (((0,), (0,)), ((), ())), preferred_element_type=F32
        )
        return lax.psum_scatter(product * loss_scale, "tiles", scatter_dimension=0, tiled=True)

    full_one = lax.all_gather(weight_one, "tiles", axis=0, tiled=True)
    full_two = lax.all_gather(weight_two, "tiles", axis=0, tiled=True)
    weight_back = jnp.swapaxes(full_two.reshape(27, channels, channels), 1, 2).reshape(
        27 * channels, channels
    )
    inputs = (features * own_mask).astype(BF)
    feature_cols = tap_columns(cube(inputs), False)
    hidden_pre = jnp.dot(feature_cols, full_one, preferred_element_type=F32)
    active = (jax.nn.silu(hidden_pre) * own_flat).astype(BF).reshape(features.shape)
    active_cols = tap_columns(cube(active), False)
    second = jnp.dot(active_cols, full_two, preferred_element_type=F32)
    features_out = (second * own_flat).astype(BF).reshape(features.shape)
    cot = (cotangent * own_mask).astype(BF)
    grad_two = grad_piece(active_cols, cot.reshape(-1, channels))
    upstream = jnp.dot(tap_columns(cube(cot), True), weight_back, preferred_element_type=F32)
    hidden_grad = (upstream * silu_slope(hidden_pre) * own_flat).astype(BF)
    grad_one = grad_piece(feature_cols, hidden_grad)
    return (features_out, grad_one, grad_two)


def chip_at(place):
    return jnp.where(place < 4, 2 * place, 15 - 2 * place)


def place_of(tile):
    chip = tile // 2
    return jnp.where(chip % 2 == 0, chip // 2, 7 - chip // 2)


def shard_rows(tile, core, hop, flip, rows):
    step = jnp.where(core == 0, -hop, hop)
    chip = chip_at((place_of(tile) + step + 8) % 8)
    return pl.multiple_of((2 * chip + (1 - core if flip else core)) * rows, 16)


def store_shifted(out_ref, x0, rows, ny, nz, channels):
    planes = rows.shape[0] // (ny * nz)
    wide = rows.astype(F32)
    z = lax.broadcasted_iota(jnp.int32, wide.shape, 0) % nz
    before = jnp.where(z == 0, 0.0, pltpu.roll(wide, 1, 0)).astype(BF)
    after = jnp.where(z == nz - 1, 0.0, pltpu.roll(wide, wide.shape[0] - 1, 0)).astype(BF)
    for rho, value in enumerate((before, rows.astype(BF), after)):
        out_ref[x0 : x0 + planes, 1 : ny + 1, :, rho * channels : (rho + 1) * channels] = (
            value.reshape(planes, ny, nz, channels)
        )


def clear_edges(out_ref, ny):
    edge = jnp.zeros((out_ref.shape[0], 1) + tuple(out_ref.shape[2:]), BF)
    out_ref[:, 0:1] = edge
    out_ref[:, ny + 1 : ny + 2] = edge


def prep_kernel(tile_ref, cells_ref, low, f_own, c_own, high, sx_ref, sc_ref, int_ref, mask_ref):
    depth, ny, nz, channels = f_own.shape
    area = ny * nz
    tile = tile_ref[0]
    last = cells_ref.shape[0] - 1
    row = lax.broadcasted_iota(jnp.int32, (area, channels), 0)
    block_y, block_z = row // (B * nz), (row % nz) // B
    m = []
    for i in range(3):
        at = tile + i - 1
        inside = jnp.logical_and(at >= 0, at <= last)
        at = jnp.clip(at, 0, last)
        value = jnp.zeros((area, channels), F32)
        for y in range(ny // B):
            for z in range(nz // B):
                cell = jnp.where(inside, cells_ref[at, y * (nz // B) + z], 0).astype(F32)
                here = jnp.logical_and(block_y == y, block_z == z)
                value = jnp.where(here, cell, value)
        value = value.astype(BF)
        mask_ref[i] = value
        m.append(value.reshape(1, area, channels))

    def rows(value, side):
        planes = value.shape[0]
        value = value.reshape(planes, area, channels) * m[side]
        return value.reshape(planes * area, channels)

    clear_edges(sx_ref, ny)
    clear_edges(sc_ref, ny)
    fs = [rows(low[0:2], 0), rows(f_own[...], 1), rows(high[0:2], 2)]
    for x0, value in zip((0, 2, 2 + depth), fs):
        store_shifted(sx_ref, x0, value, ny, nz, channels)
    int_ref[:, 0:area] = fs[0][area:].T
    int_ref[:, area : area + depth * area] = fs[1].T
    int_ref[:, area + depth * area :] = fs[2][:area].T
    for x0, value, side in ((0, low[2:3], 0), (1, c_own[...], 1), (1 + depth, high[2:3], 2)):
        store_shifted(sc_ref, x0, rows(value, side), ny, nz, channels)


def fill_weight(tile_ref, pieces, w_ref):
    tile = tile_ref[0]
    core = tile % 2
    rows = w_ref.shape[0] // 16
    for k, piece in enumerate(pieces):
        hop, holder = (k, core) if k < 5 else (k - 4, 1 - core)
        for half in range(piece.shape[0] // rows):
            start = shard_rows(tile, holder, hop, half == 1, rows)
            w_ref[pl.ds(start, rows)] = piece[half * rows : (half + 1) * rows]


def split_shards(tile_ref, g_ref, keep_ref, send_ref):
    tile = tile_ref[0]
    core = tile % 2
    rows = g_ref.shape[0] // 16
    for out_ref, holder in ((send_ref, 1 - core), (keep_ref, core)):
        at = 0
        for hop in (4, 3, 2, 1, 0):
            for flip in (False,) if hop in (0, 4) else (False, True):
                start = shard_rows(tile, holder, -hop, flip, rows)
                out_ref[at : at + rows] = g_ref[pl.ds(start, rows)]
                at += rows


def window(ref, x, y, planes, ny, lo=0, hi=None):
    value = ref[x : x + planes, y : y + ny, :, lo:hi]
    return value.reshape(-1, value.shape[-1])


def conv(s_ref, w_ref, x0, planes, ny, channels):
    acc = None
    for p in range(3):
        for q in range(3):
            t = 9 * p + 3 * q
            part = jnp.dot(
                window(s_ref, x0 + p, q, planes, ny),
                w_ref[t * channels : (t + 3) * channels],
                preferred_element_type=F32,
            )
            acc = part if acc is None else acc + part
    return acc


def store_taps(g_ref, p, q, part, channels):
    for rho in range(3):
        t = 9 * p + 3 * q + 2 - rho
        g_ref[t * channels : (t + 1) * channels] = part[:, rho * channels : (rho + 1) * channels]


def masked(value, mask_ref, side):
    area, channels = mask_ref.shape[1:]
    own = mask_ref[side].reshape(1, area, channels).astype(F32)
    return (value.reshape(-1, area, channels) * own).reshape(-1, channels)


def first_kernel(n, tile_ref, sx_ref, sc_ref, mask_ref, *rest):
    pieces, (pre_ref, act_ref, keep_ref, send_ref, w_ref, g_ref) = rest[:n], rest[n:]
    area, channels = mask_ref.shape[1:]
    ny = sx_ref.shape[1] - 2
    depth = pre_ref.shape[0] // area
    fill_weight(tile_ref, pieces, w_ref)
    pre = conv(sx_ref, w_ref, 1, depth, ny, channels)
    pre_ref[...] = pre
    act = masked(pre * jax.nn.sigmoid(pre), mask_ref, 1).astype(BF)
    act_ref[...] = act
    act_t = act.T
    for p in range(3):
        for q in range(3):
            part = jnp.dot(
                act_t, window(sc_ref, 2 - p, 2 - q, depth, ny), preferred_element_type=F32
            )
            store_taps(g_ref, p, q, part.astype(BF), channels)
    split_shards(tile_ref, g_ref, keep_ref, send_ref)


def second_kernel(n, tile_ref, sc_ref, int_ref, pre_ref, mask_ref, *rest):
    pieces, (keep_ref, send_ref, w_ref, sd_ref, g_ref) = rest[:n], rest[n:]
    area, channels = mask_ref.shape[1:]
    ny, nz = sc_ref.shape[1] - 2, sc_ref.shape[2]
    depth = pre_ref.shape[0] // area
    fill_weight(tile_ref, pieces, w_ref)
    acc = None
    for p in range(3):
        for q in range(3):
            for r in range(3):
                t = 9 * p + 3 * q + r
                lo = (2 - r) * channels
                part = lax.dot_general(
                    window(sc_ref, 2 - p, 2 - q, depth, ny, lo, lo + channels),
                    w_ref[t * channels : (t + 1) * channels],
                    (((1,), (1,)), ((), ())),
                    preferred_element_type=F32,
                )
                acc = part if acc is None else acc + part
    delta = masked(acc * silu_slope(pre_ref[...]), mask_ref, 1).astype(BF)
    clear_edges(sd_ref, ny)
    store_shifted(sd_ref, 0, delta, ny, nz, channels)
    for q in range(3):
        right = window(sd_ref, 0, 2 - q, depth, ny)
        for p in range(3):
            part = jnp.dot(
                int_ref[:, p * area : (p + depth) * area], right, preferred_element_type=F32
            )
            store_taps(g_ref, p, q, part.astype(BF), channels)
    split_shards(tile_ref, g_ref, keep_ref, send_ref)


def third_kernel(n, tile_ref, sx_ref, act_ref, mask_ref, *rest):
    out_ref, w_ref, v_ref, sa_ref = rest[2 * n :]
    area, channels = mask_ref.shape[1:]
    ny, nz = sx_ref.shape[1] - 2, sx_ref.shape[2]
    depth = act_ref.shape[0] // area
    fill_weight(tile_ref, rest[:n], w_ref)
    fill_weight(tile_ref, rest[n : 2 * n], v_ref)
    clear_edges(sa_ref, ny)
    store_shifted(sa_ref, 1, act_ref[...], ny, nz, channels)
    for x0, side in ((0, 0), (1 + depth, 2)):
        pre = conv(sx_ref, w_ref, x0, 1, ny, channels)
        act = masked(pre * jax.nn.sigmoid(pre), mask_ref, side).astype(BF)
        store_shifted(sa_ref, x0, act, ny, nz, channels)
    second = conv(sa_ref, v_ref, 0, depth, ny, channels)
    out_ref[...] = masked(second, mask_ref, 1).astype(BF).reshape(out_ref.shape)


VMEM_LIMIT = 32 * 1024 * 1024


def on_ring(features, weight_one, weight_two, cotangent, block_mask):
    depth, ny, nz, channels = features.shape
    area = ny * nz
    rows = weight_one.shape[0]
    chips = len(RING)
    tiles = 2 * chips
    loss_scale = 1.0 / math.sqrt(tiles * depth * area)
    tile = lax.axis_index("tiles").astype(jnp.int32)[None]

    def permute(pairs):
        return functools.partial(lax.ppermute, axis_name="tiles", perm=pairs)

    onward = permute(
        [(2 * RING[i], 2 * RING[(i + 1) % chips]) for i in range(chips)]
        + [(2 * RING[i] + 1, 2 * RING[i - 1] + 1) for i in range(chips)]
    )
    sibling = permute([(i, i ^ 1) for i in range(tiles)])
    up = permute([(i, (i + 1) % tiles) for i in range(tiles)])
    down = permute([(i, (i - 1) % tiles) for i in range(tiles)])

    def gathered(weight, other):
        pair = jnp.concatenate([weight, other])
        p1 = onward(pair)
        p2 = onward(p1)
        p3 = onward(p2)
        p4 = onward(p3[:rows])
        return [pair, p1, p2, p3, p4] + [sibling(p) for p in (p1, p2, p3, p4)]

    other_one, other_two = sibling(weight_one), sibling(weight_two)
    features_late, cot_late, _ = lax.optimization_barrier((features, cotangent, other_one))
    low = up(jnp.concatenate([features_late[-2:], cot_late[-1:]]))
    high = down(jnp.concatenate([features_late[:2], cot_late[:1]]))
    ones, twos = gathered(weight_one, other_one), gathered(weight_two, other_two)
    n = len(ones)

    smem = pl.BlockSpec(memory_space=pltpu.SMEM)
    vmem = pl.BlockSpec(memory_space=pltpu.VMEM)
    params = pltpu.CompilerParams(vmem_limit_bytes=VMEM_LIMIT)
    shape = jax.ShapeDtypeStruct
    flops = 2 * depth * area * 27 * channels * channels

    def cost(convs):
        return pl.CostEstimate(
            flops=convs * flops, transcendentals=0, bytes_accessed=8 << 20
        )

    sx, sc, in_t, near = pl.pallas_call(
        prep_kernel,
        name="prep",
        out_shape=(
            shape((depth + 4, ny + 2, nz, 3 * channels), BF),
            shape((depth + 2, ny + 2, nz, 3 * channels), BF),
            shape((channels, (depth + 2) * area), BF),
            shape((3, area, channels), BF),
        ),
        in_specs=[smem, smem] + [vmem] * 4,
        out_specs=(vmem,) * 4,
        compiler_params=params,
    )(tile, block_mask.reshape(tiles, -1), low, features, cotangent, high)

    shards = (shape((chips * rows, channels), BF),) * 2
    weights = pltpu.VMEM((27 * channels, channels), BF)
    pre, act, keep_two, send_two = pl.pallas_call(
        functools.partial(first_kernel, n),
        name="first",
        out_shape=(shape((depth * area, channels), F32), shape((depth * area, channels), BF))
        + shards,
        in_specs=[smem] + [vmem] * (3 + n),
        out_specs=(vmem,) * 4,
        scratch_shapes=[weights, weights],
        compiler_params=params,
        cost_estimate=cost(2),
    )(tile, sx, sc, near, *ones)
    got_two = sibling(send_two)

    keep_one, send_one = pl.pallas_call(
        functools.partial(second_kernel, n),
        name="second",
        out_shape=shards,
        in_specs=[smem] + [vmem] * (4 + n),
        out_specs=(vmem,) * 2,
        scratch_shapes=[
            weights,
            pltpu.VMEM((depth, ny + 2, nz, 3 * channels), BF),
            weights,
        ],
        compiler_params=params,
        cost_estimate=cost(2),
    )(tile, sc, in_t, pre, near, *twos)
    got_one = sibling(send_one)

    act_late, _ = lax.optimization_barrier((act, got_two))
    features_out = pl.pallas_call(
        functools.partial(third_kernel, n),
        name="third",
        out_shape=shape(features.shape, BF),
        in_specs=[smem] + [vmem] * (3 + 2 * n),
        out_specs=vmem,
        scratch_shapes=[
            weights,
            weights,
            pltpu.VMEM((depth + 2, ny + 2, nz, 3 * channels), BF),
        ],
        compiler_params=params,
        cost_estimate=cost(2),
    )(tile, sx, act_late, near, *ones, *twos)

    def scattered(keep, got):
        def both(lo, hi):
            return keep[lo:hi].astype(F32) + got[lo:hi].astype(F32)

        moving = onward(both(0, rows).astype(BF)).astype(F32)
        moving = jnp.concatenate([moving, jnp.zeros_like(moving)])
        for k in range(3):
            lo = (1 + 2 * k) * rows
            moving = onward((both(lo, lo + 2 * rows) + moving).astype(BF)).astype(F32)
        across = sibling(moving[rows:].astype(BF)).astype(F32)
        return (both(7 * rows, 8 * rows) + moving[:rows] + across) * loss_scale

    return (features_out, scattered(keep_one, got_one), scattered(keep_two, got_two))


def solution(mesh):
    placed = (
        P(("groups", "tiles"), None, None, None),
        P("tiles", None),
        P("tiles", None),
        P(("groups", "tiles"), None, None, None),
        P("groups", None, None),
    )
    on_device = on_ring if mesh.shape["tiles"] == 2 * len(RING) else on_any
    return jax.shard_map(
        on_device,
        mesh=mesh,
        in_specs=placed,
        out_specs=(
            P(("groups", "tiles"), None, None, None),
            P(("groups", "tiles"), None),
            P(("groups", "tiles"), None),
        ),
        check_vma=False,
    )
```

```python
import functools
import math

import jax
import jax.numpy as jnp
from jax import lax
from jax.experimental import pallas as pl
from jax.experimental.pallas import tpu as pltpu
from jax.sharding import PartitionSpec as P

B = 4
RING = (0, 2, 4, 6, 7, 5, 3, 1)
BF = jnp.bfloat16
F32 = jnp.float32


def with_halo(block, axis, width):
    count = lax.axis_size(axis)
    forward = [(i, i + 1) for i in range(count - 1)]
    backward = [(target, source) for source, target in forward]
    low = lax.ppermute(block[-width:], axis, forward)
    high = lax.ppermute(block[:width], axis, backward)
    return low, high


def tap_columns(padded, flipped):
    extent = [padded.shape[d] - 2 for d in range(3)]
    taps = []
    for a in range(3):
        for b in range(3):
            for c in range(3):
                x, y, z = (2 - a, 2 - b, 2 - c) if flipped else (a, b, c)
                taps.append(padded[x : x + extent[0], y : y + extent[1], z : z + extent[2]])
    stacked = jnp.stack(taps, axis=3)
    return stacked.reshape(extent[0] * extent[1] * extent[2], 27 * padded.shape[3])


def expand_mask(cells, edge):
    planes, rows_y, rows_z = cells.shape
    values = jnp.broadcast_to(
        cells.astype(F32)[:, None, :, None, :, None], (planes, edge, rows_y, edge, rows_z, edge)
    )
    return values.reshape(planes * edge, rows_y * edge, rows_z * edge, 1)


def silu_slope(values):
    logistic = jax.nn.sigmoid(values)
    return logistic * (1.0 + values * (1.0 - logistic))


def near_cells_of(block_mask):
    padded_cells = jnp.pad(block_mask, ((1, 1), (0, 0), (0, 0)))
    return lax.dynamic_slice_in_dim(padded_cells, lax.axis_index("tiles"), 3, 0)


def on_any(features, weight_one, weight_two, cotangent, block_mask):
    depth, width_y, width_z, channels = features.shape
    loss_scale = 1.0 / math.sqrt(lax.axis_size("tiles") * depth * width_y * width_z)
    own_mask = expand_mask(near_cells_of(block_mask), B)[depth : 2 * depth]
    own_flat = own_mask.reshape(-1, 1)

    def cube(field):
        low, high = with_halo(field, "tiles", 1)
        field = jnp.concatenate([low, field, high], axis=0)
        return jnp.pad(field, ((0, 0), (1, 1), (1, 1), (0, 0)))

    def grad_piece(columns_in, rows_in):
        product = lax.dot_general(
            columns_in, rows_in, (((0,), (0,)), ((), ())), preferred_element_type=F32
        )
        return lax.psum_scatter(product * loss_scale, "tiles", scatter_dimension=0, tiled=True)

    full_one = lax.all_gather(weight_one, "tiles", axis=0, tiled=True)
    full_two = lax.all_gather(weight_two, "tiles", axis=0, tiled=True)
    weight_back = jnp.swapaxes(full_two.reshape(27, channels, channels), 1, 2).reshape(
        27 * channels, channels
    )
    inputs = (features * own_mask).astype(BF)
    feature_cols = tap_columns(cube(inputs), False)
    hidden_pre = jnp.dot(feature_cols, full_one, preferred_element_type=F32)
    active = (jax.nn.silu(hidden_pre) * own_flat).astype(BF).reshape(features.shape)
    active_cols = tap_columns(cube(active), False)
    second = jnp.dot(active_cols, full_two, preferred_element_type=F32)
    features_out = (second * own_flat).astype(BF).reshape(features.shape)
    cot = (cotangent * own_mask).astype(BF)
    grad_two = grad_piece(active_cols, cot.reshape(-1, channels))
    upstream = jnp.dot(tap_columns(cube(cot), True), weight_back, preferred_element_type=F32)
    hidden_grad = (upstream * silu_slope(hidden_pre) * own_flat).astype(BF)
    grad_one = grad_piece(feature_cols, hidden_grad)
    return (features_out, grad_one, grad_two)


def chip_at(place):
    return jnp.where(place < 4, 2 * place, 15 - 2 * place)


def place_of(tile):
    chip = tile // 2
    return jnp.where(chip % 2 == 0, chip // 2, 7 - chip // 2)


def shard_rows(tile, core, hop, flip, rows):
    step = jnp.where(core == 0, -hop, hop)
    chip = chip_at((place_of(tile) + step + 8) % 8)
    return pl.multiple_of((2 * chip + (1 - core if flip else core)) * rows, 16)


def store_shifted(out_ref, x0, rows, ny, nz, channels):
    planes = rows.shape[0] // (ny * nz)
    wide = rows.astype(F32)
    z = lax.broadcasted_iota(jnp.int32, wide.shape, 0) % nz
    before = jnp.where(z == 0, 0.0, pltpu.roll(wide, 1, 0)).astype(BF)
    after = jnp.where(z == nz - 1, 0.0, pltpu.roll(wide, wide.shape[0] - 1, 0)).astype(BF)
    for rho, value in enumerate((before, rows.astype(BF), after)):
        out_ref[x0 : x0 + planes, 1 : ny + 1, :, rho * channels : (rho + 1) * channels] = (
            value.reshape(planes, ny, nz, channels)
        )


def clear_edges(out_ref, ny):
    edge = jnp.zeros((out_ref.shape[0], 1) + tuple(out_ref.shape[2:]), BF)
    out_ref[:, 0:1] = edge
    out_ref[:, ny + 1 : ny + 2] = edge


def prep_kernel(tile_ref, cells_ref, low, f_own, c_own, high, sx_ref, sc_ref, int_ref, mask_ref):
    depth, ny, nz, channels = f_own.shape
    area = ny * nz
    tile = tile_ref[0]
    last = cells_ref.shape[0] - 1
    row = lax.broadcasted_iota(jnp.int32, (area, channels), 0)
    block_y, block_z = row // (B * nz), (row % nz) // B
    m = []
    for i in range(3):
        at = tile + i - 1
        inside = jnp.logical_and(at >= 0, at <= last)
        at = jnp.clip(at, 0, last)
        value = jnp.zeros((area, channels), F32)
        for y in range(ny // B):
            for z in range(nz // B):
                cell = jnp.where(inside, cells_ref[at, y * (nz // B) + z], 0).astype(F32)
                here = jnp.logical_and(block_y == y, block_z == z)
                value = jnp.where(here, cell, value)
        value = value.astype(BF)
        mask_ref[i] = value
        m.append(value.reshape(1, area, channels))

    def rows(value, side):
        planes = value.shape[0]
        value = value.reshape(planes, area, channels) * m[side]
        return value.reshape(planes * area, channels)

    clear_edges(sx_ref, ny)
    clear_edges(sc_ref, ny)
    fs = [rows(low[0:2], 0), rows(f_own[...], 1), rows(high[0:2], 2)]
    for x0, value in zip((0, 2, 2 + depth), fs):
        store_shifted(sx_ref, x0, value, ny, nz, channels)
    int_ref[:, 0:area] = fs[0][area:].T
    int_ref[:, area : area + depth * area] = fs[1].T
    int_ref[:, area + depth * area :] = fs[2][:area].T
    for x0, value, side in ((0, low[2:3], 0), (1, c_own[...], 1), (1 + depth, high[2:3], 2)):
        store_shifted(sc_ref, x0, rows(value, side), ny, nz, channels)


def fill_weight(tile_ref, pieces, w_ref):
    tile = tile_ref[0]
    core = tile % 2
    rows = w_ref.shape[0] // 16
    for k, piece in enumerate(pieces):
        hop, holder = (k, core) if k < 5 else (k - 4, 1 - core)
        for half in range(piece.shape[0] // rows):
            start = shard_rows(tile, holder, hop, half == 1, rows)
            w_ref[pl.ds(start, rows)] = piece[half * rows : (half + 1) * rows]


def split_shards(tile_ref, g_ref, keep_ref, send_ref):
    tile = tile_ref[0]
    core = tile % 2
    rows = g_ref.shape[0] // 16
    for out_ref, holder in ((send_ref, 1 - core), (keep_ref, core)):
        at = 0
        for hop in (4, 3, 2, 1, 0):
            for flip in (False,) if hop in (0, 4) else (False, True):
                start = shard_rows(tile, holder, -hop, flip, rows)
                out_ref[at : at + rows] = g_ref[pl.ds(start, rows)]
                at += rows


def window(ref, x, y, planes, ny, lo=0, hi=None):
    value = ref[x : x + planes, y : y + ny, :, lo:hi]
    return value.reshape(-1, value.shape[-1])


def conv(s_ref, w_ref, x0, planes, ny, channels):
    acc = None
    for p in range(3):
        for q in range(3):
            t = 9 * p + 3 * q
            part = jnp.dot(
                window(s_ref, x0 + p, q, planes, ny),
                w_ref[t * channels : (t + 3) * channels],
                preferred_element_type=F32,
            )
            acc = part if acc is None else acc + part
    return acc


def store_taps(g_ref, p, q, part, channels):
    for rho in range(3):
        t = 9 * p + 3 * q + 2 - rho
        g_ref[t * channels : (t + 1) * channels] = part[:, rho * channels : (rho + 1) * channels]


def masked(value, mask_ref, side):
    area, channels = mask_ref.shape[1:]
    own = mask_ref[side].reshape(1, area, channels).astype(F32)
    return (value.reshape(-1, area, channels) * own).reshape(-1, channels)


def first_kernel(n, tile_ref, sx_ref, sc_ref, mask_ref, *rest):
    pieces, (pre_ref, act_ref, keep_ref, send_ref, w_ref, g_ref) = rest[:n], rest[n:]
    area, channels = mask_ref.shape[1:]
    ny = sx_ref.shape[1] - 2
    depth = pre_ref.shape[0] // area
    fill_weight(tile_ref, pieces, w_ref)
    pre = conv(sx_ref, w_ref, 1, depth, ny, channels)
    pre_ref[...] = pre
    act = masked(pre * jax.nn.sigmoid(pre), mask_ref, 1).astype(BF)
    act_ref[...] = act
    act_t = act.T
    for p in range(3):
        for q in range(3):
            part = jnp.dot(
                act_t, window(sc_ref, 2 - p, 2 - q, depth, ny), preferred_element_type=F32
            )
            store_taps(g_ref, p, q, part.astype(BF), channels)
    split_shards(tile_ref, g_ref, keep_ref, send_ref)


def back_kernel(n, tile_ref, sc_ref, pre_ref, mask_ref, *rest):
    pieces, (sd_ref, w_ref) = rest[:n], rest[n:]
    area, channels = mask_ref.shape[1:]
    ny, nz = sc_ref.shape[1] - 2, sc_ref.shape[2]
    depth = pre_ref.shape[0] // area
    fill_weight(tile_ref, pieces, w_ref)
    acc = None
    for p in range(3):
        for q in range(3):
            for r in range(3):
                t = 9 * p + 3 * q + r
                lo = (2 - r) * channels
                part = lax.dot_general(
                    window(sc_ref, 2 - p, 2 - q, depth, ny, lo, lo + channels),
                    w_ref[t * channels : (t + 1) * channels],
                    (((1,), (1,)), ((), ())),
                    preferred_element_type=F32,
                )
                acc = part if acc is None else acc + part
    delta = masked(acc * silu_slope(pre_ref[...]), mask_ref, 1).astype(BF)
    clear_edges(sd_ref, ny)
    store_shifted(sd_ref, 0, delta, ny, nz, channels)


def grad_kernel(tile_ref, sd_ref, int_ref, keep_ref, send_ref, g_ref):
    depth, ny, nz, channels = sd_ref.shape
    ny, area, channels = ny - 2, (ny - 2) * nz, channels // 3
    for q in range(3):
        right = window(sd_ref, 0, 2 - q, depth, ny)
        for p in range(3):
            part = jnp.dot(
                int_ref[:, p * area : (p + depth) * area], right, preferred_element_type=F32
            )
            store_taps(g_ref, p, q, part.astype(BF), channels)
    split_shards(tile_ref, g_ref, keep_ref, send_ref)


def third_kernel(n, tile_ref, sx_ref, act_ref, mask_ref, *rest):
    out_ref, w_ref, v_ref, sa_ref = rest[2 * n :]
    area, channels = mask_ref.shape[1:]
    ny, nz = sx_ref.shape[1] - 2, sx_ref.shape[2]
    depth = act_ref.shape[0] // area
    fill_weight(tile_ref, rest[:n], w_ref)
    fill_weight(tile_ref, rest[n : 2 * n], v_ref)
    clear_edges(sa_ref, ny)
    store_shifted(sa_ref, 1, act_ref[...], ny, nz, channels)
    for x0, side in ((0, 0), (1 + depth, 2)):
        pre = conv(sx_ref, w_ref, x0, 1, ny, channels)
        act = masked(pre * jax.nn.sigmoid(pre), mask_ref, side).astype(BF)
        store_shifted(sa_ref, x0, act, ny, nz, channels)
    second = conv(sa_ref, v_ref, 0, depth, ny, channels)
    out_ref[...] = masked(second, mask_ref, 1).astype(BF).reshape(out_ref.shape)


VMEM_LIMIT = 24 * 1024 * 1024


def on_ring(features, weight_one, weight_two, cotangent, block_mask):
    depth, ny, nz, channels = features.shape
    area = ny * nz
    rows = weight_one.shape[0]
    chips = len(RING)
    tiles = 2 * chips
    loss_scale = 1.0 / math.sqrt(tiles * depth * area)
    tile = lax.axis_index("tiles").astype(jnp.int32)[None]

    def permute(pairs):
        return functools.partial(lax.ppermute, axis_name="tiles", perm=pairs)

    onward = permute(
        [(2 * RING[i], 2 * RING[(i + 1) % chips]) for i in range(chips)]
        + [(2 * RING[i] + 1, 2 * RING[i - 1] + 1) for i in range(chips)]
    )
    sibling = permute([(i, i ^ 1) for i in range(tiles)])
    up = permute([(i, (i + 1) % tiles) for i in range(tiles)])
    down = permute([(i, (i - 1) % tiles) for i in range(tiles)])

    def after(value, *others):
        return lax.optimization_barrier((value,) + others)[0]

    smem = pl.BlockSpec(memory_space=pltpu.SMEM)
    vmem = pl.BlockSpec(memory_space=pltpu.VMEM)
    params = pltpu.CompilerParams(vmem_limit_bytes=VMEM_LIMIT)
    shape = jax.ShapeDtypeStruct
    flops = 2 * depth * area * 27 * channels * channels

    def cost(convs):
        return pl.CostEstimate(
            flops=convs * flops, transcendentals=0, bytes_accessed=8 << 20
        )

    pair_one = jnp.concatenate([weight_one, sibling(weight_one)])
    pair_two = jnp.concatenate([after(weight_two, pair_one), sibling(weight_two)])
    pairs = [pair_one, pair_two]
    rings = [[pair, onward(pair)] for pair in pairs]
    features_late, cot_late, _ = lax.optimization_barrier((features, cotangent, pairs[1]))
    low = up(jnp.concatenate([features_late[-2:], cot_late[-1:]]))
    high = down(jnp.concatenate([features_late[:2], cot_late[:1]]))

    prep = pl.pallas_call(
        prep_kernel,
        name="prep",
        out_shape=(
            shape((depth + 4, ny + 2, nz, 3 * channels), BF),
            shape((depth + 2, ny + 2, nz, 3 * channels), BF),
            shape((channels, (depth + 2) * area), BF),
            shape((3, area, channels), BF),
        ),
        in_specs=[smem, smem] + [vmem] * 4,
        out_specs=(vmem,) * 4,
        compiler_params=params,
    )
    crossed = [[], []]
    sx, sc, in_t, near = None, None, None, None
    for hop in (1, 2, 3):
        for k in range(2):
            here = rings[k][hop]
            if k == 0 and hop > 1:
                here = after(here, rings[1][hop - 1])
            if hop == 1:
                if k == 0:
                    here = after(here, low, high)
                    sx, sc, in_t, near = prep(
                        tile, block_mask.reshape(tiles, -1), low, features, cotangent, high
                    )
            elif hop == 2:
                here = after(here, crossed[k][0], sx) if k == 0 else after(here, crossed[k][0])
            else:
                here = after(here, crossed[k][1])
            rings[k].append(onward(here[:rows] if hop == 3 else here))
            crossed[k].append(sibling(rings[k][hop]))
    for k in range(2):
        crossed[k].append(sibling(rings[k][4]))
    ones, twos = (rings[k] + crossed[k] for k in range(2))
    n = len(ones)

    shards = (shape((chips * rows, channels), BF),) * 2
    weights = pltpu.VMEM((27 * channels, channels), BF)
    pre, act, keep_two, send_two = pl.pallas_call(
        functools.partial(first_kernel, n),
        name="first",
        out_shape=(shape((depth * area, channels), F32), shape((depth * area, channels), BF))
        + shards,
        in_specs=[smem] + [vmem] * (3 + n),
        out_specs=(vmem,) * 4,
        scratch_shapes=[weights, weights],
        compiler_params=params,
        cost_estimate=cost(2),
    )(tile, after(sx, rings[1][3]), sc, near, *ones)
    got_two = sibling(send_two)

    features_out = pl.pallas_call(
        functools.partial(third_kernel, n),
        name="third",
        out_shape=shape(features.shape, BF),
        in_specs=[smem] + [vmem] * (3 + 2 * n),
        out_specs=vmem,
        scratch_shapes=[
            weights,
            weights,
            pltpu.VMEM((depth + 2, ny + 2, nz, 3 * channels), BF),
        ],
        compiler_params=params,
        cost_estimate=cost(1),
    )(tile, sx, act, near, *ones, *twos)

    def both(keep, got, lo, hi):
        return keep[lo * rows : hi * rows].astype(F32) + got[lo * rows : hi * rows].astype(F32)

    def step(keep, got, moving, k):
        if k == 0:
            return both(keep, got, 0, 1).astype(BF)
        if k == 1:
            moving = jnp.concatenate([moving, jnp.zeros_like(moving)])
        return (both(keep, got, 2 * k - 1, 2 * k + 1) + moving.astype(F32)).astype(BF)

    def finish(keep, got, moving):
        across = sibling(moving[rows:])
        total = both(keep, got, 7, 8) + moving[:rows].astype(F32) + across.astype(F32)
        return total * loss_scale

    message = step(keep_two, got_two, None, 0)
    two = onward(message)

    delta = pl.pallas_call(
        functools.partial(back_kernel, n),
        name="back",
        out_shape=shape((depth, ny + 2, nz, 3 * channels), BF),
        in_specs=[smem] + [vmem] * (3 + n),
        out_specs=vmem,
        scratch_shapes=[weights],
        compiler_params=params,
        cost_estimate=cost(1),
    )(tile, after(sc, message, features_out), pre, near, *twos)
    message = step(keep_two, got_two, after(two, delta), 1)
    two = onward(message)

    keep_one, send_one = pl.pallas_call(
        grad_kernel,
        name="grad",
        out_shape=shards,
        in_specs=[smem] + [vmem] * 2,
        out_specs=(vmem,) * 2,
        scratch_shapes=[weights],
        compiler_params=params,
        cost_estimate=cost(1),
    )(tile, after(delta, message), in_t)
    got_one = sibling(after(send_one, two))

    two = onward(step(keep_two, got_two, two, 2))
    one = onward(step(keep_one, got_one, None, 0))
    one = onward(step(keep_one, got_one, one, 1))
    two = onward(step(keep_two, got_two, two, 3))
    one = onward(step(keep_one, got_one, one, 2))
    grad_two = finish(keep_two, got_two, two)
    one = onward(step(keep_one, got_one, one, 3))
    return (features_out, finish(keep_one, got_one, one), grad_two)


def solution(mesh):
    placed = (
        P(("groups", "tiles"), None, None, None),
        P("tiles", None),
        P("tiles", None),
        P(("groups", "tiles"), None, None, None),
        P("groups", None, None),
    )
    on_device = on_ring if mesh.shape["tiles"] == 2 * len(RING) else on_any
    return jax.shard_map(
        on_device,
        mesh=mesh,
        in_specs=placed,
        out_specs=(
            P(("groups", "tiles"), None, None, None),
            P(("groups", "tiles"), None),
            P(("groups", "tiles"), None),
        ),
        check_vma=False,
    )
```

```python
import functools
import math

import jax
import jax.numpy as jnp
from jax import lax
from jax.experimental import pallas as pl
from jax.experimental.pallas import tpu as pltpu
from jax.sharding import PartitionSpec as P

B = 4
RING = (0, 2, 4, 6, 7, 5, 3, 1)
BF = jnp.bfloat16
F32 = jnp.float32


def with_halo(block, axis, width):
    count = lax.axis_size(axis)
    forward = [(i, i + 1) for i in range(count - 1)]
    backward = [(target, source) for source, target in forward]
    low = lax.ppermute(block[-width:], axis, forward)
    high = lax.ppermute(block[:width], axis, backward)
    return low, high


def tap_columns(padded, flipped):
    extent = [padded.shape[d] - 2 for d in range(3)]
    taps = []
    for a in range(3):
        for b in range(3):
            for c in range(3):
                x, y, z = (2 - a, 2 - b, 2 - c) if flipped else (a, b, c)
                taps.append(padded[x : x + extent[0], y : y + extent[1], z : z + extent[2]])
    stacked = jnp.stack(taps, axis=3)
    return stacked.reshape(extent[0] * extent[1] * extent[2], 27 * padded.shape[3])


def expand_mask(cells, edge):
    planes, rows_y, rows_z = cells.shape
    values = jnp.broadcast_to(
        cells.astype(F32)[:, None, :, None, :, None], (planes, edge, rows_y, edge, rows_z, edge)
    )
    return values.reshape(planes * edge, rows_y * edge, rows_z * edge, 1)


def silu_slope(values):
    logistic = jax.nn.sigmoid(values)
    return logistic * (1.0 + values * (1.0 - logistic))


def near_cells_of(block_mask):
    padded_cells = jnp.pad(block_mask, ((1, 1), (0, 0), (0, 0)))
    return lax.dynamic_slice_in_dim(padded_cells, lax.axis_index("tiles"), 3, 0)


def on_any(features, weight_one, weight_two, cotangent, block_mask):
    depth, width_y, width_z, channels = features.shape
    loss_scale = 1.0 / math.sqrt(lax.axis_size("tiles") * depth * width_y * width_z)
    own_mask = expand_mask(near_cells_of(block_mask), B)[depth : 2 * depth]
    own_flat = own_mask.reshape(-1, 1)

    def cube(field):
        low, high = with_halo(field, "tiles", 1)
        field = jnp.concatenate([low, field, high], axis=0)
        return jnp.pad(field, ((0, 0), (1, 1), (1, 1), (0, 0)))

    def grad_piece(columns_in, rows_in):
        product = lax.dot_general(
            columns_in, rows_in, (((0,), (0,)), ((), ())), preferred_element_type=F32
        )
        return lax.psum_scatter(product * loss_scale, "tiles", scatter_dimension=0, tiled=True)

    full_one = lax.all_gather(weight_one, "tiles", axis=0, tiled=True)
    full_two = lax.all_gather(weight_two, "tiles", axis=0, tiled=True)
    weight_back = jnp.swapaxes(full_two.reshape(27, channels, channels), 1, 2).reshape(
        27 * channels, channels
    )
    inputs = (features * own_mask).astype(BF)
    feature_cols = tap_columns(cube(inputs), False)
    hidden_pre = jnp.dot(feature_cols, full_one, preferred_element_type=F32)
    active = (jax.nn.silu(hidden_pre) * own_flat).astype(BF).reshape(features.shape)
    active_cols = tap_columns(cube(active), False)
    second = jnp.dot(active_cols, full_two, preferred_element_type=F32)
    features_out = (second * own_flat).astype(BF).reshape(features.shape)
    cot = (cotangent * own_mask).astype(BF)
    grad_two = grad_piece(active_cols, cot.reshape(-1, channels))
    upstream = jnp.dot(tap_columns(cube(cot), True), weight_back, preferred_element_type=F32)
    hidden_grad = (upstream * silu_slope(hidden_pre) * own_flat).astype(BF)
    grad_one = grad_piece(feature_cols, hidden_grad)
    return (features_out, grad_one, grad_two)


def chip_at(place):
    return jnp.where(place < 4, 2 * place, 15 - 2 * place)


def place_of(tile):
    chip = tile // 2
    return jnp.where(chip % 2 == 0, chip // 2, 7 - chip // 2)


def shard_rows(tile, core, hop, flip, rows):
    step = jnp.where(core == 0, -hop, hop)
    chip = chip_at((place_of(tile) + step + 8) % 8)
    return pl.multiple_of((2 * chip + (1 - core if flip else core)) * rows, 16)


def store_shifted(out_ref, x0, rows, ny, nz, channels):
    planes = rows.shape[0] // (ny * nz)
    wide = rows.astype(F32)
    z = lax.broadcasted_iota(jnp.int32, wide.shape, 0) % nz
    before = jnp.where(z == 0, 0.0, pltpu.roll(wide, 1, 0)).astype(BF)
    after = jnp.where(z == nz - 1, 0.0, pltpu.roll(wide, wide.shape[0] - 1, 0)).astype(BF)
    for rho, value in enumerate((before, rows.astype(BF), after)):
        out_ref[x0 : x0 + planes, 1 : ny + 1, :, rho * channels : (rho + 1) * channels] = (
            value.reshape(planes, ny, nz, channels)
        )


def clear_edges(out_ref, ny):
    edge = jnp.zeros((out_ref.shape[0], 1) + tuple(out_ref.shape[2:]), BF)
    out_ref[:, 0:1] = edge
    out_ref[:, ny + 1 : ny + 2] = edge


def prep_kernel(cells_ref, low, f_own, c_own, high, sx_ref, sc_ref, int_ref, mask_ref):
    depth, ny, nz, channels = f_own.shape
    area = ny * nz
    tile = lax.axis_index("tiles")
    last = cells_ref.shape[2] - 1
    row = lax.broadcasted_iota(jnp.int32, (area, channels), 0)
    block_y, block_z = row // (B * nz), (row % nz) // B
    m = []
    for i in range(3):
        at = tile + i - 1
        inside = jnp.logical_and(at >= 0, at <= last)
        at = jnp.clip(at, 0, last)
        value = jnp.zeros((area, channels), F32)
        for y in range(ny // B):
            for z in range(nz // B):
                cell = jnp.where(inside, cells_ref[y, z, at], 0).astype(F32)
                here = jnp.logical_and(block_y == y, block_z == z)
                value = jnp.where(here, cell, value)
        value = value.astype(BF)
        mask_ref[i] = value
        m.append(value.reshape(1, area, channels))

    def rows(value, side):
        planes = value.shape[0]
        value = value.reshape(planes, area, channels) * m[side]
        return value.reshape(planes * area, channels)

    clear_edges(sx_ref, ny)
    clear_edges(sc_ref, ny)
    fs = [rows(low[0:2], 0), rows(f_own[...], 1), rows(high[0:2], 2)]
    for x0, value in zip((0, 2, 2 + depth), fs):
        store_shifted(sx_ref, x0, value, ny, nz, channels)
    int_ref[:, 0:area] = fs[0][area:].T
    int_ref[:, area : area + depth * area] = fs[1].T
    int_ref[:, area + depth * area :] = fs[2][:area].T
    for x0, value, side in ((0, low[2:3], 0), (1, c_own[...], 1), (1 + depth, high[2:3], 2)):
        store_shifted(sc_ref, x0, rows(value, side), ny, nz, channels)


def fill_weight(pieces, w_ref):
    tile = lax.axis_index("tiles")
    core = tile % 2
    rows = w_ref.shape[0] // 16
    for k, piece in enumerate(pieces):
        hop, holder = (k, core) if k < 5 else (k - 4, 1 - core)
        for half in range(piece.shape[0] // rows):
            start = shard_rows(tile, holder, hop, half == 1, rows)
            w_ref[pl.ds(start, rows)] = piece[half * rows : (half + 1) * rows]


def split_shards(g_ref, keep_ref, send_ref):
    tile = lax.axis_index("tiles")
    core = tile % 2
    rows = g_ref.shape[0] // 16
    for out_ref, holder in ((send_ref, 1 - core), (keep_ref, core)):
        at = 0
        for hop in (4, 3, 2, 1, 0):
            for flip in (False,) if hop in (0, 4) else (False, True):
                start = shard_rows(tile, holder, -hop, flip, rows)
                out_ref[at : at + rows] = g_ref[pl.ds(start, rows)]
                at += rows


def window(ref, x, y, planes, ny, lo=0, hi=None):
    value = ref[x : x + planes, y : y + ny, :, lo:hi]
    return value.reshape(-1, value.shape[-1])


def conv(s_ref, w_ref, x0, planes, ny, channels):
    acc = None
    for p in range(3):
        for q in range(3):
            t = 9 * p + 3 * q
            part = jnp.dot(
                window(s_ref, x0 + p, q, planes, ny),
                w_ref[t * channels : (t + 3) * channels],
                preferred_element_type=F32,
            )
            acc = part if acc is None else acc + part
    return acc


def store_taps(g_ref, p, q, part, channels):
    for rho in range(3):
        t = 9 * p + 3 * q + 2 - rho
        g_ref[t * channels : (t + 1) * channels] = part[:, rho * channels : (rho + 1) * channels]


def masked(value, mask_ref, side):
    area, channels = mask_ref.shape[1:]
    own = mask_ref[side].reshape(1, area, channels).astype(F32)
    return (value.reshape(-1, area, channels) * own).reshape(-1, channels)


def first_kernel(n, sx_ref, sc_ref, mask_ref, *rest):
    pieces, (pre_ref, act_ref, keep_ref, send_ref, w_ref, g_ref) = rest[:n], rest[n:]
    area, channels = mask_ref.shape[1:]
    ny = sx_ref.shape[1] - 2
    depth = pre_ref.shape[0] // area
    fill_weight(pieces, w_ref)
    pre = conv(sx_ref, w_ref, 1, depth, ny, channels)
    pre_ref[...] = pre
    act = masked(pre * jax.nn.sigmoid(pre), mask_ref, 1).astype(BF)
    act_ref[...] = act
    act_t = act.T
    for p in range(3):
        for q in range(3):
            part = jnp.dot(
                act_t, window(sc_ref, 2 - p, 2 - q, depth, ny), preferred_element_type=F32
            )
            store_taps(g_ref, p, q, part.astype(BF), channels)
    split_shards(g_ref, keep_ref, send_ref)


def back_kernel(n, sc_ref, pre_ref, mask_ref, *rest):
    pieces, (sd_ref, w_ref) = rest[:n], rest[n:]
    area, channels = mask_ref.shape[1:]
    ny, nz = sc_ref.shape[1] - 2, sc_ref.shape[2]
    depth = pre_ref.shape[0] // area
    fill_weight(pieces, w_ref)
    acc = None
    for p in range(3):
        for q in range(3):
            for r in range(3):
                t = 9 * p + 3 * q + r
                lo = (2 - r) * channels
                part = lax.dot_general(
                    window(sc_ref, 2 - p, 2 - q, depth, ny, lo, lo + channels),
                    w_ref[t * channels : (t + 1) * channels],
                    (((1,), (1,)), ((), ())),
                    preferred_element_type=F32,
                )
                acc = part if acc is None else acc + part
    delta = masked(acc * silu_slope(pre_ref[...]), mask_ref, 1).astype(BF)
    clear_edges(sd_ref, ny)
    store_shifted(sd_ref, 0, delta, ny, nz, channels)


def grad_kernel(sd_ref, int_ref, keep_ref, send_ref, g_ref):
    depth, ny, nz, channels = sd_ref.shape
    ny, area, channels = ny - 2, (ny - 2) * nz, channels // 3
    for q in range(3):
        right = window(sd_ref, 0, 2 - q, depth, ny)
        for p in range(3):
            part = jnp.dot(
                int_ref[:, p * area : (p + depth) * area], right, preferred_element_type=F32
            )
            store_taps(g_ref, p, q, part.astype(BF), channels)
    split_shards(g_ref, keep_ref, send_ref)


def third_kernel(n, sx_ref, act_ref, mask_ref, *rest):
    out_ref, w_ref, v_ref, sa_ref = rest[2 * n :]
    area, channels = mask_ref.shape[1:]
    ny, nz = sx_ref.shape[1] - 2, sx_ref.shape[2]
    depth = act_ref.shape[0] // area
    fill_weight(rest[:n], w_ref)
    fill_weight(rest[n : 2 * n], v_ref)
    clear_edges(sa_ref, ny)
    store_shifted(sa_ref, 1, act_ref[...], ny, nz, channels)
    for x0, side in ((0, 0), (1 + depth, 2)):
        pre = conv(sx_ref, w_ref, x0, 1, ny, channels)
        act = masked(pre * jax.nn.sigmoid(pre), mask_ref, side).astype(BF)
        store_shifted(sa_ref, x0, act, ny, nz, channels)
    second = conv(sa_ref, v_ref, 0, depth, ny, channels)
    out_ref[...] = masked(second, mask_ref, 1).astype(BF).reshape(out_ref.shape)


def on_ring(features, weight_one, weight_two, cotangent, block_mask):
    depth, ny, nz, channels = features.shape
    area = ny * nz
    rows = weight_one.shape[0]
    chips = len(RING)
    tiles = 2 * chips
    loss_scale = 1.0 / math.sqrt(tiles * depth * area)

    def permute(pairs):
        return functools.partial(lax.ppermute, axis_name="tiles", perm=pairs)

    onward = permute(
        [(2 * RING[i], 2 * RING[(i + 1) % chips]) for i in range(chips)]
        + [(2 * RING[i] + 1, 2 * RING[i - 1] + 1) for i in range(chips)]
    )
    sibling = permute([(i, i ^ 1) for i in range(tiles)])
    up = permute([(i, (i + 1) % tiles) for i in range(tiles)])
    down = permute([(i, (i - 1) % tiles) for i in range(tiles)])

    def after(value, *others):
        return lax.optimization_barrier((value,) + others)[0]

    smem = pl.BlockSpec(memory_space=pltpu.SMEM)
    vmem = pl.BlockSpec(memory_space=pltpu.VMEM)

    def params(mib):
        return pltpu.CompilerParams(vmem_limit_bytes=mib << 20)

    shape = jax.ShapeDtypeStruct
    flops = 2 * depth * area * 27 * channels * channels

    def cost(convs):
        return pl.CostEstimate(
            flops=convs * flops, transcendentals=0, bytes_accessed=8 << 20
        )

    pair_one = jnp.concatenate([weight_one, sibling(weight_one)])
    pair_two = jnp.concatenate([after(weight_two, pair_one), sibling(weight_two)])
    pairs = [pair_one, pair_two]
    rings = [[pair, onward(pair)] for pair in pairs]
    features_late, cot_late, _ = lax.optimization_barrier((features, cotangent, pairs[1]))
    low = up(jnp.concatenate([features_late[-2:], cot_late[-1:]]))
    high = down(jnp.concatenate([features_late[:2], cot_late[:1]]))

    prep = pl.pallas_call(
        prep_kernel,
        name="prep",
        out_shape=(
            shape((depth + 4, ny + 2, nz, 3 * channels), BF),
            shape((depth + 2, ny + 2, nz, 3 * channels), BF),
            shape((channels, (depth + 2) * area), BF),
            shape((3, area, channels), BF),
        ),
        in_specs=[smem] + [vmem] * 4,
        out_specs=(vmem,) * 4,
        compiler_params=params(8),
    )
    crossed = [[], []]
    for hop in (1, 2, 3):
        for k in range(2):
            here = rings[k][hop]
            if hop == 3:
                here = here[:rows]
            if k == 0 and hop > 1:
                here = after(here, rings[1][hop - 1])
            if k == 0 and hop == 2:
                here = after(here, low, high)
                sx, sc, in_t, near = prep(
                    jnp.transpose(block_mask, (1, 2, 0)), low, features, cotangent, high
                )
            if k == 0 and hop == 3:
                here = after(here, sx)
            if hop > 1:
                here = after(here, crossed[k][hop - 2])
            rings[k].append(onward(here))
            crossed[k].append(sibling(rings[k][hop]))
    for k in range(2):
        crossed[k].append(sibling(rings[k][4]))
    ones, twos = (rings[k] + crossed[k] for k in range(2))
    n = len(ones)

    shards = (shape((chips * rows, channels), BF),) * 2
    weights = pltpu.VMEM((27 * channels, channels), BF)
    pre, act, keep_two, send_two = pl.pallas_call(
        functools.partial(first_kernel, n),
        name="first",
        out_shape=(shape((depth * area, channels), F32), shape((depth * area, channels), BF))
        + shards,
        in_specs=[vmem] * (3 + n),
        out_specs=(vmem,) * 4,
        scratch_shapes=[weights, weights],
        compiler_params=params(12),
        cost_estimate=cost(2),
    )(after(sx, rings[1][4]), sc, near, *ones)
    got_two = sibling(send_two)

    def both(keep, got, lo, hi):
        return keep[lo * rows : hi * rows].astype(F32) + got[lo * rows : hi * rows].astype(F32)

    def step(keep, got, moving, k):
        if k == 0:
            return both(keep, got, 0, 1).astype(BF)
        if k == 1:
            moving = jnp.concatenate([moving, jnp.zeros_like(moving)])
        return (both(keep, got, 2 * k - 1, 2 * k + 1) + moving.astype(F32)).astype(BF)

    def finish(keep, got, moving):
        across = sibling(moving[rows:])
        total = both(keep, got, 7, 8) + moving[:rows].astype(F32) + across.astype(F32)
        return total * loss_scale

    delta = pl.pallas_call(
        functools.partial(back_kernel, n),
        name="back",
        out_shape=shape((depth, ny + 2, nz, 3 * channels), BF),
        in_specs=[vmem] * (3 + n),
        out_specs=vmem,
        scratch_shapes=[weights],
        compiler_params=params(8),
        cost_estimate=cost(1),
    )(sc, pre, near, *twos)
    keep_one, send_one = pl.pallas_call(
        grad_kernel,
        name="grad",
        out_shape=shards,
        in_specs=[vmem] * 2,
        out_specs=(vmem,) * 2,
        scratch_shapes=[weights],
        compiler_params=params(8),
        cost_estimate=cost(1),
    )(delta, in_t)
    got_two_late = after(got_two, keep_one)
    two = onward(step(keep_two, got_two_late, None, 0))
    got_one = sibling(send_one)
    one = onward(step(keep_one, got_one, None, 0))
    features_out = pl.pallas_call(
        functools.partial(third_kernel, n),
        name="third",
        out_shape=shape(features.shape, BF),
        in_specs=[vmem] * (3 + 2 * n),
        out_specs=vmem,
        scratch_shapes=[
            weights,
            weights,
            pltpu.VMEM((depth + 2, ny + 2, nz, 3 * channels), BF),
        ],
        compiler_params=params(14),
        cost_estimate=cost(1),
    )(sx, after(act, two), near, *ones, *twos)

    two = onward(step(keep_two, got_two, two, 1))
    one = onward(step(keep_one, got_one, one, 1))
    two = onward(step(keep_two, got_two, after(two, features_out), 2))
    one = onward(step(keep_one, got_one, one, 2))
    two = onward(step(keep_two, got_two, two, 3))
    one = onward(step(keep_one, got_one, one, 3))
    grad_two = finish(keep_two, got_two, two)
    return (features_out, finish(keep_one, got_one, one), grad_two)


def solution(mesh):
    placed = (
        P(("groups", "tiles"), None, None, None),
        P("tiles", None),
        P("tiles", None),
        P(("groups", "tiles"), None, None, None),
        P("groups", None, None),
    )
    on_device = on_ring if mesh.shape["tiles"] == 2 * len(RING) else on_any
    return jax.shard_map(
        on_device,
        mesh=mesh,
        in_specs=placed,
        out_specs=(
            P(("groups", "tiles"), None, None, None),
            P(("groups", "tiles"), None),
            P(("groups", "tiles"), None),
        ),
        check_vma=False,
    )
```

```python
import functools
import math

import jax
import jax.numpy as jnp
from jax import lax
from jax.experimental import pallas as pl
from jax.experimental.pallas import tpu as pltpu
from jax.sharding import PartitionSpec as P

B = 4
RING = (0, 2, 4, 6, 7, 5, 3, 1)
BF = jnp.bfloat16
F32 = jnp.float32


def with_halo(block, axis, width):
    count = lax.axis_size(axis)
    forward = [(i, i + 1) for i in range(count - 1)]
    backward = [(target, source) for source, target in forward]
    low = lax.ppermute(block[-width:], axis, forward)
    high = lax.ppermute(block[:width], axis, backward)
    return low, high


def tap_columns(padded, flipped):
    extent = [padded.shape[d] - 2 for d in range(3)]
    taps = []
    for a in range(3):
        for b in range(3):
            for c in range(3):
                x, y, z = (2 - a, 2 - b, 2 - c) if flipped else (a, b, c)
                taps.append(padded[x : x + extent[0], y : y + extent[1], z : z + extent[2]])
    stacked = jnp.stack(taps, axis=3)
    return stacked.reshape(extent[0] * extent[1] * extent[2], 27 * padded.shape[3])


def expand_mask(cells, edge):
    planes, rows_y, rows_z = cells.shape
    values = jnp.broadcast_to(
        cells.astype(F32)[:, None, :, None, :, None], (planes, edge, rows_y, edge, rows_z, edge)
    )
    return values.reshape(planes * edge, rows_y * edge, rows_z * edge, 1)


def silu_slope(values):
    logistic = jax.nn.sigmoid(values)
    return logistic * (1.0 + values * (1.0 - logistic))


def near_cells_of(block_mask):
    padded_cells = jnp.pad(block_mask, ((1, 1), (0, 0), (0, 0)))
    return lax.dynamic_slice_in_dim(padded_cells, lax.axis_index("tiles"), 3, 0)


def on_any(features, weight_one, weight_two, cotangent, block_mask):
    depth, width_y, width_z, channels = features.shape
    loss_scale = 1.0 / math.sqrt(lax.axis_size("tiles") * depth * width_y * width_z)
    own_mask = expand_mask(near_cells_of(block_mask), B)[depth : 2 * depth]
    own_flat = own_mask.reshape(-1, 1)

    def cube(field):
        low, high = with_halo(field, "tiles", 1)
        field = jnp.concatenate([low, field, high], axis=0)
        return jnp.pad(field, ((0, 0), (1, 1), (1, 1), (0, 0)))

    def grad_piece(columns_in, rows_in):
        product = lax.dot_general(
            columns_in, rows_in, (((0,), (0,)), ((), ())), preferred_element_type=F32
        )
        return lax.psum_scatter(product * loss_scale, "tiles", scatter_dimension=0, tiled=True)

    full_one = lax.all_gather(weight_one, "tiles", axis=0, tiled=True)
    full_two = lax.all_gather(weight_two, "tiles", axis=0, tiled=True)
    weight_back = jnp.swapaxes(full_two.reshape(27, channels, channels), 1, 2).reshape(
        27 * channels, channels
    )
    inputs = (features * own_mask).astype(BF)
    feature_cols = tap_columns(cube(inputs), False)
    hidden_pre = jnp.dot(feature_cols, full_one, preferred_element_type=F32)
    active = (jax.nn.silu(hidden_pre) * own_flat).astype(BF).reshape(features.shape)
    active_cols = tap_columns(cube(active), False)
    second = jnp.dot(active_cols, full_two, preferred_element_type=F32)
    features_out = (second * own_flat).astype(BF).reshape(features.shape)
    cot = (cotangent * own_mask).astype(BF)
    grad_two = grad_piece(active_cols, cot.reshape(-1, channels))
    upstream = jnp.dot(tap_columns(cube(cot), True), weight_back, preferred_element_type=F32)
    hidden_grad = (upstream * silu_slope(hidden_pre) * own_flat).astype(BF)
    grad_one = grad_piece(feature_cols, hidden_grad)
    return (features_out, grad_one, grad_two)


def chip_at(place):
    return jnp.where(place < 4, 2 * place, 15 - 2 * place)


def place_of(tile):
    chip = tile // 2
    return jnp.where(chip % 2 == 0, chip // 2, 7 - chip // 2)


def shard_rows(tile, core, hop, flip, rows):
    step = jnp.where(core == 0, -hop, hop)
    chip = chip_at((place_of(tile) + step + 8) % 8)
    return pl.multiple_of((2 * chip + (1 - core if flip else core)) * rows, 16)


def store_shifted(out_ref, x0, rows, ny, nz, channels):
    planes = rows.shape[0] // (ny * nz)
    wide = rows.astype(F32)
    z = lax.broadcasted_iota(jnp.int32, wide.shape, 0) % nz
    before = jnp.where(z == 0, 0.0, pltpu.roll(wide, 1, 0)).astype(BF)
    after = jnp.where(z == nz - 1, 0.0, pltpu.roll(wide, wide.shape[0] - 1, 0)).astype(BF)
    for rho, value in enumerate((before, rows.astype(BF), after)):
        out_ref[x0 : x0 + planes, 1 : ny + 1, :, rho * channels : (rho + 1) * channels] = (
            value.reshape(planes, ny, nz, channels)
        )


def clear_edges(out_ref, ny):
    edge = jnp.zeros((out_ref.shape[0], 1) + tuple(out_ref.shape[2:]), BF)
    out_ref[:, 0:1] = edge
    out_ref[:, ny + 1 : ny + 2] = edge


def prep_kernel(cells_ref, low, f_own, c_own, high, sx_ref, sc_ref, int_ref, mask_ref):
    depth, ny, nz, channels = f_own.shape
    area = ny * nz
    tile = lax.axis_index("tiles")
    last = cells_ref.shape[2] - 1
    row = lax.broadcasted_iota(jnp.int32, (area, channels), 0)
    block_y, block_z = row // (B * nz), (row % nz) // B
    m = []
    for i in range(3):
        at = tile + i - 1
        inside = jnp.logical_and(at >= 0, at <= last)
        at = jnp.clip(at, 0, last)
        value = jnp.zeros((area, channels), F32)
        for y in range(ny // B):
            for z in range(nz // B):
                cell = jnp.where(inside, cells_ref[y, z, at], 0).astype(F32)
                here = jnp.logical_and(block_y == y, block_z == z)
                value = jnp.where(here, cell, value)
        value = value.astype(BF)
        mask_ref[i] = value
        m.append(value.reshape(1, area, channels))

    def rows(value, side):
        planes = value.shape[0]
        value = value.reshape(planes, area, channels) * m[side]
        return value.reshape(planes * area, channels)

    clear_edges(sx_ref, ny)
    clear_edges(sc_ref, ny)
    fs = [rows(low[0:2], 0), rows(f_own[...], 1), rows(high[0:2], 2)]
    for x0, value in zip((0, 2, 2 + depth), fs):
        store_shifted(sx_ref, x0, value, ny, nz, channels)
    int_ref[:, 0:area] = fs[0][area:].T
    int_ref[:, area : area + depth * area] = fs[1].T
    int_ref[:, area + depth * area :] = fs[2][:area].T
    for x0, value, side in ((0, low[2:3], 0), (1, c_own[...], 1), (1 + depth, high[2:3], 2)):
        store_shifted(sc_ref, x0, rows(value, side), ny, nz, channels)


PIECES = (
    (0, False, False),
    (0, False, True),
    (1, False, False),
    (1, False, True),
    (2, False, False),
    (3, False, False),
    (4, False, False),
    (1, True, False),
    (2, True, False),
    (3, True, False),
    (4, True, False),
)


def fill_weight(pieces, w_ref):
    tile = lax.axis_index("tiles")
    core = tile % 2
    rows = w_ref.shape[0] // 16
    for piece, (hop, crossed, flip) in zip(pieces, PIECES):
        holder = 1 - core if crossed else core
        for half in range(piece.shape[0] // rows):
            start = shard_rows(tile, holder, hop, flip or half == 1, rows)
            w_ref[pl.ds(start, rows)] = piece[half * rows : (half + 1) * rows]


def split_shards(g_ref, keep_ref, send_ref):
    tile = lax.axis_index("tiles")
    core = tile % 2
    rows = g_ref.shape[0] // 16
    for out_ref, holder in ((send_ref, 1 - core), (keep_ref, core)):
        at = 0
        for hop in (4, 3, 2, 1, 0):
            for flip in (False,) if hop in (0, 4) else (False, True):
                start = shard_rows(tile, holder, -hop, flip, rows)
                out_ref[at : at + rows] = g_ref[pl.ds(start, rows)]
                at += rows


def window(ref, x, y, planes, ny, lo=0, hi=None):
    value = ref[x : x + planes, y : y + ny, :, lo:hi]
    return value.reshape(-1, value.shape[-1])


def conv(s_ref, w_ref, x0, planes, ny, channels):
    acc = None
    for p in range(3):
        for q in range(3):
            t = 9 * p + 3 * q
            part = jnp.dot(
                window(s_ref, x0 + p, q, planes, ny),
                w_ref[t * channels : (t + 3) * channels],
                preferred_element_type=F32,
            )
            acc = part if acc is None else acc + part
    return acc


def store_taps(g_ref, p, q, part, channels):
    for rho in range(3):
        t = 9 * p + 3 * q + 2 - rho
        g_ref[t * channels : (t + 1) * channels] = part[:, rho * channels : (rho + 1) * channels]


def masked(value, mask_ref, side):
    area, channels = mask_ref.shape[1:]
    own = mask_ref[side].reshape(1, area, channels).astype(F32)
    return (value.reshape(-1, area, channels) * own).reshape(-1, channels)


def first_kernel(n, sx_ref, mask_ref, *rest):
    pieces, (pre_ref, act_ref, act_t_ref, w_ref) = rest[:n], rest[n:]
    area, channels = mask_ref.shape[1:]
    ny = sx_ref.shape[1] - 2
    depth = pre_ref.shape[0] // area
    fill_weight(pieces, w_ref)
    pre = conv(sx_ref, w_ref, 1, depth, ny, channels)
    pre_ref[...] = pre
    act = masked(pre * jax.nn.sigmoid(pre), mask_ref, 1).astype(BF)
    act_ref[...] = act
    act_t_ref[...] = act.T


def grad_two_kernel(sc_ref, act_t_ref, keep_ref, send_ref, g_ref):
    depth, ny, nz, channels = sc_ref.shape
    depth, ny, channels = depth - 2, ny - 2, channels // 3
    for p in range(3):
        for q in range(3):
            part = jnp.dot(
                act_t_ref[...],
                window(sc_ref, 2 - p, 2 - q, depth, ny),
                preferred_element_type=F32,
            )
            store_taps(g_ref, p, q, part.astype(BF), channels)
    split_shards(g_ref, keep_ref, send_ref)


def back_kernel(n, sc_ref, pre_ref, mask_ref, *rest):
    pieces, (sd_ref, w_ref) = rest[:n], rest[n:]
    area, channels = mask_ref.shape[1:]
    ny, nz = sc_ref.shape[1] - 2, sc_ref.shape[2]
    depth = pre_ref.shape[0] // area
    fill_weight(pieces, w_ref)
    acc = None
    for p in range(3):
        for q in range(3):
            for r in range(3):
                t = 9 * p + 3 * q + r
                lo = (2 - r) * channels
                part = lax.dot_general(
                    window(sc_ref, 2 - p, 2 - q, depth, ny, lo, lo + channels),
                    w_ref[t * channels : (t + 1) * channels],
                    (((1,), (1,)), ((), ())),
                    preferred_element_type=F32,
                )
                acc = part if acc is None else acc + part
    delta = masked(acc * silu_slope(pre_ref[...]), mask_ref, 1).astype(BF)
    clear_edges(sd_ref, ny)
    store_shifted(sd_ref, 0, delta, ny, nz, channels)


def grad_one_kernel(sd_ref, int_ref, keep_ref, send_ref, g_ref):
    depth, ny, nz, channels = sd_ref.shape
    ny, area, channels = ny - 2, (ny - 2) * nz, channels // 3
    for q in range(3):
        right = window(sd_ref, 0, 2 - q, depth, ny)
        for p in range(3):
            part = jnp.dot(
                int_ref[:, p * area : (p + depth) * area], right, preferred_element_type=F32
            )
            store_taps(g_ref, p, q, part.astype(BF), channels)
    split_shards(g_ref, keep_ref, send_ref)


def third_kernel(n, sx_ref, act_ref, mask_ref, *rest):
    out_ref, w_ref, v_ref, sa_ref = rest[2 * n :]
    area, channels = mask_ref.shape[1:]
    ny, nz = sx_ref.shape[1] - 2, sx_ref.shape[2]
    depth = act_ref.shape[0] // area
    fill_weight(rest[:n], w_ref)
    fill_weight(rest[n : 2 * n], v_ref)
    clear_edges(sa_ref, ny)
    store_shifted(sa_ref, 1, act_ref[...], ny, nz, channels)
    for x0, side in ((0, 0), (1 + depth, 2)):
        pre = conv(sx_ref, w_ref, x0, 1, ny, channels)
        act = masked(pre * jax.nn.sigmoid(pre), mask_ref, side).astype(BF)
        store_shifted(sa_ref, x0, act, ny, nz, channels)
    second = conv(sa_ref, v_ref, 0, depth, ny, channels)
    out_ref[...] = masked(second, mask_ref, 1).astype(BF).reshape(out_ref.shape)


def on_ring(features, weight_one, weight_two, cotangent, block_mask):
    depth, ny, nz, channels = features.shape
    area = ny * nz
    rows = weight_one.shape[0]
    chips = len(RING)
    tiles = 2 * chips
    loss_scale = 1.0 / math.sqrt(tiles * depth * area)
    shape = jax.ShapeDtypeStruct
    scratch = pltpu.VMEM
    shards = (shape((chips * rows, channels), BF),) * 2
    weights = scratch((27 * channels, channels), BF)
    flops = 2 * depth * area * 27 * channels * channels

    def permute(pairs):
        return functools.partial(lax.ppermute, axis_name="tiles", perm=pairs)

    def along_ring(core_from, core_to):
        return permute(
            [(2 * RING[i] + core_from, 2 * RING[(i + 1) % chips] + core_to) for i in range(chips)]
            + [
                (2 * RING[i] + 1 - core_from, 2 * RING[i - 1] + 1 - core_to)
                for i in range(chips)
            ]
        )

    onward, gather_across, scatter_across = along_ring(0, 0), along_ring(1, 0), along_ring(0, 1)
    sibling = permute([(i, i ^ 1) for i in range(tiles)])
    up = permute([(i, (i + 1) % tiles) for i in range(tiles)])
    down = permute([(i, (i - 1) % tiles) for i in range(tiles)])

    def after(value, *others):
        return lax.optimization_barrier((value,) + others)[0]

    def kernel(body, name, mib, convs, outs, scratches, *operands, smem=0):
        return pl.pallas_call(
            body,
            name=name,
            out_shape=outs,
            in_specs=[pl.BlockSpec(memory_space=pltpu.SMEM)] * smem
            + [pl.BlockSpec(memory_space=pltpu.VMEM)] * (len(operands) - smem),
            out_specs=jax.tree.map(lambda _: pl.BlockSpec(memory_space=pltpu.VMEM), outs),
            scratch_shapes=scratches,
            compiler_params=pltpu.CompilerParams(vmem_limit_bytes=mib << 20),
            cost_estimate=pl.CostEstimate(
                flops=4 * convs * flops, transcendentals=0, bytes_accessed=4 << 20
            ),
        )(*operands)

    a1 = [onward(weight_one), gather_across(weight_one)]
    weight_late = after(weight_two, weight_one)
    b1 = [onward(weight_late), gather_across(weight_late)]
    features_late, cot_late, _ = lax.optimization_barrier((features, cotangent, a1[0]))
    low = up(jnp.concatenate([features_late[-2:], cot_late[-1:]]))
    high = down(jnp.concatenate([features_late[:2], cot_late[:1]]))

    a1_pair = jnp.concatenate(a1)
    a2 = onward(a1_pair)
    qa1 = sibling(a1_pair)
    b1_pair = jnp.concatenate(b1)
    b2 = onward(after(b1_pair, low, high))
    a3 = onward(after(a2, qa1, b1_pair))
    qa2 = sibling(a2)
    other_one = sibling(weight_one)
    sx, sc, in_t, near = kernel(
        prep_kernel,
        "prep",
        8,
        0,
        (
            shape((depth + 4, ny + 2, nz, 3 * channels), BF),
            shape((depth + 2, ny + 2, nz, 3 * channels), BF),
            shape((channels, (depth + 2) * area), BF),
            shape((3, area, channels), BF),
        ),
        [],
        jnp.transpose(block_mask, (1, 2, 0)),
        low,
        features,
        cotangent,
        high,
        smem=1,
    )
    a4 = onward(after(a3[:rows], qa2, other_one, sx))
    qa3, qa4 = sibling(a3), sibling(a4)
    ones = [weight_one, other_one, *a1, a2, a3, a4, qa1, qa2, qa3, qa4]
    n = len(ones)

    qb1 = sibling(b1_pair)
    b3 = onward(after(b2, qb1))
    qb2 = sibling(b2)
    other_two = sibling(weight_two)
    pre, act, act_t = kernel(
        functools.partial(first_kernel, n),
        "first",
        8,
        1,
        (
            shape((depth * area, channels), F32),
            shape((depth * area, channels), BF),
            shape((channels, depth * area), BF),
        ),
        [weights],
        after(sx, b2),
        near,
        *ones,
    )
    b4 = onward(after(b3[:rows], qb2, other_two))
    qb3, qb4 = sibling(b3), sibling(b4)
    twos = [weight_two, other_two, *b1, b2, b3, b4, qb1, qb2, qb3, qb4]
    keep_two, send_two = kernel(
        grad_two_kernel, "grad_two", 8, 1, shards, [weights], sc, after(act_t, b3)
    )
    got_two = sibling(after(send_two, b4))

    def both(keep, got, lo, hi):
        return keep[lo * rows : hi * rows].astype(F32) + got[lo * rows : hi * rows].astype(F32)

    def step(keep, got, moving, k):
        if k == 0:
            return both(keep, got, 0, 1).astype(BF)
        if k == 1:
            moving = jnp.concatenate([moving, jnp.zeros_like(moving)])
        return (both(keep, got, 2 * k - 1, 2 * k + 1) + moving.astype(F32)).astype(BF)

    def finish(keep, got, message):
        total = both(keep, got, 7, 8) + onward(message[:rows]).astype(F32)
        return (total + scatter_across(message[rows:]).astype(F32)) * loss_scale

    two = onward(step(keep_two, got_two, None, 0))
    delta = kernel(
        functools.partial(back_kernel, n),
        "back",
        8,
        1,
        shape((depth, ny + 2, nz, 3 * channels), BF),
        [weights],
        sc,
        pre,
        near,
        *twos,
    )
    keep_one, send_one = kernel(
        grad_one_kernel, "grad_one", 8, 1, shards, [weights], delta, in_t
    )
    got_one = sibling(after(send_one, two))
    act_late = after(act, two)
    two = onward(step(keep_two, got_two, two, 1))
    one = onward(step(keep_one, got_one, None, 0))
    features_out = kernel(
        functools.partial(third_kernel, n),
        "third",
        14,
        1,
        shape(features.shape, BF),
        [weights, weights, scratch((depth + 2, ny + 2, nz, 3 * channels), BF)],
        sx,
        act_late,
        near,
        *ones,
        *twos,
    )
    one = onward(after(step(keep_one, got_one, one, 1), features_out, two))
    two = onward(step(keep_two, got_two, two, 2))
    grad_two = finish(keep_two, got_two, step(keep_two, got_two, two, 3))
    one = onward(step(keep_one, got_one, one, 2))
    return (features_out, finish(keep_one, got_one, step(keep_one, got_one, one, 3)), grad_two)


def solution(mesh):
    placed = (
        P(("groups", "tiles"), None, None, None),
        P("tiles", None),
        P("tiles", None),
        P(("groups", "tiles"), None, None, None),
        P("groups", None, None),
    )
    on_device = on_ring if mesh.shape["tiles"] == 2 * len(RING) else on_any
    return jax.shard_map(
        on_device,
        mesh=mesh,
        in_specs=placed,
        out_specs=(
            P(("groups", "tiles"), None, None, None),
            P(("groups", "tiles"), None),
            P(("groups", "tiles"), None),
        ),
        check_vma=False,
    )
```

```python
import functools
import math

import jax
import jax.numpy as jnp
from jax import lax
from jax.experimental import pallas as pl
from jax.experimental.pallas import tpu as pltpu
from jax.sharding import PartitionSpec as P

B = 4
RING = (0, 2, 4, 6, 7, 5, 3, 1)
BF = jnp.bfloat16
F32 = jnp.float32


def with_halo(block, axis, width):
    count = lax.axis_size(axis)
    forward = [(i, i + 1) for i in range(count - 1)]
    backward = [(target, source) for source, target in forward]
    low = lax.ppermute(block[-width:], axis, forward)
    high = lax.ppermute(block[:width], axis, backward)
    return low, high


def tap_columns(padded, flipped):
    extent = [padded.shape[d] - 2 for d in range(3)]
    taps = []
    for a in range(3):
        for b in range(3):
            for c in range(3):
                x, y, z = (2 - a, 2 - b, 2 - c) if flipped else (a, b, c)
                taps.append(padded[x : x + extent[0], y : y + extent[1], z : z + extent[2]])
    stacked = jnp.stack(taps, axis=3)
    return stacked.reshape(extent[0] * extent[1] * extent[2], 27 * padded.shape[3])


def expand_mask(cells, edge):
    planes, rows_y, rows_z = cells.shape
    values = jnp.broadcast_to(
        cells.astype(F32)[:, None, :, None, :, None], (planes, edge, rows_y, edge, rows_z, edge)
    )
    return values.reshape(planes * edge, rows_y * edge, rows_z * edge, 1)


def silu_slope(values):
    logistic = jax.nn.sigmoid(values)
    return logistic * (1.0 + values * (1.0 - logistic))


def near_cells_of(block_mask):
    padded_cells = jnp.pad(block_mask, ((1, 1), (0, 0), (0, 0)))
    return lax.dynamic_slice_in_dim(padded_cells, lax.axis_index("tiles"), 3, 0)


def on_any(features, weight_one, weight_two, cotangent, block_mask):
    depth, width_y, width_z, channels = features.shape
    loss_scale = 1.0 / math.sqrt(lax.axis_size("tiles") * depth * width_y * width_z)
    own_mask = expand_mask(near_cells_of(block_mask), B)[depth : 2 * depth]
    own_flat = own_mask.reshape(-1, 1)

    def cube(field):
        low, high = with_halo(field, "tiles", 1)
        field = jnp.concatenate([low, field, high], axis=0)
        return jnp.pad(field, ((0, 0), (1, 1), (1, 1), (0, 0)))

    def grad_piece(columns_in, rows_in):
        product = lax.dot_general(
            columns_in, rows_in, (((0,), (0,)), ((), ())), preferred_element_type=F32
        )
        return lax.psum_scatter(product * loss_scale, "tiles", scatter_dimension=0, tiled=True)

    full_one = lax.all_gather(weight_one, "tiles", axis=0, tiled=True)
    full_two = lax.all_gather(weight_two, "tiles", axis=0, tiled=True)
    weight_back = jnp.swapaxes(full_two.reshape(27, channels, channels), 1, 2).reshape(
        27 * channels, channels
    )
    inputs = (features * own_mask).astype(BF)
    feature_cols = tap_columns(cube(inputs), False)
    hidden_pre = jnp.dot(feature_cols, full_one, preferred_element_type=F32)
    active = (jax.nn.silu(hidden_pre) * own_flat).astype(BF).reshape(features.shape)
    active_cols = tap_columns(cube(active), False)
    second = jnp.dot(active_cols, full_two, preferred_element_type=F32)
    features_out = (second * own_flat).astype(BF).reshape(features.shape)
    cot = (cotangent * own_mask).astype(BF)
    grad_two = grad_piece(active_cols, cot.reshape(-1, channels))
    upstream = jnp.dot(tap_columns(cube(cot), True), weight_back, preferred_element_type=F32)
    hidden_grad = (upstream * silu_slope(hidden_pre) * own_flat).astype(BF)
    grad_one = grad_piece(feature_cols, hidden_grad)
    return (features_out, grad_one, grad_two)


def chip_at(place):
    return jnp.where(place < 4, 2 * place, 15 - 2 * place)


def place_of(tile):
    chip = tile // 2
    return jnp.where(chip % 2 == 0, chip // 2, 7 - chip // 2)


def shard_rows(tile, core, hop, flip, rows):
    step = jnp.where(core == 0, -hop, hop)
    chip = chip_at((place_of(tile) + step + 8) % 8)
    return pl.multiple_of((2 * chip + (1 - core if flip else core)) * rows, 16)


def store_shifted(out_ref, x0, rows, ny, nz, channels):
    planes = rows.shape[0] // (ny * nz)
    wide = rows.astype(F32)
    z = lax.broadcasted_iota(jnp.int32, wide.shape, 0) % nz
    before = jnp.where(z == 0, 0.0, pltpu.roll(wide, 1, 0)).astype(BF)
    after = jnp.where(z == nz - 1, 0.0, pltpu.roll(wide, wide.shape[0] - 1, 0)).astype(BF)
    for rho, value in enumerate((before, rows.astype(BF), after)):
        out_ref[x0 : x0 + planes, 1 : ny + 1, :, rho * channels : (rho + 1) * channels] = (
            value.reshape(planes, ny, nz, channels)
        )


def clear_edges(out_ref, ny):
    edge = jnp.zeros((out_ref.shape[0], 1) + tuple(out_ref.shape[2:]), BF)
    out_ref[:, 0:1] = edge
    out_ref[:, ny + 1 : ny + 2] = edge


def prep_kernel(cells_ref, low, f_own, c_own, high, sx_ref, sc_ref, int_ref, mask_ref):
    depth, ny, nz, channels = f_own.shape
    area = ny * nz
    tile = lax.axis_index("tiles")
    last = cells_ref.shape[2] - 1
    row = lax.broadcasted_iota(jnp.int32, (area, channels), 0)
    block_y, block_z = row // (B * nz), (row % nz) // B
    m = []
    for i in range(3):
        at = tile + i - 1
        inside = jnp.logical_and(at >= 0, at <= last)
        at = jnp.clip(at, 0, last)
        value = jnp.zeros((area, channels), F32)
        for y in range(ny // B):
            for z in range(nz // B):
                cell = jnp.where(inside, cells_ref[y, z, at], 0).astype(F32)
                here = jnp.logical_and(block_y == y, block_z == z)
                value = jnp.where(here, cell, value)
        value = value.astype(BF)
        mask_ref[i] = value
        m.append(value.reshape(1, area, channels))

    def rows(value, side):
        planes = value.shape[0]
        value = value.reshape(planes, area, channels) * m[side]
        return value.reshape(planes * area, channels)

    clear_edges(sx_ref, ny)
    clear_edges(sc_ref, ny)
    fs = [rows(low[0:2], 0), rows(f_own[...], 1), rows(high[0:2], 2)]
    for x0, value in zip((0, 2, 2 + depth), fs):
        store_shifted(sx_ref, x0, value, ny, nz, channels)
    int_ref[:, 0:area] = fs[0][area:].T
    int_ref[:, area : area + depth * area] = fs[1].T
    int_ref[:, area + depth * area :] = fs[2][:area].T
    for x0, value, side in ((0, low[2:3], 0), (1, c_own[...], 1), (1 + depth, high[2:3], 2)):
        store_shifted(sc_ref, x0, rows(value, side), ny, nz, channels)


PIECES = (
    (0, False, False),
    (0, False, True),
    (1, False, False),
    (1, False, True),
    (2, False, False),
    (3, False, False),
    (4, False, False),
    (1, True, False),
    (2, True, False),
    (3, True, False),
    (4, True, False),
)


def fill_weight(pieces, w_ref):
    tile = lax.axis_index("tiles")
    core = tile % 2
    rows = w_ref.shape[0] // 16
    for piece, (hop, crossed, flip) in zip(pieces, PIECES):
        holder = 1 - core if crossed else core
        for half in range(piece.shape[0] // rows):
            start = shard_rows(tile, holder, hop, flip or half == 1, rows)
            w_ref[pl.ds(start, rows)] = piece[half * rows : (half + 1) * rows]


def split_shards(g_ref, keep_ref, send_ref):
    tile = lax.axis_index("tiles")
    core = tile % 2
    rows = g_ref.shape[0] // 16
    for out_ref, holder in ((send_ref, 1 - core), (keep_ref, core)):
        at = 0
        for hop in (4, 3, 2, 1, 0):
            for flip in (False,) if hop in (0, 4) else (False, True):
                start = shard_rows(tile, holder, -hop, flip, rows)
                out_ref[at : at + rows] = g_ref[pl.ds(start, rows)]
                at += rows


def window(ref, x, y, planes, ny, lo=0, hi=None):
    value = ref[x : x + planes, y : y + ny, :, lo:hi]
    return value.reshape(-1, value.shape[-1])


def conv(s_ref, w_ref, x0, planes, ny, channels):
    acc = None
    for p in range(3):
        for q in range(3):
            t = 9 * p + 3 * q
            part = jnp.dot(
                window(s_ref, x0 + p, q, planes, ny),
                w_ref[t * channels : (t + 3) * channels],
                preferred_element_type=F32,
            )
            acc = part if acc is None else acc + part
    return acc


def store_taps(g_ref, p, q, part, channels):
    for rho in range(3):
        t = 9 * p + 3 * q + 2 - rho
        g_ref[t * channels : (t + 1) * channels] = part[:, rho * channels : (rho + 1) * channels]


def masked(value, mask_ref, side):
    area, channels = mask_ref.shape[1:]
    own = mask_ref[side].reshape(1, area, channels).astype(F32)
    return (value.reshape(-1, area, channels) * own).reshape(-1, channels)


def first_kernel(n, sx_ref, mask_ref, *rest):
    pieces, (pre_ref, act_ref, act_t_ref, w_ref) = rest[:n], rest[n:]
    area, channels = mask_ref.shape[1:]
    ny = sx_ref.shape[1] - 2
    depth = pre_ref.shape[0] // area
    fill_weight(pieces, w_ref)
    pre = conv(sx_ref, w_ref, 1, depth, ny, channels)
    pre_ref[...] = pre
    act = masked(pre * jax.nn.sigmoid(pre), mask_ref, 1).astype(BF)
    act_ref[...] = act
    act_t_ref[...] = act.T


def grad_two_kernel(sc_ref, act_t_ref, keep_ref, send_ref, g_ref):
    depth, ny, nz, channels = sc_ref.shape
    depth, ny, channels = depth - 2, ny - 2, channels // 3
    for p in range(3):
        for q in range(3):
            part = jnp.dot(
                act_t_ref[...],
                window(sc_ref, 2 - p, 2 - q, depth, ny),
                preferred_element_type=F32,
            )
            store_taps(g_ref, p, q, part.astype(BF), channels)
    split_shards(g_ref, keep_ref, send_ref)


def back_kernel(n, sc_ref, pre_ref, mask_ref, *rest):
    pieces, (sd_ref, w_ref) = rest[:n], rest[n:]
    area, channels = mask_ref.shape[1:]
    ny, nz = sc_ref.shape[1] - 2, sc_ref.shape[2]
    depth = pre_ref.shape[0] // area
    fill_weight(pieces, w_ref)
    acc = None
    for p in range(3):
        for q in range(3):
            for r in range(3):
                t = 9 * p + 3 * q + r
                lo = (2 - r) * channels
                part = lax.dot_general(
                    window(sc_ref, 2 - p, 2 - q, depth, ny, lo, lo + channels),
                    w_ref[t * channels : (t + 1) * channels],
                    (((1,), (1,)), ((), ())),
                    preferred_element_type=F32,
                )
                acc = part if acc is None else acc + part
    delta = masked(acc * silu_slope(pre_ref[...]), mask_ref, 1).astype(BF)
    clear_edges(sd_ref, ny)
    store_shifted(sd_ref, 0, delta, ny, nz, channels)


def grad_one_kernel(sd_ref, int_ref, keep_ref, send_ref, g_ref):
    depth, ny, nz, channels = sd_ref.shape
    ny, area, channels = ny - 2, (ny - 2) * nz, channels // 3
    for q in range(3):
        right = window(sd_ref, 0, 2 - q, depth, ny)
        for p in range(3):
            part = jnp.dot(
                int_ref[:, p * area : (p + depth) * area], right, preferred_element_type=F32
            )
            store_taps(g_ref, p, q, part.astype(BF), channels)
    split_shards(g_ref, keep_ref, send_ref)


def third_kernel(n, sx_ref, act_ref, mask_ref, *rest):
    out_ref, w_ref, v_ref, sa_ref = rest[2 * n :]
    area, channels = mask_ref.shape[1:]
    ny, nz = sx_ref.shape[1] - 2, sx_ref.shape[2]
    depth = act_ref.shape[0] // area
    fill_weight(rest[:n], w_ref)
    fill_weight(rest[n : 2 * n], v_ref)
    clear_edges(sa_ref, ny)
    store_shifted(sa_ref, 1, act_ref[...], ny, nz, channels)
    for x0, side in ((0, 0), (1 + depth, 2)):
        pre = conv(sx_ref, w_ref, x0, 1, ny, channels)
        act = masked(pre * jax.nn.sigmoid(pre), mask_ref, side).astype(BF)
        store_shifted(sa_ref, x0, act, ny, nz, channels)
    second = conv(sa_ref, v_ref, 0, depth, ny, channels)
    out_ref[...] = masked(second, mask_ref, 1).astype(BF).reshape(out_ref.shape)


def on_ring(features, weight_one, weight_two, cotangent, block_mask):
    depth, ny, nz, channels = features.shape
    area = ny * nz
    rows = weight_one.shape[0]
    chips = len(RING)
    tiles = 2 * chips
    loss_scale = 1.0 / math.sqrt(tiles * depth * area)
    shape = jax.ShapeDtypeStruct
    scratch = pltpu.VMEM
    shards = (shape((chips * rows, channels), BF),) * 2
    weights = scratch((27 * channels, channels), BF)
    flops = 2 * depth * area * 27 * channels * channels

    def permute(pairs):
        return functools.partial(lax.ppermute, axis_name="tiles", perm=pairs)

    def along_ring(core_from, core_to):
        return permute(
            [(2 * RING[i] + core_from, 2 * RING[(i + 1) % chips] + core_to) for i in range(chips)]
            + [
                (2 * RING[i] + 1 - core_from, 2 * RING[i - 1] + 1 - core_to)
                for i in range(chips)
            ]
        )

    onward, gather_across, scatter_across = along_ring(0, 0), along_ring(1, 0), along_ring(0, 1)
    sibling = permute([(i, i ^ 1) for i in range(tiles)])
    up = permute([(i, (i + 1) % tiles) for i in range(tiles)])
    down = permute([(i, (i - 1) % tiles) for i in range(tiles)])

    def after(value, *others):
        return lax.optimization_barrier((value,) + others)[0]

    def kernel(body, name, mib, convs, outs, scratches, *operands, smem=0):
        return pl.pallas_call(
            body,
            name=name,
            out_shape=outs,
            in_specs=[pl.BlockSpec(memory_space=pltpu.SMEM)] * smem
            + [pl.BlockSpec(memory_space=pltpu.VMEM)] * (len(operands) - smem),
            out_specs=jax.tree.map(lambda _: pl.BlockSpec(memory_space=pltpu.VMEM), outs),
            scratch_shapes=scratches,
            compiler_params=pltpu.CompilerParams(vmem_limit_bytes=mib << 20),
            cost_estimate=pl.CostEstimate(
                flops=convs * flops, transcendentals=0, bytes_accessed=4 << 20
            ),
        )(*operands)

    a1 = [onward(weight_one), gather_across(weight_one)]
    weight_late = after(weight_two, a1[0])
    b1 = [onward(weight_late), gather_across(weight_late)]
    low = up(jnp.concatenate([features[-2:], cotangent[-1:]]))
    high = down(jnp.concatenate([features[:2], cotangent[:1]]))

    a1_pair = after(jnp.concatenate(a1), low, high)
    a2 = onward(a1_pair)
    qa1 = sibling(a1_pair)
    b1_pair = jnp.concatenate(b1)
    b2 = onward(b1_pair)
    a3 = onward(after(a2, qa1, b1_pair))
    qa2 = sibling(a2)
    other_one = sibling(weight_one)
    sx, sc, in_t, near = kernel(
        prep_kernel,
        "prep",
        8,
        0,
        (
            shape((depth + 4, ny + 2, nz, 3 * channels), BF),
            shape((depth + 2, ny + 2, nz, 3 * channels), BF),
            shape((channels, (depth + 2) * area), BF),
            shape((3, area, channels), BF),
        ),
        [],
        jnp.transpose(block_mask, (1, 2, 0)),
        low,
        features,
        cotangent,
        high,
        smem=1,
    )
    a4 = onward(after(a3[:rows], qa2, other_one, sx))
    qa3, qa4 = sibling(a3), sibling(a4)
    ones = [weight_one, other_one, *a1, a2, a3, a4, qa1, qa2, qa3, qa4]
    n = len(ones)

    qb1 = sibling(b1_pair)
    b3 = onward(after(b2, qb1))
    qb2 = sibling(b2)
    other_two = sibling(weight_two)
    pre, act, act_t = kernel(
        functools.partial(first_kernel, n),
        "first",
        8,
        1,
        (
            shape((depth * area, channels), F32),
            shape((depth * area, channels), BF),
            shape((channels, depth * area), BF),
        ),
        [weights],
        after(sx, b2),
        near,
        *ones,
    )
    b4 = onward(after(b3[:rows], qb2, other_two, act_t))
    qb3, qb4 = sibling(b3), sibling(b4)
    twos = [weight_two, other_two, *b1, b2, b3, b4, qb1, qb2, qb3, qb4]
    keep_two, send_two = kernel(
        grad_two_kernel, "grad_two", 8, 1, shards, [weights], sc, after(act_t, b3)
    )
    got_two = sibling(after(send_two, b4))

    def both(keep, got, lo, hi):
        return keep[lo * rows : hi * rows].astype(F32) + got[lo * rows : hi * rows].astype(F32)

    def step(keep, got, moving, k):
        if k == 0:
            return both(keep, got, 0, 1).astype(BF)
        if k == 1:
            moving = jnp.concatenate([moving, jnp.zeros_like(moving)])
        return (both(keep, got, 2 * k - 1, 2 * k + 1) + moving.astype(F32)).astype(BF)

    def finish(keep, got, message):
        total = both(keep, got, 7, 8) + onward(message[:rows]).astype(F32)
        return (total + scatter_across(message[rows:]).astype(F32)) * loss_scale

    two = onward(step(keep_two, got_two, None, 0))
    delta = kernel(
        functools.partial(back_kernel, n),
        "back",
        8,
        1,
        shape((depth, ny + 2, nz, 3 * channels), BF),
        [weights],
        sc,
        pre,
        near,
        *twos,
    )
    keep_one, send_one = kernel(
        grad_one_kernel, "grad_one", 8, 1, shards, [weights], delta, in_t
    )
    got_one = sibling(after(send_one, two))
    act_late = after(act, two)
    two = onward(step(keep_two, got_two, two, 1))
    one = onward(step(keep_one, got_one, None, 0))
    features_out = kernel(
        functools.partial(third_kernel, n),
        "third",
        14,
        4,
        shape(features.shape, BF),
        [weights, weights, scratch((depth + 2, ny + 2, nz, 3 * channels), BF)],
        sx,
        act_late,
        near,
        *ones,
        *twos,
    )
    one = onward(after(step(keep_one, got_one, one, 1), features_out, two))
    two = onward(step(keep_two, got_two, two, 2))
    grad_two = finish(keep_two, got_two, step(keep_two, got_two, two, 3))
    one = onward(step(keep_one, got_one, one, 2))
    return (features_out, finish(keep_one, got_one, step(keep_one, got_one, one, 3)), grad_two)


def solution(mesh):
    placed = (
        P(("groups", "tiles"), None, None, None),
        P("tiles", None),
        P("tiles", None),
        P(("groups", "tiles"), None, None, None),
        P("groups", None, None),
    )
    on_device = on_ring if mesh.shape["tiles"] == 2 * len(RING) else on_any
    return jax.shard_map(
        on_device,
        mesh=mesh,
        in_specs=placed,
        out_specs=(
            P(("groups", "tiles"), None, None, None),
            P(("groups", "tiles"), None),
            P(("groups", "tiles"), None),
        ),
        check_vma=False,
    )
```

```python
import functools
import math

import jax
import jax.numpy as jnp
from jax import lax
from jax.experimental import pallas as pl
from jax.experimental.pallas import tpu as pltpu
from jax.sharding import PartitionSpec as P

B = 4
RING = (0, 2, 4, 6, 7, 5, 3, 1)
BF = jnp.bfloat16
F32 = jnp.float32


def with_halo(block, axis, width):
    count = lax.axis_size(axis)
    forward = [(i, i + 1) for i in range(count - 1)]
    backward = [(target, source) for source, target in forward]
    low = lax.ppermute(block[-width:], axis, forward)
    high = lax.ppermute(block[:width], axis, backward)
    return low, high


def tap_columns(padded, flipped):
    extent = [padded.shape[d] - 2 for d in range(3)]
    taps = []
    for a in range(3):
        for b in range(3):
            for c in range(3):
                x, y, z = (2 - a, 2 - b, 2 - c) if flipped else (a, b, c)
                taps.append(padded[x : x + extent[0], y : y + extent[1], z : z + extent[2]])
    stacked = jnp.stack(taps, axis=3)
    return stacked.reshape(extent[0] * extent[1] * extent[2], 27 * padded.shape[3])


def expand_mask(cells, edge):
    planes, rows_y, rows_z = cells.shape
    values = jnp.broadcast_to(
        cells.astype(F32)[:, None, :, None, :, None], (planes, edge, rows_y, edge, rows_z, edge)
    )
    return values.reshape(planes * edge, rows_y * edge, rows_z * edge, 1)


def silu_slope(values):
    logistic = jax.nn.sigmoid(values)
    return logistic * (1.0 + values * (1.0 - logistic))


def near_cells_of(block_mask):
    padded_cells = jnp.pad(block_mask, ((1, 1), (0, 0), (0, 0)))
    return lax.dynamic_slice_in_dim(padded_cells, lax.axis_index("tiles"), 3, 0)


def on_any(features, weight_one, weight_two, cotangent, block_mask):
    depth, width_y, width_z, channels = features.shape
    loss_scale = 1.0 / math.sqrt(lax.axis_size("tiles") * depth * width_y * width_z)
    own_mask = expand_mask(near_cells_of(block_mask), B)[depth : 2 * depth]
    own_flat = own_mask.reshape(-1, 1)

    def cube(field):
        low, high = with_halo(field, "tiles", 1)
        field = jnp.concatenate([low, field, high], axis=0)
        return jnp.pad(field, ((0, 0), (1, 1), (1, 1), (0, 0)))

    def grad_piece(columns_in, rows_in):
        product = lax.dot_general(
            columns_in, rows_in, (((0,), (0,)), ((), ())), preferred_element_type=F32
        )
        return lax.psum_scatter(product * loss_scale, "tiles", scatter_dimension=0, tiled=True)

    full_one = lax.all_gather(weight_one, "tiles", axis=0, tiled=True)
    full_two = lax.all_gather(weight_two, "tiles", axis=0, tiled=True)
    weight_back = jnp.swapaxes(full_two.reshape(27, channels, channels), 1, 2).reshape(
        27 * channels, channels
    )
    inputs = (features * own_mask).astype(BF)
    feature_cols = tap_columns(cube(inputs), False)
    hidden_pre = jnp.dot(feature_cols, full_one, preferred_element_type=F32)
    active = (jax.nn.silu(hidden_pre) * own_flat).astype(BF).reshape(features.shape)
    active_cols = tap_columns(cube(active), False)
    second = jnp.dot(active_cols, full_two, preferred_element_type=F32)
    features_out = (second * own_flat).astype(BF).reshape(features.shape)
    cot = (cotangent * own_mask).astype(BF)
    grad_two = grad_piece(active_cols, cot.reshape(-1, channels))
    upstream = jnp.dot(tap_columns(cube(cot), True), weight_back, preferred_element_type=F32)
    hidden_grad = (upstream * silu_slope(hidden_pre) * own_flat).astype(BF)
    grad_one = grad_piece(feature_cols, hidden_grad)
    return (features_out, grad_one, grad_two)


def chip_at(place):
    return jnp.where(place < 4, 2 * place, 15 - 2 * place)


def place_of(tile):
    chip = tile // 2
    return jnp.where(chip % 2 == 0, chip // 2, 7 - chip // 2)


def shard_rows(tile, core, hop, flip, rows):
    step = jnp.where(core == 0, -hop, hop)
    chip = chip_at((place_of(tile) + step + 8) % 8)
    return pl.multiple_of((2 * chip + (1 - core if flip else core)) * rows, 16)


def store_shifted(out_ref, x0, rows, ny, nz, channels):
    planes = rows.shape[0] // (ny * nz)
    wide = rows.astype(F32)
    z = lax.broadcasted_iota(jnp.int32, wide.shape, 0) % nz
    before = jnp.where(z == 0, 0.0, pltpu.roll(wide, 1, 0)).astype(BF)
    after = jnp.where(z == nz - 1, 0.0, pltpu.roll(wide, wide.shape[0] - 1, 0)).astype(BF)
    for rho, value in enumerate((before, rows.astype(BF), after)):
        out_ref[x0 : x0 + planes, 1 : ny + 1, :, rho * channels : (rho + 1) * channels] = (
            value.reshape(planes, ny, nz, channels)
        )


def clear_edges(out_ref, ny):
    edge = jnp.zeros((out_ref.shape[0], 1) + tuple(out_ref.shape[2:]), BF)
    out_ref[:, 0:1] = edge
    out_ref[:, ny + 1 : ny + 2] = edge


def prep_kernel(cells_ref, low, f_own, c_own, high, sx_ref, sc_ref, int_ref, mask_ref):
    depth, ny, nz, channels = f_own.shape
    area = ny * nz
    tile = lax.axis_index("tiles")
    last = cells_ref.shape[2] - 1
    row = lax.broadcasted_iota(jnp.int32, (area, channels), 0)
    block_y, block_z = row // (B * nz), (row % nz) // B
    m = []
    for i in range(3):
        at = tile + i - 1
        inside = jnp.logical_and(at >= 0, at <= last)
        at = jnp.clip(at, 0, last)
        value = jnp.zeros((area, channels), F32)
        for y in range(ny // B):
            for z in range(nz // B):
                cell = jnp.where(inside, cells_ref[y, z, at], 0).astype(F32)
                here = jnp.logical_and(block_y == y, block_z == z)
                value = jnp.where(here, cell, value)
        value = value.astype(BF)
        mask_ref[i] = value
        m.append(value.reshape(1, area, channels))

    def rows(value, side):
        planes = value.shape[0]
        value = value.reshape(planes, area, channels) * m[side]
        return value.reshape(planes * area, channels)

    clear_edges(sx_ref, ny)
    clear_edges(sc_ref, ny)
    fs = [rows(low[0:2], 0), rows(f_own[...], 1), rows(high[0:2], 2)]
    for x0, value in zip((0, 2, 2 + depth), fs):
        store_shifted(sx_ref, x0, value, ny, nz, channels)
    int_ref[:, 0:area] = fs[0][area:].T
    int_ref[:, area : area + depth * area] = fs[1].T
    int_ref[:, area + depth * area :] = fs[2][:area].T
    for x0, value, side in ((0, low[2:3], 0), (1, c_own[...], 1), (1 + depth, high[2:3], 2)):
        store_shifted(sc_ref, x0, rows(value, side), ny, nz, channels)


PAIRS = (
    (0, False, False),
    (0, False, True),
    (1, False, False),
    (2, False, False),
    (3, False, False),
    (4, False, False),
    (1, True, False),
    (2, True, False),
    (3, True, False),
    (4, True, False),
)
SHARDS = PAIRS[:2] + tuple((hop, False, flip) for hop in (1, 2, 3) for flip in (False, True)) + PAIRS[5:]


def fill_weight(kinds, pieces, w_ref):
    tile = lax.axis_index("tiles")
    core = tile % 2
    rows = w_ref.shape[0] // 16
    for piece, (hop, crossed, flip) in zip(pieces, kinds):
        holder = 1 - core if crossed else core
        for half in range(piece.shape[0] // rows):
            start = shard_rows(tile, holder, hop, flip or half == 1, rows)
            w_ref[pl.ds(start, rows)] = piece[half * rows : (half + 1) * rows]


def split_shards(g_ref, keep_ref, send_ref):
    tile = lax.axis_index("tiles")
    core = tile % 2
    rows = g_ref.shape[0] // 16
    for out_ref, holder in ((send_ref, 1 - core), (keep_ref, core)):
        at = 0
        for hop in (4, 3, 2, 1, 0):
            for flip in (False,) if hop in (0, 4) else (False, True):
                start = shard_rows(tile, holder, -hop, flip, rows)
                out_ref[at : at + rows] = g_ref[pl.ds(start, rows)]
                at += rows


def window(ref, x, y, planes, ny, lo=0, hi=None):
    value = ref[x : x + planes, y : y + ny, :, lo:hi]
    return value.reshape(-1, value.shape[-1])


def conv(s_ref, w_ref, x0, planes, ny, channels):
    acc = None
    for p in range(3):
        for q in range(3):
            t = 9 * p + 3 * q
            part = jnp.dot(
                window(s_ref, x0 + p, q, planes, ny),
                w_ref[t * channels : (t + 3) * channels],
                preferred_element_type=F32,
            )
            acc = part if acc is None else acc + part
    return acc


def store_taps(g_ref, p, q, part, channels):
    for rho in range(3):
        t = 9 * p + 3 * q + 2 - rho
        g_ref[t * channels : (t + 1) * channels] = part[:, rho * channels : (rho + 1) * channels]


def masked(value, mask_ref, side):
    area, channels = mask_ref.shape[1:]
    own = mask_ref[side].reshape(1, area, channels).astype(F32)
    return (value.reshape(-1, area, channels) * own).reshape(-1, channels)


def first_kernel(sx_ref, mask_ref, *rest):
    n = len(PAIRS)
    pieces, (pre_ref, act_ref, act_t_ref, w_ref) = rest[:n], rest[n:]
    area, channels = mask_ref.shape[1:]
    ny = sx_ref.shape[1] - 2
    depth = pre_ref.shape[0] // area
    fill_weight(PAIRS, pieces, w_ref)
    pre = conv(sx_ref, w_ref, 1, depth, ny, channels)
    pre_ref[...] = pre
    act = masked(pre * jax.nn.sigmoid(pre), mask_ref, 1).astype(BF)
    act_ref[...] = act
    act_t_ref[...] = act.T


def grad_two_kernel(sc_ref, act_t_ref, keep_ref, send_ref, g_ref):
    depth, ny, nz, channels = sc_ref.shape
    depth, ny, channels = depth - 2, ny - 2, channels // 3
    for p in range(3):
        for q in range(3):
            part = jnp.dot(
                act_t_ref[...],
                window(sc_ref, 2 - p, 2 - q, depth, ny),
                preferred_element_type=F32,
            )
            store_taps(g_ref, p, q, part.astype(BF), channels)
    split_shards(g_ref, keep_ref, send_ref)


def back_kernel(sc_ref, pre_ref, mask_ref, *rest):
    n = len(SHARDS)
    pieces, (sd_ref, w_ref) = rest[:n], rest[n:]
    area, channels = mask_ref.shape[1:]
    ny, nz = sc_ref.shape[1] - 2, sc_ref.shape[2]
    depth = pre_ref.shape[0] // area
    fill_weight(SHARDS, pieces, w_ref)
    acc = None
    for p in range(3):
        for q in range(3):
            for r in range(3):
                t = 9 * p + 3 * q + r
                lo = (2 - r) * channels
                part = lax.dot_general(
                    window(sc_ref, 2 - p, 2 - q, depth, ny, lo, lo + channels),
                    w_ref[t * channels : (t + 1) * channels],
                    (((1,), (1,)), ((), ())),
                    preferred_element_type=F32,
                )
                acc = part if acc is None else acc + part
    delta = masked(acc * silu_slope(pre_ref[...]), mask_ref, 1).astype(BF)
    clear_edges(sd_ref, ny)
    store_shifted(sd_ref, 0, delta, ny, nz, channels)


def grad_one_kernel(sd_ref, int_ref, keep_ref, send_ref, g_ref):
    depth, ny, nz, channels = sd_ref.shape
    ny, area, channels = ny - 2, (ny - 2) * nz, channels // 3
    for q in range(3):
        right = window(sd_ref, 0, 2 - q, depth, ny)
        for p in range(3):
            part = jnp.dot(
                int_ref[:, p * area : (p + depth) * area], right, preferred_element_type=F32
            )
            store_taps(g_ref, p, q, part.astype(BF), channels)
    split_shards(g_ref, keep_ref, send_ref)


def third_kernel(sx_ref, act_ref, mask_ref, *rest):
    n = len(PAIRS)
    pieces, (out_ref, w_ref, v_ref, sa_ref) = rest[:-4], rest[-4:]
    area, channels = mask_ref.shape[1:]
    ny, nz = sx_ref.shape[1] - 2, sx_ref.shape[2]
    depth = act_ref.shape[0] // area
    fill_weight(PAIRS, pieces[:n], w_ref)
    fill_weight(SHARDS, pieces[n:], v_ref)
    clear_edges(sa_ref, ny)
    store_shifted(sa_ref, 1, act_ref[...], ny, nz, channels)
    for x0, side in ((0, 0), (1 + depth, 2)):
        pre = conv(sx_ref, w_ref, x0, 1, ny, channels)
        act = masked(pre * jax.nn.sigmoid(pre), mask_ref, side).astype(BF)
        store_shifted(sa_ref, x0, act, ny, nz, channels)
    second = conv(sa_ref, v_ref, 0, depth, ny, channels)
    out_ref[...] = masked(second, mask_ref, 1).astype(BF).reshape(out_ref.shape)


def on_ring(features, weight_one, weight_two, cotangent, block_mask):
    depth, ny, nz, channels = features.shape
    area = ny * nz
    rows = weight_one.shape[0]
    chips = len(RING)
    tiles = 2 * chips
    loss_scale = 1.0 / math.sqrt(tiles * depth * area)
    shape = jax.ShapeDtypeStruct
    scratch = pltpu.VMEM
    shards = (shape((chips * rows, channels), BF),) * 2
    weights = scratch((27 * channels, channels), BF)
    flops = 2 * depth * area * 27 * channels * channels

    def permute(pairs):
        return functools.partial(lax.ppermute, axis_name="tiles", perm=pairs)

    def along_ring(core_from, core_to):
        return permute(
            [(2 * RING[i] + core_from, 2 * RING[(i + 1) % chips] + core_to) for i in range(chips)]
            + [
                (2 * RING[i] + 1 - core_from, 2 * RING[i - 1] + 1 - core_to)
                for i in range(chips)
            ]
        )

    onward, gather_across, scatter_across = along_ring(0, 0), along_ring(1, 0), along_ring(0, 1)
    sibling = permute([(i, i ^ 1) for i in range(tiles)])
    up = permute([(i, (i + 1) % tiles) for i in range(tiles)])
    down = permute([(i, (i - 1) % tiles) for i in range(tiles)])

    def after(value, *others):
        return lax.optimization_barrier((value,) + others)[0]

    def kernel(body, name, mib, convs, outs, scratches, *operands, smem=0):
        return pl.pallas_call(
            body,
            name=name,
            out_shape=outs,
            in_specs=[pl.BlockSpec(memory_space=pltpu.SMEM)] * smem
            + [pl.BlockSpec(memory_space=pltpu.VMEM)] * (len(operands) - smem),
            out_specs=jax.tree.map(lambda _: pl.BlockSpec(memory_space=pltpu.VMEM), outs),
            scratch_shapes=scratches,
            compiler_params=pltpu.CompilerParams(vmem_limit_bytes=mib << 20),
            cost_estimate=pl.CostEstimate(
                flops=convs * flops, transcendentals=0, bytes_accessed=4 << 20
            ),
        )(*operands)

    a1 = [onward(weight_one), gather_across(weight_one)]
    x1 = onward(after(weight_two, a1[0]))
    low = up(jnp.concatenate([features[-2:], cotangent[-1:]]))
    high = down(jnp.concatenate([features[:2], cotangent[:1]]))
    a1 = jnp.concatenate(a1)
    a2 = onward(a1)
    qa1 = sibling(a1)
    y1 = gather_across(after(weight_two, a1))
    a3 = onward(after(a2, x1, low, high))
    qa2 = sibling(a2)
    other_one = sibling(weight_one)
    x2 = onward(after(x1, a2))
    sx, sc, in_t, near = kernel(
        prep_kernel,
        "prep",
        8,
        0,
        (
            shape((depth + 4, ny + 2, nz, 3 * channels), BF),
            shape((depth + 2, ny + 2, nz, 3 * channels), BF),
            shape((channels, (depth + 2) * area), BF),
            shape((3, area, channels), BF),
        ),
        [],
        jnp.transpose(block_mask, (1, 2, 0)),
        low,
        features,
        cotangent,
        high,
        smem=1,
    )
    a4 = onward(after(a3[:rows], y1, qa1, qa2, other_one, sx))
    qa3, qa4 = sibling(a3), sibling(a4)
    ones = [weight_one, other_one, a1, a2, a3, a4, qa1, qa2, qa3, qa4]

    y2 = onward(after(y1, a3))
    qb1 = sibling(jnp.concatenate([x1, y1]))
    other_two = sibling(weight_two)
    x3 = onward(after(x2, qb1, other_two))
    pre, act, act_t = kernel(
        first_kernel,
        "first",
        8,
        1,
        (
            shape((depth * area, channels), F32),
            shape((depth * area, channels), BF),
            shape((channels, depth * area), BF),
        ),
        [weights],
        after(sx, x2),
        near,
        *ones,
    )
    qb2 = sibling(jnp.concatenate([x2, y2]))
    keep_two, send_two = kernel(
        grad_two_kernel, "grad_two", 8, 1, shards, [weights], sc, after(act_t, y2)
    )
    got_two = sibling(after(send_two, x3))
    y3 = onward(after(y2, act_t))
    x4 = onward(after(x3, qb2))
    def both(keep, got, lo, hi):
        return keep[lo * rows : hi * rows].astype(F32) + got[lo * rows : hi * rows].astype(F32)

    def step(keep, got, moving, k):
        if k == 0:
            return both(keep, got, 0, 1).astype(BF)
        if k == 1:
            moving = jnp.concatenate([moving, jnp.zeros_like(moving)])
        return (both(keep, got, 2 * k - 1, 2 * k + 1) + moving.astype(F32)).astype(BF)

    def finish(keep, got, message):
        total = both(keep, got, 7, 8) + onward(message[:rows]).astype(F32)
        return (total + scatter_across(message[rows:]).astype(F32)) * loss_scale

    message = step(keep_two, got_two, None, 0)
    two = onward(message)
    qb3 = sibling(jnp.concatenate([x3, after(y3, message)]))
    qb4 = sibling(x4)
    twos = [weight_two, other_two, x1, y1, x2, y2, x3, y3, x4, qb1, qb2, qb3, qb4]
    delta = kernel(
        back_kernel,
        "back",
        8,
        1,
        shape((depth, ny + 2, nz, 3 * channels), BF),
        [weights],
        sc,
        pre,
        near,
        *twos,
    )
    keep_one, send_one = kernel(
        grad_one_kernel, "grad_one", 8, 1, shards, [weights], delta, in_t
    )
    got_one = sibling(after(send_one, two))
    act_late = after(act, two)
    two = onward(step(keep_two, got_two, two, 1))
    one = onward(step(keep_one, got_one, None, 0))
    features_out = kernel(
        third_kernel,
        "third",
        14,
        4,
        shape(features.shape, BF),
        [weights, weights, scratch((depth + 2, ny + 2, nz, 3 * channels), BF)],
        sx,
        act_late,
        near,
        *ones,
        *twos,
    )
    one = onward(after(step(keep_one, got_one, one, 1), features_out, two))
    two = onward(step(keep_two, got_two, two, 2))
    grad_two = finish(keep_two, got_two, step(keep_two, got_two, two, 3))
    one = onward(step(keep_one, got_one, one, 2))
    return (features_out, finish(keep_one, got_one, step(keep_one, got_one, one, 3)), grad_two)


def solution(mesh):
    placed = (
        P(("groups", "tiles"), None, None, None),
        P("tiles", None),
        P("tiles", None),
        P(("groups", "tiles"), None, None, None),
        P("groups", None, None),
    )
    on_device = on_ring if mesh.shape["tiles"] == 2 * len(RING) else on_any
    return jax.shard_map(
        on_device,
        mesh=mesh,
        in_specs=placed,
        out_specs=(
            P(("groups", "tiles"), None, None, None),
            P(("groups", "tiles"), None),
            P(("groups", "tiles"), None),
        ),
        check_vma=False,
    )
```

```python
import functools
import math

import jax
import jax.numpy as jnp
from jax import lax
from jax.experimental import pallas as pl
from jax.experimental.pallas import tpu as pltpu
from jax.sharding import PartitionSpec as P

B = 4
RING = (0, 2, 4, 6, 7, 5, 3, 1)
BF = jnp.bfloat16
F32 = jnp.float32


def with_halo(block, axis, width):
    count = lax.axis_size(axis)
    forward = [(i, i + 1) for i in range(count - 1)]
    backward = [(target, source) for source, target in forward]
    low = lax.ppermute(block[-width:], axis, forward)
    high = lax.ppermute(block[:width], axis, backward)
    return low, high


def tap_columns(padded, flipped):
    extent = [padded.shape[d] - 2 for d in range(3)]
    taps = []
    for a in range(3):
        for b in range(3):
            for c in range(3):
                x, y, z = (2 - a, 2 - b, 2 - c) if flipped else (a, b, c)
                taps.append(padded[x : x + extent[0], y : y + extent[1], z : z + extent[2]])
    stacked = jnp.stack(taps, axis=3)
    return stacked.reshape(extent[0] * extent[1] * extent[2], 27 * padded.shape[3])


def expand_mask(cells, edge):
    planes, rows_y, rows_z = cells.shape
    values = jnp.broadcast_to(
        cells.astype(F32)[:, None, :, None, :, None], (planes, edge, rows_y, edge, rows_z, edge)
    )
    return values.reshape(planes * edge, rows_y * edge, rows_z * edge, 1)


def silu_slope(values):
    logistic = jax.nn.sigmoid(values)
    return logistic * (1.0 + values * (1.0 - logistic))


def near_cells_of(block_mask):
    padded_cells = jnp.pad(block_mask, ((1, 1), (0, 0), (0, 0)))
    return lax.dynamic_slice_in_dim(padded_cells, lax.axis_index("tiles"), 3, 0)


def on_any(features, weight_one, weight_two, cotangent, block_mask):
    depth, width_y, width_z, channels = features.shape
    loss_scale = 1.0 / math.sqrt(lax.axis_size("tiles") * depth * width_y * width_z)
    own_mask = expand_mask(near_cells_of(block_mask), B)[depth : 2 * depth]
    own_flat = own_mask.reshape(-1, 1)

    def cube(field):
        low, high = with_halo(field, "tiles", 1)
        field = jnp.concatenate([low, field, high], axis=0)
        return jnp.pad(field, ((0, 0), (1, 1), (1, 1), (0, 0)))

    def grad_piece(columns_in, rows_in):
        product = lax.dot_general(
            columns_in, rows_in, (((0,), (0,)), ((), ())), preferred_element_type=F32
        )
        return lax.psum_scatter(product * loss_scale, "tiles", scatter_dimension=0, tiled=True)

    full_one = lax.all_gather(weight_one, "tiles", axis=0, tiled=True)
    full_two = lax.all_gather(weight_two, "tiles", axis=0, tiled=True)
    weight_back = jnp.swapaxes(full_two.reshape(27, channels, channels), 1, 2).reshape(
        27 * channels, channels
    )
    inputs = (features * own_mask).astype(BF)
    feature_cols = tap_columns(cube(inputs), False)
    hidden_pre = jnp.dot(feature_cols, full_one, preferred_element_type=F32)
    active = (jax.nn.silu(hidden_pre) * own_flat).astype(BF).reshape(features.shape)
    active_cols = tap_columns(cube(active), False)
    second = jnp.dot(active_cols, full_two, preferred_element_type=F32)
    features_out = (second * own_flat).astype(BF).reshape(features.shape)
    cot = (cotangent * own_mask).astype(BF)
    grad_two = grad_piece(active_cols, cot.reshape(-1, channels))
    upstream = jnp.dot(tap_columns(cube(cot), True), weight_back, preferred_element_type=F32)
    hidden_grad = (upstream * silu_slope(hidden_pre) * own_flat).astype(BF)
    grad_one = grad_piece(feature_cols, hidden_grad)
    return (features_out, grad_one, grad_two)


def chip_at(place):
    return jnp.where(place < 4, 2 * place, 15 - 2 * place)


def place_of(tile):
    chip = tile // 2
    return jnp.where(chip % 2 == 0, chip // 2, 7 - chip // 2)


def shard_rows(tile, core, hop, flip, rows):
    step = jnp.where(core == 0, -hop, hop)
    chip = chip_at((place_of(tile) + step + 8) % 8)
    return pl.multiple_of((2 * chip + (1 - core if flip else core)) * rows, 16)


def store_shifted(out_ref, x0, rows, ny, nz, channels):
    planes = rows.shape[0] // (ny * nz)
    wide = rows.astype(F32)
    z = lax.broadcasted_iota(jnp.int32, wide.shape, 0) % nz
    before = jnp.where(z == 0, 0.0, pltpu.roll(wide, 1, 0)).astype(BF)
    after = jnp.where(z == nz - 1, 0.0, pltpu.roll(wide, wide.shape[0] - 1, 0)).astype(BF)
    for rho, value in enumerate((before, rows.astype(BF), after)):
        out_ref[x0 : x0 + planes, 1 : ny + 1, :, rho * channels : (rho + 1) * channels] = (
            value.reshape(planes, ny, nz, channels)
        )


def clear_edges(out_ref, ny):
    edge = jnp.zeros((out_ref.shape[0], 1) + tuple(out_ref.shape[2:]), BF)
    out_ref[:, 0:1] = edge
    out_ref[:, ny + 1 : ny + 2] = edge


def prep_kernel(cells_ref, low, f_own, c_own, high, sx_ref, sc_ref, int_ref, mask_ref):
    depth, ny, nz, channels = f_own.shape
    area = ny * nz
    tile = lax.axis_index("tiles")
    last = cells_ref.shape[2] - 1
    row = lax.broadcasted_iota(jnp.int32, (area, channels), 0)
    block_y, block_z = row // (B * nz), (row % nz) // B
    m = []
    for i in range(3):
        at = tile + i - 1
        inside = jnp.logical_and(at >= 0, at <= last)
        at = jnp.clip(at, 0, last)
        value = jnp.zeros((area, channels), F32)
        for y in range(ny // B):
            for z in range(nz // B):
                cell = jnp.where(inside, cells_ref[y, z, at], 0).astype(F32)
                here = jnp.logical_and(block_y == y, block_z == z)
                value = jnp.where(here, cell, value)
        value = value.astype(BF)
        mask_ref[i] = value
        m.append(value.reshape(1, area, channels))

    def rows(value, side):
        planes = value.shape[0]
        value = value.reshape(planes, area, channels) * m[side]
        return value.reshape(planes * area, channels)

    clear_edges(sx_ref, ny)
    clear_edges(sc_ref, ny)
    fs = [rows(low[0:2], 0), rows(f_own[...], 1), rows(high[0:2], 2)]
    for x0, value in zip((0, 2, 2 + depth), fs):
        store_shifted(sx_ref, x0, value, ny, nz, channels)
    int_ref[:, 0:area] = fs[0][area:].T
    int_ref[:, area : area + depth * area] = fs[1].T
    int_ref[:, area + depth * area :] = fs[2][:area].T
    for x0, value, side in ((0, low[2:3], 0), (1, c_own[...], 1), (1 + depth, high[2:3], 2)):
        store_shifted(sc_ref, x0, rows(value, side), ny, nz, channels)


PAIRS = (
    (False, ((0, False),)),
    (False, ((0, True),)),
) + tuple(
    (crossed, rows)
    for crossed in (False, True)
    for rows in [((hop, False), (hop, True)) for hop in (1, 2, 3)] + [((4, False),)]
)
SHARDS = (
    PAIRS[:2]
    + ((False, ((1, False),)), (False, ((1, True),)), (True, ((1, False), (1, True))))
    + tuple(
        (crossed, rows)
        for crossed in (False, True)
        for rows in (((2, False),), ((2, True), (3, False)), ((3, True), (4, False)))
    )
)


def fill_weight(kinds, pieces, w_ref):
    tile = lax.axis_index("tiles")
    core = tile % 2
    rows = w_ref.shape[0] // 16
    for piece, (crossed, parts) in zip(pieces, kinds):
        holder = 1 - core if crossed else core
        for part, (hop, flip) in enumerate(parts):
            start = shard_rows(tile, holder, hop, flip, rows)
            w_ref[pl.ds(start, rows)] = piece[part * rows : (part + 1) * rows]


def split_shards(g_ref, keep_ref, send_ref):
    tile = lax.axis_index("tiles")
    core = tile % 2
    rows = g_ref.shape[0] // 16
    for out_ref, holder in ((send_ref, 1 - core), (keep_ref, core)):
        at = 0
        for hop in (4, 3, 2, 1, 0):
            for flip in (False,) if hop in (0, 4) else (False, True):
                start = shard_rows(tile, holder, -hop, flip, rows)
                out_ref[at : at + rows] = g_ref[pl.ds(start, rows)]
                at += rows


def window(ref, x, y, planes, ny, lo=0, hi=None):
    value = ref[x : x + planes, y : y + ny, :, lo:hi]
    return value.reshape(-1, value.shape[-1])


def conv(s_ref, w_ref, x0, planes, ny, channels):
    acc = None
    for p in range(3):
        for q in range(3):
            t = 9 * p + 3 * q
            part = jnp.dot(
                window(s_ref, x0 + p, q, planes, ny),
                w_ref[t * channels : (t + 3) * channels],
                preferred_element_type=F32,
            )
            acc = part if acc is None else acc + part
    return acc


def store_taps(g_ref, p, q, part, channels):
    for rho in range(3):
        t = 9 * p + 3 * q + 2 - rho
        g_ref[t * channels : (t + 1) * channels] = part[:, rho * channels : (rho + 1) * channels]


def masked(value, mask_ref, side):
    area, channels = mask_ref.shape[1:]
    own = mask_ref[side].reshape(1, area, channels).astype(F32)
    return (value.reshape(-1, area, channels) * own).reshape(-1, channels)


def first_kernel(sx_ref, mask_ref, *rest):
    n = len(PAIRS)
    pieces, (pre_ref, act_ref, act_t_ref, w_ref) = rest[:n], rest[n:]
    area, channels = mask_ref.shape[1:]
    ny = sx_ref.shape[1] - 2
    depth = pre_ref.shape[0] // area
    fill_weight(PAIRS, pieces, w_ref)
    pre = conv(sx_ref, w_ref, 1, depth, ny, channels)
    pre_ref[...] = pre
    act = masked(pre * jax.nn.sigmoid(pre), mask_ref, 1).astype(BF)
    act_ref[...] = act
    act_t_ref[...] = act.T


def grad_two_kernel(sc_ref, act_t_ref, keep_ref, send_ref, g_ref):
    depth, ny, nz, channels = sc_ref.shape
    depth, ny, channels = depth - 2, ny - 2, channels // 3
    for p in range(3):
        for q in range(3):
            part = jnp.dot(
                act_t_ref[...],
                window(sc_ref, 2 - p, 2 - q, depth, ny),
                preferred_element_type=F32,
            )
            store_taps(g_ref, p, q, part.astype(BF), channels)
    split_shards(g_ref, keep_ref, send_ref)


def back_kernel(sc_ref, pre_ref, mask_ref, *rest):
    n = len(SHARDS)
    pieces, (sd_ref, w_ref) = rest[:n], rest[n:]
    area, channels = mask_ref.shape[1:]
    ny, nz = sc_ref.shape[1] - 2, sc_ref.shape[2]
    depth = pre_ref.shape[0] // area
    fill_weight(SHARDS, pieces, w_ref)
    acc = None
    for p in range(3):
        for q in range(3):
            for r in range(3):
                t = 9 * p + 3 * q + r
                lo = (2 - r) * channels
                part = lax.dot_general(
                    window(sc_ref, 2 - p, 2 - q, depth, ny, lo, lo + channels),
                    w_ref[t * channels : (t + 1) * channels],
                    (((1,), (1,)), ((), ())),
                    preferred_element_type=F32,
                )
                acc = part if acc is None else acc + part
    delta = masked(acc * silu_slope(pre_ref[...]), mask_ref, 1).astype(BF)
    clear_edges(sd_ref, ny)
    store_shifted(sd_ref, 0, delta, ny, nz, channels)


def grad_one_kernel(sd_ref, int_ref, keep_ref, send_ref, g_ref):
    depth, ny, nz, channels = sd_ref.shape
    ny, area, channels = ny - 2, (ny - 2) * nz, channels // 3
    for q in range(3):
        right = window(sd_ref, 0, 2 - q, depth, ny)
        for p in range(3):
            part = jnp.dot(
                int_ref[:, p * area : (p + depth) * area], right, preferred_element_type=F32
            )
            store_taps(g_ref, p, q, part.astype(BF), channels)
    split_shards(g_ref, keep_ref, send_ref)


def third_kernel(sx_ref, act_ref, mask_ref, *rest):
    n = len(PAIRS)
    pieces, (out_ref, w_ref, v_ref, sa_ref) = rest[:-4], rest[-4:]
    area, channels = mask_ref.shape[1:]
    ny, nz = sx_ref.shape[1] - 2, sx_ref.shape[2]
    depth = act_ref.shape[0] // area
    fill_weight(PAIRS, pieces[:n], w_ref)
    fill_weight(SHARDS, pieces[n:], v_ref)
    clear_edges(sa_ref, ny)
    store_shifted(sa_ref, 1, act_ref[...], ny, nz, channels)
    for x0, side in ((0, 0), (1 + depth, 2)):
        pre = conv(sx_ref, w_ref, x0, 1, ny, channels)
        act = masked(pre * jax.nn.sigmoid(pre), mask_ref, side).astype(BF)
        store_shifted(sa_ref, x0, act, ny, nz, channels)
    second = conv(sa_ref, v_ref, 0, depth, ny, channels)
    out_ref[...] = masked(second, mask_ref, 1).astype(BF).reshape(out_ref.shape)


def on_ring(features, weight_one, weight_two, cotangent, block_mask):
    depth, ny, nz, channels = features.shape
    area = ny * nz
    rows = weight_one.shape[0]
    chips = len(RING)
    tiles = 2 * chips
    loss_scale = 1.0 / math.sqrt(tiles * depth * area)
    shape = jax.ShapeDtypeStruct
    scratch = pltpu.VMEM
    shards = (shape((chips * rows, channels), BF),) * 2
    weights = scratch((27 * channels, channels), BF)
    flops = 2 * depth * area * 27 * channels * channels

    def permute(pairs):
        return functools.partial(lax.ppermute, axis_name="tiles", perm=pairs)

    def along_ring(core_from, core_to):
        return permute(
            [(2 * RING[i] + core_from, 2 * RING[(i + 1) % chips] + core_to) for i in range(chips)]
            + [
                (2 * RING[i] + 1 - core_from, 2 * RING[i - 1] + 1 - core_to)
                for i in range(chips)
            ]
        )

    onward, gather_across, scatter_across = along_ring(0, 0), along_ring(1, 0), along_ring(0, 1)
    sibling = permute([(i, i ^ 1) for i in range(tiles)])
    up = permute([(i, (i + 1) % tiles) for i in range(tiles)])
    down = permute([(i, (i - 1) % tiles) for i in range(tiles)])

    def after(value, *others):
        return lax.optimization_barrier((value,) + others)[0]

    def kernel(body, name, mib, convs, outs, scratches, *operands, smem=0):
        return pl.pallas_call(
            body,
            name=name,
            out_shape=outs,
            in_specs=[pl.BlockSpec(memory_space=pltpu.SMEM)] * smem
            + [pl.BlockSpec(memory_space=pltpu.VMEM)] * (len(operands) - smem),
            out_specs=jax.tree.map(lambda _: pl.BlockSpec(memory_space=pltpu.VMEM), outs),
            scratch_shapes=scratches,
            compiler_params=pltpu.CompilerParams(vmem_limit_bytes=mib << 20),
            cost_estimate=pl.CostEstimate(
                flops=convs * flops, transcendentals=0, bytes_accessed=4 << 20
            ),
        )(*operands)

    a1 = [onward(weight_one), gather_across(weight_one)]
    x1 = onward(after(weight_two, a1[0]))
    low = up(jnp.concatenate([features[-2:], cotangent[-1:]]))
    high = down(jnp.concatenate([features[:2], cotangent[:1]]))
    a1 = jnp.concatenate(a1)
    a2 = onward(a1)
    qa1 = sibling(a1)
    y1 = gather_across(after(weight_two, a1))
    a3 = onward(after(a2, x1))
    qa2 = sibling(a2)
    other_one = sibling(weight_one)
    x2 = onward(after(x1, y1))
    sx, sc, in_t, near = kernel(
        prep_kernel,
        "prep",
        8,
        0,
        (
            shape((depth + 4, ny + 2, nz, 3 * channels), BF),
            shape((depth + 2, ny + 2, nz, 3 * channels), BF),
            shape((channels, (depth + 2) * area), BF),
            shape((3, area, channels), BF),
        ),
        [],
        jnp.transpose(block_mask, (1, 2, 0)),
        low,
        features,
        cotangent,
        high,
        smem=1,
    )
    a4 = onward(after(a3[:rows], y1, qa1, qa2, other_one))
    qa3, qa4 = sibling(a3), sibling(after(a4, low, high))
    ones = [weight_one, other_one, a1, a2, a3, a4, qa1, qa2, qa3, qa4]

    m4 = onward(jnp.concatenate([y1, x2]))
    qb1 = sibling(jnp.concatenate([x1, y1]))
    other_two = sibling(weight_two)
    pre, act, act_t = kernel(
        first_kernel,
        "first",
        8,
        1,
        (
            shape((depth * area, channels), F32),
            shape((depth * area, channels), BF),
            shape((channels, depth * area), BF),
        ),
        [weights],
        after(sx, x2, qb1, other_two),
        near,
        *ones,
    )
    qx2 = sibling(x2)
    keep_two, send_two = kernel(
        grad_two_kernel, "grad_two", 8, 1, shards, [weights], sc, act_t
    )
    got_two = sibling(after(send_two, m4, qx2))
    m5 = onward(m4)
    qm4 = sibling(m4)

    def both(keep, got, lo, hi):
        return keep[lo * rows : hi * rows].astype(F32) + got[lo * rows : hi * rows].astype(F32)

    def step(keep, got, moving, k):
        if k == 0:
            return both(keep, got, 0, 1).astype(BF)
        if k == 1:
            moving = jnp.concatenate([moving, jnp.zeros_like(moving)])
        return (both(keep, got, 2 * k - 1, 2 * k + 1) + moving.astype(F32)).astype(BF)

    def finish(keep, got, message):
        total = both(keep, got, 7, 8) + onward(message[:rows]).astype(F32)
        return (total + scatter_across(message[rows:]).astype(F32)) * loss_scale

    message = step(keep_two, got_two, None, 0)
    two = onward(message)
    qm5 = sibling(after(m5, message))
    twos = [weight_two, other_two, x1, y1, qb1, x2, m4, m5, qx2, qm4, qm5]
    delta = kernel(
        back_kernel,
        "back",
        8,
        1,
        shape((depth, ny + 2, nz, 3 * channels), BF),
        [weights],
        sc,
        pre,
        near,
        *twos,
    )
    keep_one, send_one = kernel(
        grad_one_kernel, "grad_one", 8, 1, shards, [weights], delta, in_t
    )
    got_one = sibling(after(send_one, two))
    act_late = after(act, two)
    two = onward(step(keep_two, got_two, two, 1))
    one = onward(step(keep_one, got_one, None, 0))
    features_out = kernel(
        third_kernel,
        "third",
        14,
        4,
        shape(features.shape, BF),
        [weights, weights, scratch((depth + 2, ny + 2, nz, 3 * channels), BF)],
        sx,
        act_late,
        near,
        *ones,
        *twos,
    )
    one = onward(after(step(keep_one, got_one, one, 1), features_out, two))
    two = onward(step(keep_two, got_two, two, 2))
    grad_two = finish(keep_two, got_two, step(keep_two, got_two, two, 3))
    one = onward(step(keep_one, got_one, one, 2))
    return (features_out, finish(keep_one, got_one, step(keep_one, got_one, one, 3)), grad_two)


def solution(mesh):
    placed = (
        P(("groups", "tiles"), None, None, None),
        P("tiles", None),
        P("tiles", None),
        P(("groups", "tiles"), None, None, None),
        P("groups", None, None),
    )
    on_device = on_ring if mesh.shape["tiles"] == 2 * len(RING) else on_any
    return jax.shard_map(
        on_device,
        mesh=mesh,
        in_specs=placed,
        out_specs=(
            P(("groups", "tiles"), None, None, None),
            P(("groups", "tiles"), None),
            P(("groups", "tiles"), None),
        ),
        check_vma=False,
    )
```

```python
import functools
import math

import jax
import jax.numpy as jnp
from jax import lax
from jax.experimental import pallas as pl
from jax.experimental.pallas import tpu as pltpu
from jax.sharding import PartitionSpec as P

B = 4
RING = (0, 2, 4, 6, 7, 5, 3, 1)
BF = jnp.bfloat16
F32 = jnp.float32


def with_halo(block, axis, width):
    count = lax.axis_size(axis)
    forward = [(i, i + 1) for i in range(count - 1)]
    backward = [(target, source) for source, target in forward]
    low = lax.ppermute(block[-width:], axis, forward)
    high = lax.ppermute(block[:width], axis, backward)
    return low, high


def tap_columns(padded, flipped):
    extent = [padded.shape[d] - 2 for d in range(3)]
    taps = []
    for a in range(3):
        for b in range(3):
            for c in range(3):
                x, y, z = (2 - a, 2 - b, 2 - c) if flipped else (a, b, c)
                taps.append(padded[x : x + extent[0], y : y + extent[1], z : z + extent[2]])
    stacked = jnp.stack(taps, axis=3)
    return stacked.reshape(extent[0] * extent[1] * extent[2], 27 * padded.shape[3])


def expand_mask(cells, edge):
    planes, rows_y, rows_z = cells.shape
    values = jnp.broadcast_to(
        cells.astype(F32)[:, None, :, None, :, None], (planes, edge, rows_y, edge, rows_z, edge)
    )
    return values.reshape(planes * edge, rows_y * edge, rows_z * edge, 1)


def silu_slope(values):
    logistic = jax.nn.sigmoid(values)
    return logistic * (1.0 + values * (1.0 - logistic))


def near_cells_of(block_mask):
    padded_cells = jnp.pad(block_mask, ((1, 1), (0, 0), (0, 0)))
    return lax.dynamic_slice_in_dim(padded_cells, lax.axis_index("tiles"), 3, 0)


def on_any(features, weight_one, weight_two, cotangent, block_mask):
    depth, width_y, width_z, channels = features.shape
    loss_scale = 1.0 / math.sqrt(lax.axis_size("tiles") * depth * width_y * width_z)
    own_mask = expand_mask(near_cells_of(block_mask), B)[depth : 2 * depth]
    own_flat = own_mask.reshape(-1, 1)

    def cube(field):
        low, high = with_halo(field, "tiles", 1)
        field = jnp.concatenate([low, field, high], axis=0)
        return jnp.pad(field, ((0, 0), (1, 1), (1, 1), (0, 0)))

    def grad_piece(columns_in, rows_in):
        product = lax.dot_general(
            columns_in, rows_in, (((0,), (0,)), ((), ())), preferred_element_type=F32
        )
        return lax.psum_scatter(product * loss_scale, "tiles", scatter_dimension=0, tiled=True)

    full_one = lax.all_gather(weight_one, "tiles", axis=0, tiled=True)
    full_two = lax.all_gather(weight_two, "tiles", axis=0, tiled=True)
    weight_back = jnp.swapaxes(full_two.reshape(27, channels, channels), 1, 2).reshape(
        27 * channels, channels
    )
    inputs = (features * own_mask).astype(BF)
    feature_cols = tap_columns(cube(inputs), False)
    hidden_pre = jnp.dot(feature_cols, full_one, preferred_element_type=F32)
    active = (jax.nn.silu(hidden_pre) * own_flat).astype(BF).reshape(features.shape)
    active_cols = tap_columns(cube(active), False)
    second = jnp.dot(active_cols, full_two, preferred_element_type=F32)
    features_out = (second * own_flat).astype(BF).reshape(features.shape)
    cot = (cotangent * own_mask).astype(BF)
    grad_two = grad_piece(active_cols, cot.reshape(-1, channels))
    upstream = jnp.dot(tap_columns(cube(cot), True), weight_back, preferred_element_type=F32)
    hidden_grad = (upstream * silu_slope(hidden_pre) * own_flat).astype(BF)
    grad_one = grad_piece(feature_cols, hidden_grad)
    return (features_out, grad_one, grad_two)


def chip_at(place):
    return jnp.where(place < 4, 2 * place, 15 - 2 * place)


def place_of(tile):
    chip = tile // 2
    return jnp.where(chip % 2 == 0, chip // 2, 7 - chip // 2)


def shard_rows(tile, core, hop, flip, rows):
    step = jnp.where(core == 0, -hop, hop)
    chip = chip_at((place_of(tile) + step + 8) % 8)
    return pl.multiple_of((2 * chip + (1 - core if flip else core)) * rows, 16)


def store_shifted(out_ref, x0, rows, ny, nz, channels):
    planes = rows.shape[0] // (ny * nz)
    wide = rows.astype(F32)
    z = lax.broadcasted_iota(jnp.int32, wide.shape, 0) % nz
    before = jnp.where(z == 0, 0.0, pltpu.roll(wide, 1, 0)).astype(BF)
    after = jnp.where(z == nz - 1, 0.0, pltpu.roll(wide, wide.shape[0] - 1, 0)).astype(BF)
    for rho, value in enumerate((before, rows.astype(BF), after)):
        out_ref[x0 : x0 + planes, 1 : ny + 1, :, rho * channels : (rho + 1) * channels] = (
            value.reshape(planes, ny, nz, channels)
        )


def clear_edges(out_ref, ny):
    edge = jnp.zeros((out_ref.shape[0], 1) + tuple(out_ref.shape[2:]), BF)
    out_ref[:, 0:1] = edge
    out_ref[:, ny + 1 : ny + 2] = edge


def prep_kernel(cells_ref, low, f_own, c_own, high, sx_ref, sc_ref, int_ref, mask_ref):
    depth, ny, nz, channels = f_own.shape
    area = ny * nz
    tile = lax.axis_index("tiles")
    last = cells_ref.shape[2] - 1
    row = lax.broadcasted_iota(jnp.int32, (area, channels), 0)
    block_y, block_z = row // (B * nz), (row % nz) // B
    m = []
    for i in range(3):
        at = tile + i - 1
        inside = jnp.logical_and(at >= 0, at <= last)
        at = jnp.clip(at, 0, last)
        value = jnp.zeros((area, channels), F32)
        for y in range(ny // B):
            for z in range(nz // B):
                cell = jnp.where(inside, cells_ref[y, z, at], 0).astype(F32)
                here = jnp.logical_and(block_y == y, block_z == z)
                value = jnp.where(here, cell, value)
        value = value.astype(BF)
        mask_ref[i] = value
        m.append(value.reshape(1, area, channels))

    def rows(value, side):
        planes = value.shape[0]
        value = value.reshape(planes, area, channels) * m[side]
        return value.reshape(planes * area, channels)

    clear_edges(sx_ref, ny)
    clear_edges(sc_ref, ny)
    fs = [rows(low[0:2], 0), rows(f_own[...], 1), rows(high[0:2], 2)]
    for x0, value in zip((0, 2, 2 + depth), fs):
        store_shifted(sx_ref, x0, value, ny, nz, channels)
    int_ref[:, 0:area] = fs[0][area:].T
    int_ref[:, area : area + depth * area] = fs[1].T
    int_ref[:, area + depth * area :] = fs[2][:area].T
    for x0, value, side in ((0, low[2:3], 0), (1, c_own[...], 1), (1 + depth, high[2:3], 2)):
        store_shifted(sc_ref, x0, rows(value, side), ny, nz, channels)


PIECES = tuple((hop, False) for hop in range(5)) + tuple((hop, True) for hop in range(1, 5))


def fill_weight(pieces, w_ref):
    tile = lax.axis_index("tiles")
    core = tile % 2
    rows = w_ref.shape[0] // 16
    for piece, (hop, crossed) in zip(pieces, PIECES):
        holder = 1 - core if crossed else core
        for half in range(piece.shape[0] // rows):
            start = shard_rows(tile, holder, hop, half == 1, rows)
            w_ref[pl.ds(start, rows)] = piece[half * rows : (half + 1) * rows]


def split_shards(g_ref, keep_ref, send_ref):
    tile = lax.axis_index("tiles")
    core = tile % 2
    rows = g_ref.shape[0] // 16
    for out_ref, holder in ((send_ref, 1 - core), (keep_ref, core)):
        at = 0
        for hop in (4, 3, 2, 1, 0):
            for flip in (False,) if hop in (0, 4) else (False, True):
                start = shard_rows(tile, holder, -hop, flip, rows)
                out_ref[at : at + rows] = g_ref[pl.ds(start, rows)]
                at += rows


def window(ref, x, y, planes, ny, lo=0, hi=None):
    value = ref[x : x + planes, y : y + ny, :, lo:hi]
    return value.reshape(-1, value.shape[-1])


def conv(s_ref, w_ref, x0, planes, ny, channels):
    acc = None
    for p in range(3):
        for q in range(3):
            t = 9 * p + 3 * q
            part = jnp.dot(
                window(s_ref, x0 + p, q, planes, ny),
                w_ref[t * channels : (t + 3) * channels],
                preferred_element_type=F32,
            )
            acc = part if acc is None else acc + part
    return acc


def store_taps(g_ref, p, q, part, channels):
    for rho in range(3):
        t = 9 * p + 3 * q + 2 - rho
        g_ref[t * channels : (t + 1) * channels] = part[:, rho * channels : (rho + 1) * channels]


def masked(value, mask_ref, side):
    area, channels = mask_ref.shape[1:]
    own = mask_ref[side].reshape(1, area, channels).astype(F32)
    return (value.reshape(-1, area, channels) * own).reshape(-1, channels)


def first_kernel(n, sx_ref, mask_ref, *rest):
    pieces, (pre_ref, act_ref, act_t_ref, w_ref) = rest[:n], rest[n:]
    area, channels = mask_ref.shape[1:]
    ny = sx_ref.shape[1] - 2
    depth = pre_ref.shape[0] // area
    fill_weight(pieces, w_ref)
    pre = conv(sx_ref, w_ref, 1, depth, ny, channels)
    pre_ref[...] = pre
    act = masked(pre * jax.nn.sigmoid(pre), mask_ref, 1).astype(BF)
    act_ref[...] = act
    act_t_ref[...] = act.T


def grad_two_kernel(sc_ref, act_t_ref, keep_ref, send_ref, g_ref):
    depth, ny, nz, channels = sc_ref.shape
    depth, ny, channels = depth - 2, ny - 2, channels // 3
    for p in range(3):
        for q in range(3):
            part = jnp.dot(
                act_t_ref[...],
                window(sc_ref, 2 - p, 2 - q, depth, ny),
                preferred_element_type=F32,
            )
            store_taps(g_ref, p, q, part.astype(BF), channels)
    split_shards(g_ref, keep_ref, send_ref)


def back_kernel(n, sc_ref, pre_ref, mask_ref, *rest):
    pieces, (sd_ref, w_ref) = rest[:n], rest[n:]
    area, channels = mask_ref.shape[1:]
    ny, nz = sc_ref.shape[1] - 2, sc_ref.shape[2]
    depth = pre_ref.shape[0] // area
    fill_weight(pieces, w_ref)
    acc = None
    for p in range(3):
        for q in range(3):
            for r in range(3):
                t = 9 * p + 3 * q + r
                lo = (2 - r) * channels
                part = lax.dot_general(
                    window(sc_ref, 2 - p, 2 - q, depth, ny, lo, lo + channels),
                    w_ref[t * channels : (t + 1) * channels],
                    (((1,), (1,)), ((), ())),
                    preferred_element_type=F32,
                )
                acc = part if acc is None else acc + part
    delta = masked(acc * silu_slope(pre_ref[...]), mask_ref, 1).astype(BF)
    clear_edges(sd_ref, ny)
    store_shifted(sd_ref, 0, delta, ny, nz, channels)


def grad_one_kernel(sd_ref, int_ref, keep_ref, send_ref, g_ref):
    depth, ny, nz, channels = sd_ref.shape
    ny, area, channels = ny - 2, (ny - 2) * nz, channels // 3
    for q in range(3):
        right = window(sd_ref, 0, 2 - q, depth, ny)
        for p in range(3):
            part = jnp.dot(
                int_ref[:, p * area : (p + depth) * area], right, preferred_element_type=F32
            )
            store_taps(g_ref, p, q, part.astype(BF), channels)
    split_shards(g_ref, keep_ref, send_ref)


def third_kernel(n, sx_ref, act_ref, mask_ref, *rest):
    out_ref, w_ref, v_ref, sa_ref = rest[2 * n :]
    area, channels = mask_ref.shape[1:]
    ny, nz = sx_ref.shape[1] - 2, sx_ref.shape[2]
    depth = act_ref.shape[0] // area
    fill_weight(rest[:n], w_ref)
    fill_weight(rest[n : 2 * n], v_ref)
    clear_edges(sa_ref, ny)
    store_shifted(sa_ref, 1, act_ref[...], ny, nz, channels)
    for x0, side in ((0, 0), (1 + depth, 2)):
        pre = conv(sx_ref, w_ref, x0, 1, ny, channels)
        act = masked(pre * jax.nn.sigmoid(pre), mask_ref, side).astype(BF)
        store_shifted(sa_ref, x0, act, ny, nz, channels)
    second = conv(sa_ref, v_ref, 0, depth, ny, channels)
    out_ref[...] = masked(second, mask_ref, 1).astype(BF).reshape(out_ref.shape)


def on_ring(features, weight_one, weight_two, cotangent, block_mask):
    depth, ny, nz, channels = features.shape
    area = ny * nz
    rows = weight_one.shape[0]
    chips = len(RING)
    tiles = 2 * chips
    loss_scale = 1.0 / math.sqrt(tiles * depth * area)
    shape = jax.ShapeDtypeStruct
    scratch = pltpu.VMEM
    shards = (shape((chips * rows, channels), BF),) * 2
    weights = scratch((27 * channels, channels), BF)
    flops = 2 * depth * area * 27 * channels * channels

    def permute(pairs):
        return functools.partial(lax.ppermute, axis_name="tiles", perm=pairs)

    def along_ring(core_from, core_to):
        return permute(
            [(2 * RING[i] + core_from, 2 * RING[(i + 1) % chips] + core_to) for i in range(chips)]
            + [
                (2 * RING[i] + 1 - core_from, 2 * RING[i - 1] + 1 - core_to)
                for i in range(chips)
            ]
        )

    onward, scatter_across = along_ring(0, 0), along_ring(0, 1)
    sibling = permute([(i, i ^ 1) for i in range(tiles)])
    up = permute([(i, (i + 1) % tiles) for i in range(tiles)])
    down = permute([(i, (i - 1) % tiles) for i in range(tiles)])

    def after(value, *others):
        return lax.optimization_barrier((value,) + others)[0]

    def kernel(body, name, mib, convs, outs, scratches, *operands, smem=0):
        return pl.pallas_call(
            body,
            name=name,
            out_shape=outs,
            in_specs=[pl.BlockSpec(memory_space=pltpu.SMEM)] * smem
            + [pl.BlockSpec(memory_space=pltpu.VMEM)] * (len(operands) - smem),
            out_specs=jax.tree.map(lambda _: pl.BlockSpec(memory_space=pltpu.VMEM), outs),
            scratch_shapes=scratches,
            compiler_params=pltpu.CompilerParams(vmem_limit_bytes=mib << 20),
            cost_estimate=pl.CostEstimate(
                flops=convs * flops, transcendentals=0, bytes_accessed=4 << 20
            ),
        )(*operands)

    a0 = jnp.concatenate([weight_one, sibling(weight_one)])
    b0 = jnp.concatenate([after(weight_two, a0), sibling(weight_two)])
    features_late, cot_late, _ = lax.optimization_barrier((features, cotangent, b0))
    low = up(jnp.concatenate([features_late[-2:], cot_late[-1:]]))
    high = down(jnp.concatenate([features_late[:2], cot_late[:1]]))

    a1, b1 = onward(a0), onward(b0)
    a2, qa1 = onward(a1), sibling(a1)
    b2, qb1 = onward(b1), sibling(b1)
    a3, qa2 = onward(after(a2, b1, low, high, qa1)), sibling(a2)
    sx, sc, in_t, near = kernel(
        prep_kernel,
        "prep",
        8,
        0,
        (
            shape((depth + 4, ny + 2, nz, 3 * channels), BF),
            shape((depth + 2, ny + 2, nz, 3 * channels), BF),
            shape((channels, (depth + 2) * area), BF),
            shape((3, area, channels), BF),
        ),
        [],
        jnp.transpose(block_mask, (1, 2, 0)),
        low,
        features,
        cotangent,
        high,
        smem=1,
    )
    b3, qb2 = onward(after(b2, qb1)), sibling(b2)
    a4, qa3 = onward(after(a3[:rows], b2, sx, qa2)), sibling(a3)
    b4, qb3 = onward(after(b3[:rows], qb2)), sibling(b3)
    qa4, qb4 = sibling(a4), sibling(b4)
    ones = [a0, a1, a2, a3, a4, qa1, qa2, qa3, qa4]
    twos = [b0, b1, b2, b3, b4, qb1, qb2, qb3, qb4]
    n = len(ones)

    pre, act, act_t = kernel(
        functools.partial(first_kernel, n),
        "first",
        8,
        1,
        (
            shape((depth * area, channels), F32),
            shape((depth * area, channels), BF),
            shape((channels, depth * area), BF),
        ),
        [weights],
        after(sx, b4),
        near,
        *ones,
    )
    keep_two, send_two = kernel(
        grad_two_kernel, "grad_two", 8, 1, shards, [weights], sc, act_t
    )
    got_two = sibling(send_two)

    def both(keep, got, lo, hi):
        return keep[lo * rows : hi * rows].astype(F32) + got[lo * rows : hi * rows].astype(F32)

    def step(keep, got, moving, k):
        if k == 0:
            return both(keep, got, 0, 1).astype(BF)
        if k == 1:
            moving = jnp.concatenate([moving, jnp.zeros_like(moving)])
        return (both(keep, got, 2 * k - 1, 2 * k + 1) + moving.astype(F32)).astype(BF)

    def finish(keep, got, message):
        total = both(keep, got, 7, 8) + onward(message[:rows]).astype(F32)
        return (total + scatter_across(message[rows:]).astype(F32)) * loss_scale

    delta = kernel(
        functools.partial(back_kernel, n),
        "back",
        8,
        1,
        shape((depth, ny + 2, nz, 3 * channels), BF),
        [weights],
        sc,
        pre,
        near,
        *twos,
    )
    keep_one, send_one = kernel(
        grad_one_kernel, "grad_one", 8, 1, shards, [weights], delta, in_t
    )
    two = onward(step(keep_two, after(got_two, keep_one), None, 0))
    got_one = sibling(send_one)
    one = onward(step(keep_one, got_one, None, 0))
    features_out = kernel(
        functools.partial(third_kernel, n),
        "third",
        14,
        1,
        shape(features.shape, BF),
        [weights, weights, scratch((depth + 2, ny + 2, nz, 3 * channels), BF)],
        sx,
        after(act, two),
        near,
        *ones,
        *twos,
    )
    two = onward(step(keep_two, got_two, two, 1))
    one = onward(step(keep_one, got_one, one, 1))
    two = onward(step(keep_two, got_two, after(two, features_out), 2))
    one = onward(step(keep_one, got_one, one, 2))
    grad_two = finish(keep_two, got_two, step(keep_two, got_two, two, 3))
    return (features_out, finish(keep_one, got_one, step(keep_one, got_one, one, 3)), grad_two)


def solution(mesh):
    placed = (
        P(("groups", "tiles"), None, None, None),
        P("tiles", None),
        P("tiles", None),
        P(("groups", "tiles"), None, None, None),
        P("groups", None, None),
    )
    on_device = on_ring if mesh.shape["tiles"] == 2 * len(RING) else on_any
    return jax.shard_map(
        on_device,
        mesh=mesh,
        in_specs=placed,
        out_specs=(
            P(("groups", "tiles"), None, None, None),
            P(("groups", "tiles"), None),
            P(("groups", "tiles"), None),
        ),
        check_vma=False,
    )
```

```python
import functools
import math

import jax
import jax.numpy as jnp
from jax import lax
from jax.experimental import pallas as pl
from jax.experimental.pallas import tpu as pltpu
from jax.sharding import PartitionSpec as P

B = 4
RING = (0, 2, 4, 6, 7, 5, 3, 1)
BF = jnp.bfloat16
F32 = jnp.float32


def with_halo(block, axis, width):
    count = lax.axis_size(axis)
    forward = [(i, i + 1) for i in range(count - 1)]
    backward = [(target, source) for source, target in forward]
    low = lax.ppermute(block[-width:], axis, forward)
    high = lax.ppermute(block[:width], axis, backward)
    return low, high


def tap_columns(padded, flipped):
    extent = [padded.shape[d] - 2 for d in range(3)]
    taps = []
    for a in range(3):
        for b in range(3):
            for c in range(3):
                x, y, z = (2 - a, 2 - b, 2 - c) if flipped else (a, b, c)
                taps.append(padded[x : x + extent[0], y : y + extent[1], z : z + extent[2]])
    stacked = jnp.stack(taps, axis=3)
    return stacked.reshape(extent[0] * extent[1] * extent[2], 27 * padded.shape[3])


def expand_mask(cells, edge):
    planes, rows_y, rows_z = cells.shape
    values = jnp.broadcast_to(
        cells.astype(F32)[:, None, :, None, :, None], (planes, edge, rows_y, edge, rows_z, edge)
    )
    return values.reshape(planes * edge, rows_y * edge, rows_z * edge, 1)


def silu_slope(values):
    logistic = jax.nn.sigmoid(values)
    return logistic * (1.0 + values * (1.0 - logistic))


def near_cells_of(block_mask):
    padded_cells = jnp.pad(block_mask, ((1, 1), (0, 0), (0, 0)))
    return lax.dynamic_slice_in_dim(padded_cells, lax.axis_index("tiles"), 3, 0)


def on_any(features, weight_one, weight_two, cotangent, block_mask):
    depth, width_y, width_z, channels = features.shape
    loss_scale = 1.0 / math.sqrt(lax.axis_size("tiles") * depth * width_y * width_z)
    own_mask = expand_mask(near_cells_of(block_mask), B)[depth : 2 * depth]
    own_flat = own_mask.reshape(-1, 1)

    def cube(field):
        low, high = with_halo(field, "tiles", 1)
        field = jnp.concatenate([low, field, high], axis=0)
        return jnp.pad(field, ((0, 0), (1, 1), (1, 1), (0, 0)))

    def grad_piece(columns_in, rows_in):
        product = lax.dot_general(
            columns_in, rows_in, (((0,), (0,)), ((), ())), preferred_element_type=F32
        )
        return lax.psum_scatter(product * loss_scale, "tiles", scatter_dimension=0, tiled=True)

    full_one = lax.all_gather(weight_one, "tiles", axis=0, tiled=True)
    full_two = lax.all_gather(weight_two, "tiles", axis=0, tiled=True)
    weight_back = jnp.swapaxes(full_two.reshape(27, channels, channels), 1, 2).reshape(
        27 * channels, channels
    )
    inputs = (features * own_mask).astype(BF)
    feature_cols = tap_columns(cube(inputs), False)
    hidden_pre = jnp.dot(feature_cols, full_one, preferred_element_type=F32)
    active = (jax.nn.silu(hidden_pre) * own_flat).astype(BF).reshape(features.shape)
    active_cols = tap_columns(cube(active), False)
    second = jnp.dot(active_cols, full_two, preferred_element_type=F32)
    features_out = (second * own_flat).astype(BF).reshape(features.shape)
    cot = (cotangent * own_mask).astype(BF)
    grad_two = grad_piece(active_cols, cot.reshape(-1, channels))
    upstream = jnp.dot(tap_columns(cube(cot), True), weight_back, preferred_element_type=F32)
    hidden_grad = (upstream * silu_slope(hidden_pre) * own_flat).astype(BF)
    grad_one = grad_piece(feature_cols, hidden_grad)
    return (features_out, grad_one, grad_two)


def chip_at(place):
    return jnp.where(place < 4, 2 * place, 15 - 2 * place)


def place_of(tile):
    chip = tile // 2
    return jnp.where(chip % 2 == 0, chip // 2, 7 - chip // 2)


def shard_rows(tile, core, hop, flip, rows):
    step = jnp.where(core == 0, -hop, hop)
    chip = chip_at((place_of(tile) + step + 8) % 8)
    return pl.multiple_of((2 * chip + (1 - core if flip else core)) * rows, 16)


def store_shifted(out_ref, x0, rows, ny, nz, channels):
    planes = rows.shape[0] // (ny * nz)
    wide = rows.astype(F32)
    z = lax.broadcasted_iota(jnp.int32, wide.shape, 0) % nz
    before = jnp.where(z == 0, 0.0, pltpu.roll(wide, 1, 0)).astype(BF)
    after = jnp.where(z == nz - 1, 0.0, pltpu.roll(wide, wide.shape[0] - 1, 0)).astype(BF)
    for rho, value in enumerate((before, rows.astype(BF), after)):
        out_ref[x0 : x0 + planes, 1 : ny + 1, :, rho * channels : (rho + 1) * channels] = (
            value.reshape(planes, ny, nz, channels)
        )


def clear_edges(out_ref, ny):
    edge = jnp.zeros((out_ref.shape[0], 1) + tuple(out_ref.shape[2:]), BF)
    out_ref[:, 0:1] = edge
    out_ref[:, ny + 1 : ny + 2] = edge


def prep_kernel(cells_ref, low, f_own, c_own, high, sx_ref, sc_ref, int_ref, mask_ref):
    depth, ny, nz, channels = f_own.shape
    area = ny * nz
    tile = lax.axis_index("tiles")
    last = cells_ref.shape[2] - 1
    row = lax.broadcasted_iota(jnp.int32, (area, channels), 0)
    block_y, block_z = row // (B * nz), (row % nz) // B
    m = []
    for i in range(3):
        at = tile + i - 1
        inside = jnp.logical_and(at >= 0, at <= last)
        at = jnp.clip(at, 0, last)
        value = jnp.zeros((area, channels), F32)
        for y in range(ny // B):
            for z in range(nz // B):
                cell = jnp.where(inside, cells_ref[y, z, at], 0).astype(F32)
                here = jnp.logical_and(block_y == y, block_z == z)
                value = jnp.where(here, cell, value)
        value = value.astype(BF)
        mask_ref[i] = value
        m.append(value.reshape(1, area, channels))

    def rows(value, side):
        planes = value.shape[0]
        value = value.reshape(planes, area, channels) * m[side]
        return value.reshape(planes * area, channels)

    clear_edges(sx_ref, ny)
    clear_edges(sc_ref, ny)
    fs = [rows(low[0:2], 0), rows(f_own[...], 1), rows(high[0:2], 2)]
    for x0, value in zip((0, 2, 2 + depth), fs):
        store_shifted(sx_ref, x0, value, ny, nz, channels)
    int_ref[:, 0:area] = fs[0][area:].T
    int_ref[:, area : area + depth * area] = fs[1].T
    int_ref[:, area + depth * area :] = fs[2][:area].T
    for x0, value, side in ((0, low[2:3], 0), (1, c_own[...], 1), (1 + depth, high[2:3], 2)):
        store_shifted(sc_ref, x0, rows(value, side), ny, nz, channels)


PIECES = tuple((hop, False) for hop in range(5)) + tuple((hop, True) for hop in range(1, 5))


def fill_weight(pieces, w_ref):
    tile = lax.axis_index("tiles")
    core = tile % 2
    rows = w_ref.shape[0] // 16
    for piece, (hop, crossed) in zip(pieces, PIECES):
        holder = 1 - core if crossed else core
        for half in range(piece.shape[0] // rows):
            start = shard_rows(tile, holder, hop, half == 1, rows)
            w_ref[pl.ds(start, rows)] = piece[half * rows : (half + 1) * rows]


def split_shards(g_ref, keep_ref, send_ref):
    tile = lax.axis_index("tiles")
    core = tile % 2
    rows = g_ref.shape[0] // 16
    for out_ref, holder in ((send_ref, 1 - core), (keep_ref, core)):
        at = 0
        for hop in (4, 3, 2, 1, 0):
            for flip in (False,) if hop in (0, 4) else (False, True):
                start = shard_rows(tile, holder, -hop, flip, rows)
                out_ref[at : at + rows] = g_ref[pl.ds(start, rows)]
                at += rows


def window(ref, x, y, planes, ny, lo=0, hi=None):
    value = ref[x : x + planes, y : y + ny, :, lo:hi]
    return value.reshape(-1, value.shape[-1])


def conv(s_ref, w_ref, x0, planes, ny, channels):
    acc = None
    for p in range(3):
        for q in range(3):
            t = 9 * p + 3 * q
            part = jnp.dot(
                window(s_ref, x0 + p, q, planes, ny),
                w_ref[t * channels : (t + 3) * channels],
                preferred_element_type=F32,
            )
            acc = part if acc is None else acc + part
    return acc


def store_taps(g_ref, p, q, part, channels):
    for rho in range(3):
        t = 9 * p + 3 * q + 2 - rho
        g_ref[t * channels : (t + 1) * channels] = part[:, rho * channels : (rho + 1) * channels]


def masked(value, mask_ref, side):
    area, channels = mask_ref.shape[1:]
    own = mask_ref[side].reshape(1, area, channels).astype(F32)
    return (value.reshape(-1, area, channels) * own).reshape(-1, channels)


def first_kernel(n, sx_ref, mask_ref, *rest):
    pieces, (pre_ref, act_ref, act_t_ref, w_ref) = rest[:n], rest[n:]
    area, channels = mask_ref.shape[1:]
    ny = sx_ref.shape[1] - 2
    depth = pre_ref.shape[0] // area
    fill_weight(pieces, w_ref)
    pre = conv(sx_ref, w_ref, 1, depth, ny, channels)
    pre_ref[...] = pre
    act = masked(pre * jax.nn.sigmoid(pre), mask_ref, 1).astype(BF)
    act_ref[...] = act
    act_t_ref[...] = act.T


def grad_two_kernel(sc_ref, act_t_ref, keep_ref, send_ref, g_ref):
    depth, ny, nz, channels = sc_ref.shape
    depth, ny, channels = depth - 2, ny - 2, channels // 3
    for p in range(3):
        for q in range(3):
            part = jnp.dot(
                act_t_ref[...],
                window(sc_ref, 2 - p, 2 - q, depth, ny),
                preferred_element_type=F32,
            )
            store_taps(g_ref, p, q, part.astype(BF), channels)
    split_shards(g_ref, keep_ref, send_ref)


def back_kernel(n, sc_ref, pre_ref, mask_ref, *rest):
    pieces, (sd_ref, w_ref) = rest[:n], rest[n:]
    area, channels = mask_ref.shape[1:]
    ny, nz = sc_ref.shape[1] - 2, sc_ref.shape[2]
    depth = pre_ref.shape[0] // area
    fill_weight(pieces, w_ref)
    acc = None
    for p in range(3):
        for q in range(3):
            for r in range(3):
                t = 9 * p + 3 * q + r
                lo = (2 - r) * channels
                part = lax.dot_general(
                    window(sc_ref, 2 - p, 2 - q, depth, ny, lo, lo + channels),
                    w_ref[t * channels : (t + 1) * channels],
                    (((1,), (1,)), ((), ())),
                    preferred_element_type=F32,
                )
                acc = part if acc is None else acc + part
    delta = masked(acc * silu_slope(pre_ref[...]), mask_ref, 1).astype(BF)
    clear_edges(sd_ref, ny)
    store_shifted(sd_ref, 0, delta, ny, nz, channels)


def grad_one_kernel(sd_ref, int_ref, keep_ref, send_ref, g_ref):
    depth, ny, nz, channels = sd_ref.shape
    ny, area, channels = ny - 2, (ny - 2) * nz, channels // 3
    for q in range(3):
        right = window(sd_ref, 0, 2 - q, depth, ny)
        for p in range(3):
            part = jnp.dot(
                int_ref[:, p * area : (p + depth) * area], right, preferred_element_type=F32
            )
            store_taps(g_ref, p, q, part.astype(BF), channels)
    split_shards(g_ref, keep_ref, send_ref)


def third_kernel(n, sx_ref, act_ref, mask_ref, *rest):
    out_ref, w_ref, v_ref, sa_ref = rest[2 * n :]
    area, channels = mask_ref.shape[1:]
    ny, nz = sx_ref.shape[1] - 2, sx_ref.shape[2]
    depth = act_ref.shape[0] // area
    fill_weight(rest[:n], w_ref)
    fill_weight(rest[n : 2 * n], v_ref)
    clear_edges(sa_ref, ny)
    store_shifted(sa_ref, 1, act_ref[...], ny, nz, channels)
    for x0, side in ((0, 0), (1 + depth, 2)):
        pre = conv(sx_ref, w_ref, x0, 1, ny, channels)
        act = masked(pre * jax.nn.sigmoid(pre), mask_ref, side).astype(BF)
        store_shifted(sa_ref, x0, act, ny, nz, channels)
    second = conv(sa_ref, v_ref, 0, depth, ny, channels)
    out_ref[...] = masked(second, mask_ref, 1).astype(BF).reshape(out_ref.shape)


def on_ring(features, weight_one, weight_two, cotangent, block_mask):
    depth, ny, nz, channels = features.shape
    area = ny * nz
    rows = weight_one.shape[0]
    chips = len(RING)
    tiles = 2 * chips
    loss_scale = 1.0 / math.sqrt(tiles * depth * area)
    shape = jax.ShapeDtypeStruct
    scratch = pltpu.VMEM
    shards = (shape((chips * rows, channels), BF),) * 2
    weights = scratch((27 * channels, channels), BF)
    flops = 2 * depth * area * 27 * channels * channels

    def permute(pairs):
        return functools.partial(lax.ppermute, axis_name="tiles", perm=pairs)

    def along_ring(core_from, core_to):
        return permute(
            [(2 * RING[i] + core_from, 2 * RING[(i + 1) % chips] + core_to) for i in range(chips)]
            + [
                (2 * RING[i] + 1 - core_from, 2 * RING[i - 1] + 1 - core_to)
                for i in range(chips)
            ]
        )

    onward, scatter_across = along_ring(0, 0), along_ring(0, 1)
    sibling = permute([(i, i ^ 1) for i in range(tiles)])
    up = permute([(i, (i + 1) % tiles) for i in range(tiles)])
    down = permute([(i, (i - 1) % tiles) for i in range(tiles)])

    def after(value, *others):
        return lax.optimization_barrier((value,) + others)[0]

    def kernel(body, name, mib, convs, outs, scratches, *operands, smem=0):
        return pl.pallas_call(
            body,
            name=name,
            out_shape=outs,
            in_specs=[pl.BlockSpec(memory_space=pltpu.SMEM)] * smem
            + [pl.BlockSpec(memory_space=pltpu.VMEM)] * (len(operands) - smem),
            out_specs=jax.tree.map(lambda _: pl.BlockSpec(memory_space=pltpu.VMEM), outs),
            scratch_shapes=scratches,
            compiler_params=pltpu.CompilerParams(vmem_limit_bytes=mib << 20),
            cost_estimate=pl.CostEstimate(
                flops=convs * flops, transcendentals=0, bytes_accessed=4 << 20
            ),
        )(*operands)

    a0 = jnp.concatenate([weight_one, sibling(weight_one)])
    b0 = jnp.concatenate([after(weight_two, a0), sibling(weight_two)])
    features_late, cot_late, _ = lax.optimization_barrier((features, cotangent, b0))
    low = up(jnp.concatenate([features_late[-2:], cot_late[-1:]]))
    high = down(jnp.concatenate([features_late[:2], cot_late[:1]]))

    a1, b1 = onward(a0), onward(b0)
    a2, qa1 = onward(a1), sibling(after(a1, low, high))
    b2, qb1 = onward(b1), sibling(after(b1, low, high))
    a3, qa2 = onward(after(a2, b1, low, high)), sibling(a2)
    sx, sc, in_t, near = kernel(
        prep_kernel,
        "prep",
        8,
        0,
        (
            shape((depth + 4, ny + 2, nz, 3 * channels), BF),
            shape((depth + 2, ny + 2, nz, 3 * channels), BF),
            shape((channels, (depth + 2) * area), BF),
            shape((3, area, channels), BF),
        ),
        [],
        jnp.transpose(block_mask, (1, 2, 0)),
        low,
        features,
        cotangent,
        high,
        smem=1,
    )
    a4, qa3 = onward(after(a3[:rows], b2, sx, qa1, qa2)), sibling(a3)
    b3, qb2 = onward(after(b2, qb1, qa3)), sibling(b2)
    b4, qb3 = onward(b3[:rows]), sibling(b3)
    qa4, qb4 = sibling(a4), sibling(b4)
    ones = [a0, a1, a2, a3, a4, qa1, qa2, qa3, qa4]
    twos = [b0, b1, b2, b3, b4, qb1, qb2, qb3, qb4]
    n = len(ones)

    pre, act, act_t = kernel(
        functools.partial(first_kernel, n),
        "first",
        8,
        1,
        (
            shape((depth * area, channels), F32),
            shape((depth * area, channels), BF),
            shape((channels, depth * area), BF),
        ),
        [weights],
        sx,
        near,
        *ones,
    )
    keep_two, send_two = kernel(
        grad_two_kernel, "grad_two", 8, 1, shards, [weights], sc, act_t
    )
    got_two = sibling(after(send_two, b3))

    def both(keep, got, lo, hi):
        return keep[lo * rows : hi * rows].astype(F32) + got[lo * rows : hi * rows].astype(F32)

    def step(keep, got, moving, k):
        if k == 0:
            return both(keep, got, 0, 1).astype(BF)
        if k == 1:
            moving = jnp.concatenate([moving, jnp.zeros_like(moving)])
        return (both(keep, got, 2 * k - 1, 2 * k + 1) + moving.astype(F32)).astype(BF)

    def finish(keep, got, message):
        total = both(keep, got, 7, 8) + onward(message[:rows]).astype(F32)
        return (total + scatter_across(message[rows:]).astype(F32)) * loss_scale

    delta = kernel(
        functools.partial(back_kernel, n),
        "back",
        8,
        1,
        shape((depth, ny + 2, nz, 3 * channels), BF),
        [weights],
        sc,
        pre,
        near,
        *twos,
    )
    keep_one, send_one = kernel(
        grad_one_kernel, "grad_one", 8, 1, shards, [weights], delta, in_t
    )
    two = onward(step(keep_two, got_two, None, 0))
    got_one = sibling(after(send_one, two))
    one = onward(step(keep_one, got_one, None, 0))
    features_out = kernel(
        functools.partial(third_kernel, n),
        "third",
        14,
        4,
        shape(features.shape, BF),
        [weights, weights, scratch((depth + 2, ny + 2, nz, 3 * channels), BF)],
        sx,
        after(act, two),
        near,
        *ones,
        *twos,
    )
    two = onward(step(keep_two, got_two, two, 1))
    one = onward(step(keep_one, got_one, one, 1))
    two = onward(step(keep_two, got_two, after(two, features_out), 2))
    one = onward(step(keep_one, got_one, one, 2))
    grad_two = finish(keep_two, got_two, step(keep_two, got_two, two, 3))
    return (features_out, finish(keep_one, got_one, step(keep_one, got_one, one, 3)), grad_two)


def solution(mesh):
    placed = (
        P(("groups", "tiles"), None, None, None),
        P("tiles", None),
        P("tiles", None),
        P(("groups", "tiles"), None, None, None),
        P("groups", None, None),
    )
    on_device = on_ring if mesh.shape["tiles"] == 2 * len(RING) else on_any
    return jax.shard_map(
        on_device,
        mesh=mesh,
        in_specs=placed,
        out_specs=(
            P(("groups", "tiles"), None, None, None),
            P(("groups", "tiles"), None),
            P(("groups", "tiles"), None),
        ),
        check_vma=False,
    )
```

```python
import functools
import math

import jax
import jax.numpy as jnp
from jax import lax
from jax.experimental import pallas as pl
from jax.experimental.pallas import tpu as pltpu
from jax.sharding import PartitionSpec as P

B = 4
RING = (0, 2, 4, 6, 7, 5, 3, 1)
BF = jnp.bfloat16
F32 = jnp.float32


def with_halo(block, axis, width):
    count = lax.axis_size(axis)
    forward = [(i, i + 1) for i in range(count - 1)]
    backward = [(target, source) for source, target in forward]
    low = lax.ppermute(block[-width:], axis, forward)
    high = lax.ppermute(block[:width], axis, backward)
    return low, high


def tap_columns(padded, flipped):
    extent = [padded.shape[d] - 2 for d in range(3)]
    taps = []
    for a in range(3):
        for b in range(3):
            for c in range(3):
                x, y, z = (2 - a, 2 - b, 2 - c) if flipped else (a, b, c)
                taps.append(padded[x : x + extent[0], y : y + extent[1], z : z + extent[2]])
    stacked = jnp.stack(taps, axis=3)
    return stacked.reshape(extent[0] * extent[1] * extent[2], 27 * padded.shape[3])


def expand_mask(cells, edge):
    planes, rows_y, rows_z = cells.shape
    values = jnp.broadcast_to(
        cells.astype(F32)[:, None, :, None, :, None], (planes, edge, rows_y, edge, rows_z, edge)
    )
    return values.reshape(planes * edge, rows_y * edge, rows_z * edge, 1)


def silu_slope(values):
    logistic = jax.nn.sigmoid(values)
    return logistic * (1.0 + values * (1.0 - logistic))


def near_cells_of(block_mask):
    padded_cells = jnp.pad(block_mask, ((1, 1), (0, 0), (0, 0)))
    return lax.dynamic_slice_in_dim(padded_cells, lax.axis_index("tiles"), 3, 0)


def on_any(features, weight_one, weight_two, cotangent, block_mask):
    depth, width_y, width_z, channels = features.shape
    loss_scale = 1.0 / math.sqrt(lax.axis_size("tiles") * depth * width_y * width_z)
    own_mask = expand_mask(near_cells_of(block_mask), B)[depth : 2 * depth]
    own_flat = own_mask.reshape(-1, 1)

    def cube(field):
        low, high = with_halo(field, "tiles", 1)
        field = jnp.concatenate([low, field, high], axis=0)
        return jnp.pad(field, ((0, 0), (1, 1), (1, 1), (0, 0)))

    def grad_piece(columns_in, rows_in):
        product = lax.dot_general(
            columns_in, rows_in, (((0,), (0,)), ((), ())), preferred_element_type=F32
        )
        return lax.psum_scatter(product * loss_scale, "tiles", scatter_dimension=0, tiled=True)

    full_one = lax.all_gather(weight_one, "tiles", axis=0, tiled=True)
    full_two = lax.all_gather(weight_two, "tiles", axis=0, tiled=True)
    weight_back = jnp.swapaxes(full_two.reshape(27, channels, channels), 1, 2).reshape(
        27 * channels, channels
    )
    inputs = (features * own_mask).astype(BF)
    feature_cols = tap_columns(cube(inputs), False)
    hidden_pre = jnp.dot(feature_cols, full_one, preferred_element_type=F32)
    active = (jax.nn.silu(hidden_pre) * own_flat).astype(BF).reshape(features.shape)
    active_cols = tap_columns(cube(active), False)
    second = jnp.dot(active_cols, full_two, preferred_element_type=F32)
    features_out = (second * own_flat).astype(BF).reshape(features.shape)
    cot = (cotangent * own_mask).astype(BF)
    grad_two = grad_piece(active_cols, cot.reshape(-1, channels))
    upstream = jnp.dot(tap_columns(cube(cot), True), weight_back, preferred_element_type=F32)
    hidden_grad = (upstream * silu_slope(hidden_pre) * own_flat).astype(BF)
    grad_one = grad_piece(feature_cols, hidden_grad)
    return (features_out, grad_one, grad_two)


def chip_at(place):
    return jnp.where(place < 4, 2 * place, 15 - 2 * place)


def place_of(tile):
    chip = tile // 2
    return jnp.where(chip % 2 == 0, chip // 2, 7 - chip // 2)


def shard_rows(tile, core, hop, flip, rows):
    step = jnp.where(core == 0, -hop, hop)
    chip = chip_at((place_of(tile) + step + 8) % 8)
    return pl.multiple_of((2 * chip + (1 - core if flip else core)) * rows, 16)


def store_shifted(out_ref, x0, rows, ny, nz, channels):
    planes = rows.shape[0] // (ny * nz)
    wide = rows.astype(F32)
    z = lax.broadcasted_iota(jnp.int32, wide.shape, 0) % nz
    before = jnp.where(z == 0, 0.0, pltpu.roll(wide, 1, 0)).astype(BF)
    after = jnp.where(z == nz - 1, 0.0, pltpu.roll(wide, wide.shape[0] - 1, 0)).astype(BF)
    for rho, value in enumerate((before, rows.astype(BF), after)):
        out_ref[x0 : x0 + planes, 1 : ny + 1, :, rho * channels : (rho + 1) * channels] = (
            value.reshape(planes, ny, nz, channels)
        )


def clear_edges(out_ref, ny):
    edge = jnp.zeros((out_ref.shape[0], 1) + tuple(out_ref.shape[2:]), BF)
    out_ref[:, 0:1] = edge
    out_ref[:, ny + 1 : ny + 2] = edge


def prep_kernel(cells_ref, low, f_own, c_own, high, sx_ref, sc_ref, int_ref, mask_ref):
    depth, ny, nz, channels = f_own.shape
    area = ny * nz
    tile = lax.axis_index("tiles")
    last = cells_ref.shape[2] - 1
    row = lax.broadcasted_iota(jnp.int32, (area, channels), 0)
    block_y, block_z = row // (B * nz), (row % nz) // B
    m = []
    for i in range(3):
        at = tile + i - 1
        inside = jnp.logical_and(at >= 0, at <= last)
        at = jnp.clip(at, 0, last)
        value = jnp.zeros((area, channels), F32)
        for y in range(ny // B):
            for z in range(nz // B):
                cell = jnp.where(inside, cells_ref[y, z, at], 0).astype(F32)
                here = jnp.logical_and(block_y == y, block_z == z)
                value = jnp.where(here, cell, value)
        value = value.astype(BF)
        mask_ref[i] = value
        m.append(value.reshape(1, area, channels))

    def rows(value, side):
        planes = value.shape[0]
        value = value.reshape(planes, area, channels) * m[side]
        return value.reshape(planes * area, channels)

    clear_edges(sx_ref, ny)
    clear_edges(sc_ref, ny)
    fs = [rows(low[0:2], 0), rows(f_own[...], 1), rows(high[0:2], 2)]
    for x0, value in zip((0, 2, 2 + depth), fs):
        store_shifted(sx_ref, x0, value, ny, nz, channels)
    int_ref[:, 0:area] = fs[0][area:].T
    int_ref[:, area : area + depth * area] = fs[1].T
    int_ref[:, area + depth * area :] = fs[2][:area].T
    for x0, value, side in ((0, low[2:3], 0), (1, c_own[...], 1), (1 + depth, high[2:3], 2)):
        store_shifted(sc_ref, x0, rows(value, side), ny, nz, channels)


PIECES = tuple((hop, False) for hop in range(5)) + tuple((hop, True) for hop in range(1, 5))


def fill_weight(pieces, w_ref):
    tile = lax.axis_index("tiles")
    core = tile % 2
    rows = w_ref.shape[0] // 16
    for piece, (hop, crossed) in zip(pieces, PIECES):
        holder = 1 - core if crossed else core
        for half in range(piece.shape[0] // rows):
            start = shard_rows(tile, holder, hop, half == 1, rows)
            w_ref[pl.ds(start, rows)] = piece[half * rows : (half + 1) * rows]


def split_shards(g_ref, keep_ref, send_ref):
    tile = lax.axis_index("tiles")
    core = tile % 2
    rows = g_ref.shape[0] // 16
    for out_ref, holder in ((send_ref, 1 - core), (keep_ref, core)):
        at = 0
        for hop in (4, 3, 2, 1, 0):
            for flip in (False,) if hop in (0, 4) else (False, True):
                start = shard_rows(tile, holder, -hop, flip, rows)
                out_ref[at : at + rows] = g_ref[pl.ds(start, rows)]
                at += rows


def window(ref, x, y, planes, ny, lo=0, hi=None):
    value = ref[x : x + planes, y : y + ny, :, lo:hi]
    return value.reshape(-1, value.shape[-1])


def conv(s_ref, w_ref, x0, planes, ny, channels):
    acc = None
    for p in range(3):
        for q in range(3):
            t = 9 * p + 3 * q
            part = jnp.dot(
                window(s_ref, x0 + p, q, planes, ny),
                w_ref[t * channels : (t + 3) * channels],
                preferred_element_type=F32,
            )
            acc = part if acc is None else acc + part
    return acc


def store_taps(g_ref, p, q, part, channels):
    for rho in range(3):
        t = 9 * p + 3 * q + 2 - rho
        g_ref[t * channels : (t + 1) * channels] = part[:, rho * channels : (rho + 1) * channels]


def masked(value, mask_ref, side):
    area, channels = mask_ref.shape[1:]
    own = mask_ref[side].reshape(1, area, channels).astype(F32)
    return (value.reshape(-1, area, channels) * own).reshape(-1, channels)


def first_kernel(n, sx_ref, mask_ref, *rest):
    pieces, (pre_ref, act_ref, act_t_ref, w_ref) = rest[:n], rest[n:]
    area, channels = mask_ref.shape[1:]
    ny = sx_ref.shape[1] - 2
    depth = pre_ref.shape[0] // area
    fill_weight(pieces, w_ref)
    pre = conv(sx_ref, w_ref, 1, depth, ny, channels)
    pre_ref[...] = pre
    act = masked(pre * jax.nn.sigmoid(pre), mask_ref, 1).astype(BF)
    act_ref[...] = act
    act_t_ref[...] = act.T


def grad_two_kernel(sc_ref, act_t_ref, keep_ref, send_ref, g_ref):
    depth, ny, nz, channels = sc_ref.shape
    depth, ny, channels = depth - 2, ny - 2, channels // 3
    for p in range(3):
        for q in range(3):
            part = jnp.dot(
                act_t_ref[...],
                window(sc_ref, 2 - p, 2 - q, depth, ny),
                preferred_element_type=F32,
            )
            store_taps(g_ref, p, q, part.astype(BF), channels)
    split_shards(g_ref, keep_ref, send_ref)


def back_kernel(n, sc_ref, pre_ref, mask_ref, *rest):
    pieces, (sd_ref, w_ref) = rest[:n], rest[n:]
    area, channels = mask_ref.shape[1:]
    ny, nz = sc_ref.shape[1] - 2, sc_ref.shape[2]
    depth = pre_ref.shape[0] // area
    fill_weight(pieces, w_ref)
    acc = None
    for p in range(3):
        for q in range(3):
            for r in range(3):
                t = 9 * p + 3 * q + r
                lo = (2 - r) * channels
                part = lax.dot_general(
                    window(sc_ref, 2 - p, 2 - q, depth, ny, lo, lo + channels),
                    w_ref[t * channels : (t + 1) * channels],
                    (((1,), (1,)), ((), ())),
                    preferred_element_type=F32,
                )
                acc = part if acc is None else acc + part
    delta = masked(acc * silu_slope(pre_ref[...]), mask_ref, 1).astype(BF)
    clear_edges(sd_ref, ny)
    store_shifted(sd_ref, 0, delta, ny, nz, channels)


def grad_one_kernel(sd_ref, int_ref, keep_ref, send_ref, g_ref):
    depth, ny, nz, channels = sd_ref.shape
    ny, area, channels = ny - 2, (ny - 2) * nz, channels // 3
    for q in range(3):
        right = window(sd_ref, 0, 2 - q, depth, ny)
        for p in range(3):
            part = jnp.dot(
                int_ref[:, p * area : (p + depth) * area], right, preferred_element_type=F32
            )
            store_taps(g_ref, p, q, part.astype(BF), channels)
    split_shards(g_ref, keep_ref, send_ref)


def third_kernel(n, sx_ref, act_ref, mask_ref, *rest):
    out_ref, w_ref, v_ref, sa_ref = rest[2 * n :]
    area, channels = mask_ref.shape[1:]
    ny, nz = sx_ref.shape[1] - 2, sx_ref.shape[2]
    depth = act_ref.shape[0] // area
    fill_weight(rest[:n], w_ref)
    fill_weight(rest[n : 2 * n], v_ref)
    clear_edges(sa_ref, ny)
    store_shifted(sa_ref, 1, act_ref[...], ny, nz, channels)
    for x0, side in ((0, 0), (1 + depth, 2)):
        pre = conv(sx_ref, w_ref, x0, 1, ny, channels)
        act = masked(pre * jax.nn.sigmoid(pre), mask_ref, side).astype(BF)
        store_shifted(sa_ref, x0, act, ny, nz, channels)
    second = conv(sa_ref, v_ref, 0, depth, ny, channels)
    out_ref[...] = masked(second, mask_ref, 1).astype(BF).reshape(out_ref.shape)


def on_ring(features, weight_one, weight_two, cotangent, block_mask):
    depth, ny, nz, channels = features.shape
    area = ny * nz
    rows = weight_one.shape[0]
    chips = len(RING)
    tiles = 2 * chips
    loss_scale = 1.0 / math.sqrt(tiles * depth * area)
    shape = jax.ShapeDtypeStruct
    scratch = pltpu.VMEM
    shards = (shape((chips * rows, channels), BF),) * 2
    weights = scratch((27 * channels, channels), BF)
    flops = 2 * depth * area * 27 * channels * channels

    def permute(pairs):
        return functools.partial(lax.ppermute, axis_name="tiles", perm=pairs)

    def along_ring(core_from, core_to):
        return permute(
            [(2 * RING[i] + core_from, 2 * RING[(i + 1) % chips] + core_to) for i in range(chips)]
            + [
                (2 * RING[i] + 1 - core_from, 2 * RING[i - 1] + 1 - core_to)
                for i in range(chips)
            ]
        )

    onward, gather_across, scatter_across = along_ring(0, 0), along_ring(1, 0), along_ring(0, 1)
    sibling = permute([(i, i ^ 1) for i in range(tiles)])
    up = permute([(i, (i + 1) % tiles) for i in range(tiles)])
    down = permute([(i, (i - 1) % tiles) for i in range(tiles)])

    def after(value, *others):
        return lax.optimization_barrier((value,) + others)[0]

    def kernel(body, name, mib, convs, outs, scratches, *operands, smem=0):
        return pl.pallas_call(
            body,
            name=name,
            out_shape=outs,
            in_specs=[pl.BlockSpec(memory_space=pltpu.SMEM)] * smem
            + [pl.BlockSpec(memory_space=pltpu.VMEM)] * (len(operands) - smem),
            out_specs=jax.tree.map(lambda _: pl.BlockSpec(memory_space=pltpu.VMEM), outs),
            scratch_shapes=scratches,
            compiler_params=pltpu.CompilerParams(vmem_limit_bytes=mib << 20),
            cost_estimate=pl.CostEstimate(
                flops=convs * flops, transcendentals=0, bytes_accessed=4 << 20
            ),
        )(*operands)

    a0 = jnp.concatenate([weight_one, sibling(weight_one)])
    b0 = jnp.concatenate([weight_two, sibling(weight_two)])
    features_late, cot_late, _ = lax.optimization_barrier((features, cotangent, b0))
    low = up(jnp.concatenate([features_late[-2:], cot_late[-1:]]))
    high = down(jnp.concatenate([features_late[:2], cot_late[:1]]))

    a1 = jnp.concatenate([onward(weight_one), gather_across(weight_one)])
    b1 = jnp.concatenate([onward(weight_two), gather_across(weight_two)])
    a2, qa1 = onward(a1), sibling(a1)
    b2, qb1 = onward(b1), sibling(b1)
    a3, qa2 = onward(after(a2, b1, low, high, qa1)), sibling(a2)
    sx, sc, in_t, near = kernel(
        prep_kernel,
        "prep",
        8,
        0,
        (
            shape((depth + 4, ny + 2, nz, 3 * channels), BF),
            shape((depth + 2, ny + 2, nz, 3 * channels), BF),
            shape((channels, (depth + 2) * area), BF),
            shape((3, area, channels), BF),
        ),
        [],
        jnp.transpose(block_mask, (1, 2, 0)),
        low,
        features,
        cotangent,
        high,
        smem=1,
    )
    b3, qb2 = onward(after(b2, qb1)), sibling(b2)
    a4, qa3 = onward(after(a3[:rows], b2, sx, qa2)), sibling(a3)
    b4, qb3 = onward(after(b3[:rows], qb2)), sibling(b3)
    qa4, qb4 = sibling(a4), sibling(b4)
    ones = [a0, a1, a2, a3, a4, qa1, qa2, qa3, qa4]
    twos = [b0, b1, b2, b3, b4, qb1, qb2, qb3, qb4]
    n = len(ones)

    pre, act, act_t = kernel(
        functools.partial(first_kernel, n),
        "first",
        8,
        1,
        (
            shape((depth * area, channels), F32),
            shape((depth * area, channels), BF),
            shape((channels, depth * area), BF),
        ),
        [weights],
        after(sx, b4),
        near,
        *ones,
    )
    keep_two, send_two = kernel(
        grad_two_kernel, "grad_two", 8, 1, shards, [weights], sc, act_t
    )
    got_two = sibling(send_two)

    def both(keep, got, lo, hi):
        return keep[lo * rows : hi * rows].astype(F32) + got[lo * rows : hi * rows].astype(F32)

    def step(keep, got, moving, k):
        if k == 0:
            return both(keep, got, 0, 1).astype(BF)
        if k == 1:
            moving = jnp.concatenate([moving, jnp.zeros_like(moving)])
        return (both(keep, got, 2 * k - 1, 2 * k + 1) + moving.astype(F32)).astype(BF)

    def finish(keep, got, message):
        total = both(keep, got, 7, 8) + onward(message[:rows]).astype(F32)
        return (total + scatter_across(message[rows:]).astype(F32)) * loss_scale

    delta = kernel(
        functools.partial(back_kernel, n),
        "back",
        8,
        1,
        shape((depth, ny + 2, nz, 3 * channels), BF),
        [weights],
        sc,
        pre,
        near,
        *twos,
    )
    keep_one, send_one = kernel(
        grad_one_kernel, "grad_one", 8, 1, shards, [weights], delta, in_t
    )
    two = onward(step(keep_two, after(got_two, keep_one), None, 0))
    got_one = sibling(send_one)
    one = onward(step(keep_one, got_one, None, 0))
    features_out = kernel(
        functools.partial(third_kernel, n),
        "third",
        14,
        1,
        shape(features.shape, BF),
        [weights, weights, scratch((depth + 2, ny + 2, nz, 3 * channels), BF)],
        sx,
        after(act, two),
        near,
        *ones,
        *twos,
    )
    two = onward(step(keep_two, got_two, two, 1))
    one = onward(step(keep_one, got_one, one, 1))
    two = onward(step(keep_two, got_two, after(two, features_out), 2))
    one = onward(step(keep_one, got_one, one, 2))
    grad_two = finish(keep_two, got_two, step(keep_two, got_two, two, 3))
    return (features_out, finish(keep_one, got_one, step(keep_one, got_one, one, 3)), grad_two)


def solution(mesh):
    placed = (
        P(("groups", "tiles"), None, None, None),
        P("tiles", None),
        P("tiles", None),
        P(("groups", "tiles"), None, None, None),
        P("groups", None, None),
    )
    on_device = on_ring if mesh.shape["tiles"] == 2 * len(RING) else on_any
    return jax.shard_map(
        on_device,
        mesh=mesh,
        in_specs=placed,
        out_specs=(
            P(("groups", "tiles"), None, None, None),
            P(("groups", "tiles"), None),
            P(("groups", "tiles"), None),
        ),
        check_vma=False,
    )
```

```python
import functools
import math

import jax
import jax.numpy as jnp
from jax import lax
from jax.experimental import pallas as pl
from jax.experimental.pallas import tpu as pltpu
from jax.sharding import PartitionSpec as P

B = 4
RING = (0, 2, 4, 6, 7, 5, 3, 1)
BF = jnp.bfloat16
F32 = jnp.float32


def with_halo(block, axis, width):
    count = lax.axis_size(axis)
    forward = [(i, i + 1) for i in range(count - 1)]
    backward = [(target, source) for source, target in forward]
    low = lax.ppermute(block[-width:], axis, forward)
    high = lax.ppermute(block[:width], axis, backward)
    return low, high


def tap_columns(padded, flipped):
    extent = [padded.shape[d] - 2 for d in range(3)]
    taps = []
    for a in range(3):
        for b in range(3):
            for c in range(3):
                x, y, z = (2 - a, 2 - b, 2 - c) if flipped else (a, b, c)
                taps.append(padded[x : x + extent[0], y : y + extent[1], z : z + extent[2]])
    stacked = jnp.stack(taps, axis=3)
    return stacked.reshape(extent[0] * extent[1] * extent[2], 27 * padded.shape[3])


def expand_mask(cells, edge):
    planes, rows_y, rows_z = cells.shape
    values = jnp.broadcast_to(
        cells.astype(F32)[:, None, :, None, :, None], (planes, edge, rows_y, edge, rows_z, edge)
    )
    return values.reshape(planes * edge, rows_y * edge, rows_z * edge, 1)


def silu_slope(values):
    logistic = jax.nn.sigmoid(values)
    return logistic * (1.0 + values * (1.0 - logistic))


def near_cells_of(block_mask):
    padded_cells = jnp.pad(block_mask, ((1, 1), (0, 0), (0, 0)))
    return lax.dynamic_slice_in_dim(padded_cells, lax.axis_index("tiles"), 3, 0)


def on_any(features, weight_one, weight_two, cotangent, block_mask):
    depth, width_y, width_z, channels = features.shape
    loss_scale = 1.0 / math.sqrt(lax.axis_size("tiles") * depth * width_y * width_z)
    own_mask = expand_mask(near_cells_of(block_mask), B)[depth : 2 * depth]
    own_flat = own_mask.reshape(-1, 1)

    def cube(field):
        low, high = with_halo(field, "tiles", 1)
        field = jnp.concatenate([low, field, high], axis=0)
        return jnp.pad(field, ((0, 0), (1, 1), (1, 1), (0, 0)))

    def grad_piece(columns_in, rows_in):
        product = lax.dot_general(
            columns_in, rows_in, (((0,), (0,)), ((), ())), preferred_element_type=F32
        )
        return lax.psum_scatter(product * loss_scale, "tiles", scatter_dimension=0, tiled=True)

    full_one = lax.all_gather(weight_one, "tiles", axis=0, tiled=True)
    full_two = lax.all_gather(weight_two, "tiles", axis=0, tiled=True)
    weight_back = jnp.swapaxes(full_two.reshape(27, channels, channels), 1, 2).reshape(
        27 * channels, channels
    )
    inputs = (features * own_mask).astype(BF)
    feature_cols = tap_columns(cube(inputs), False)
    hidden_pre = jnp.dot(feature_cols, full_one, preferred_element_type=F32)
    active = (jax.nn.silu(hidden_pre) * own_flat).astype(BF).reshape(features.shape)
    active_cols = tap_columns(cube(active), False)
    second = jnp.dot(active_cols, full_two, preferred_element_type=F32)
    features_out = (second * own_flat).astype(BF).reshape(features.shape)
    cot = (cotangent * own_mask).astype(BF)
    grad_two = grad_piece(active_cols, cot.reshape(-1, channels))
    upstream = jnp.dot(tap_columns(cube(cot), True), weight_back, preferred_element_type=F32)
    hidden_grad = (upstream * silu_slope(hidden_pre) * own_flat).astype(BF)
    grad_one = grad_piece(feature_cols, hidden_grad)
    return (features_out, grad_one, grad_two)


def chip_at(place):
    return jnp.where(place < 4, 2 * place, 15 - 2 * place)


def place_of(tile):
    chip = tile // 2
    return jnp.where(chip % 2 == 0, chip // 2, 7 - chip // 2)


def shard_rows(tile, core, hop, flip, rows):
    step = jnp.where(core == 0, -hop, hop)
    chip = chip_at((place_of(tile) + step + 8) % 8)
    return pl.multiple_of((2 * chip + (1 - core if flip else core)) * rows, 16)


def store_shifted(out_ref, x0, rows, ny, nz, channels):
    planes = rows.shape[0] // (ny * nz)
    wide = rows.astype(F32)
    z = lax.broadcasted_iota(jnp.int32, wide.shape, 0) % nz
    before = jnp.where(z == 0, 0.0, pltpu.roll(wide, 1, 0)).astype(BF)
    after = jnp.where(z == nz - 1, 0.0, pltpu.roll(wide, wide.shape[0] - 1, 0)).astype(BF)
    for rho, value in enumerate((before, rows.astype(BF), after)):
        out_ref[x0 : x0 + planes, 1 : ny + 1, :, rho * channels : (rho + 1) * channels] = (
            value.reshape(planes, ny, nz, channels)
        )


def clear_edges(out_ref, ny):
    edge = jnp.zeros((out_ref.shape[0], 1) + tuple(out_ref.shape[2:]), BF)
    out_ref[:, 0:1] = edge
    out_ref[:, ny + 1 : ny + 2] = edge


def prep_kernel(cells_ref, low, f_own, c_own, high, sx_ref, sc_ref, int_ref, mask_ref):
    depth, ny, nz, channels = f_own.shape
    area = ny * nz
    tile = lax.axis_index("tiles")
    last = cells_ref.shape[2] - 1
    row = lax.broadcasted_iota(jnp.int32, (area, channels), 0)
    block_y, block_z = row // (B * nz), (row % nz) // B
    m = []
    for i in range(3):
        at = tile + i - 1
        inside = jnp.logical_and(at >= 0, at <= last)
        at = jnp.clip(at, 0, last)
        value = jnp.zeros((area, channels), F32)
        for y in range(ny // B):
            for z in range(nz // B):
                cell = jnp.where(inside, cells_ref[y, z, at], 0).astype(F32)
                here = jnp.logical_and(block_y == y, block_z == z)
                value = jnp.where(here, cell, value)
        value = value.astype(BF)
        mask_ref[i] = value
        m.append(value.reshape(1, area, channels))

    def rows(value, side):
        planes = value.shape[0]
        value = value.reshape(planes, area, channels) * m[side]
        return value.reshape(planes * area, channels)

    clear_edges(sx_ref, ny)
    clear_edges(sc_ref, ny)
    fs = [rows(low[0:2], 0), rows(f_own[...], 1), rows(high[0:2], 2)]
    for x0, value in zip((0, 2, 2 + depth), fs):
        store_shifted(sx_ref, x0, value, ny, nz, channels)
    int_ref[:, 0:area] = fs[0][area:].T
    int_ref[:, area : area + depth * area] = fs[1].T
    int_ref[:, area + depth * area :] = fs[2][:area].T
    for x0, value, side in ((0, low[2:3], 0), (1, c_own[...], 1), (1 + depth, high[2:3], 2)):
        store_shifted(sc_ref, x0, rows(value, side), ny, nz, channels)


PIECES = tuple((hop, False) for hop in range(5)) + tuple((hop, True) for hop in range(1, 5))


def fill_weight(pieces, w_ref):
    tile = lax.axis_index("tiles")
    core = tile % 2
    rows = w_ref.shape[0] // 16
    for piece, (hop, crossed) in zip(pieces, PIECES):
        holder = 1 - core if crossed else core
        for half in range(piece.shape[0] // rows):
            start = shard_rows(tile, holder, hop, half == 1, rows)
            w_ref[pl.ds(start, rows)] = piece[half * rows : (half + 1) * rows]


def split_shards(g_ref, keep_ref, send_ref):
    tile = lax.axis_index("tiles")
    core = tile % 2
    rows = g_ref.shape[0] // 16
    for out_ref, holder in ((send_ref, 1 - core), (keep_ref, core)):
        at = 0
        for hop in (4, 3, 2, 1, 0):
            for flip in (False,) if hop in (0, 4) else (False, True):
                start = shard_rows(tile, holder, -hop, flip, rows)
                out_ref[at : at + rows] = g_ref[pl.ds(start, rows)]
                at += rows


def window(ref, x, y, planes, ny, lo=0, hi=None):
    value = ref[x : x + planes, y : y + ny, :, lo:hi]
    return value.reshape(-1, value.shape[-1])


def conv(s_ref, w_ref, x0, planes, ny, channels):
    acc = None
    for p in range(3):
        for q in range(3):
            t = 9 * p + 3 * q
            part = jnp.dot(
                window(s_ref, x0 + p, q, planes, ny),
                w_ref[t * channels : (t + 3) * channels],
                preferred_element_type=F32,
            )
            acc = part if acc is None else acc + part
    return acc


def store_taps(g_ref, p, q, part, channels):
    for rho in range(3):
        t = 9 * p + 3 * q + 2 - rho
        g_ref[t * channels : (t + 1) * channels] = part[:, rho * channels : (rho + 1) * channels]


def masked(value, mask_ref, side):
    area, channels = mask_ref.shape[1:]
    own = mask_ref[side].reshape(1, area, channels).astype(F32)
    return (value.reshape(-1, area, channels) * own).reshape(-1, channels)


def first_kernel(n, sx_ref, mask_ref, *rest):
    pieces, (pre_ref, act_ref, act_t_ref, w_ref) = rest[:n], rest[n:]
    area, channels = mask_ref.shape[1:]
    ny = sx_ref.shape[1] - 2
    depth = pre_ref.shape[0] // area
    fill_weight(pieces, w_ref)
    pre = conv(sx_ref, w_ref, 1, depth, ny, channels)
    pre_ref[...] = pre
    act = masked(pre * jax.nn.sigmoid(pre), mask_ref, 1).astype(BF)
    act_ref[...] = act
    act_t_ref[...] = act.T


def grad_two_kernel(sc_ref, act_t_ref, keep_ref, send_ref, g_ref):
    depth, ny, nz, channels = sc_ref.shape
    depth, ny, channels = depth - 2, ny - 2, channels // 3
    for p in range(3):
        for q in range(3):
            part = jnp.dot(
                act_t_ref[...],
                window(sc_ref, 2 - p, 2 - q, depth, ny),
                preferred_element_type=F32,
            )
            store_taps(g_ref, p, q, part.astype(BF), channels)
    split_shards(g_ref, keep_ref, send_ref)


def back_kernel(n, sc_ref, pre_ref, mask_ref, *rest):
    pieces, (sd_ref, w_ref) = rest[:n], rest[n:]
    area, channels = mask_ref.shape[1:]
    ny, nz = sc_ref.shape[1] - 2, sc_ref.shape[2]
    depth = pre_ref.shape[0] // area
    fill_weight(pieces, w_ref)
    acc = None
    for p in range(3):
        for q in range(3):
            for r in range(3):
                t = 9 * p + 3 * q + r
                lo = (2 - r) * channels
                part = lax.dot_general(
                    window(sc_ref, 2 - p, 2 - q, depth, ny, lo, lo + channels),
                    w_ref[t * channels : (t + 1) * channels],
                    (((1,), (1,)), ((), ())),
                    preferred_element_type=F32,
                )
                acc = part if acc is None else acc + part
    delta = masked(acc * silu_slope(pre_ref[...]), mask_ref, 1).astype(BF)
    clear_edges(sd_ref, ny)
    store_shifted(sd_ref, 0, delta, ny, nz, channels)


def grad_one_kernel(sd_ref, int_ref, keep_ref, send_ref, g_ref):
    depth, ny, nz, channels = sd_ref.shape
    ny, area, channels = ny - 2, (ny - 2) * nz, channels // 3
    for q in range(3):
        right = window(sd_ref, 0, 2 - q, depth, ny)
        for p in range(3):
            part = jnp.dot(
                int_ref[:, p * area : (p + depth) * area], right, preferred_element_type=F32
            )
            store_taps(g_ref, p, q, part.astype(BF), channels)
    split_shards(g_ref, keep_ref, send_ref)


def third_kernel(n, sx_ref, act_ref, mask_ref, *rest):
    out_ref, w_ref, v_ref, sa_ref = rest[2 * n :]
    area, channels = mask_ref.shape[1:]
    ny, nz = sx_ref.shape[1] - 2, sx_ref.shape[2]
    depth = act_ref.shape[0] // area
    fill_weight(rest[:n], w_ref)
    fill_weight(rest[n : 2 * n], v_ref)
    clear_edges(sa_ref, ny)
    store_shifted(sa_ref, 1, act_ref[...], ny, nz, channels)
    for x0, side in ((0, 0), (1 + depth, 2)):
        pre = conv(sx_ref, w_ref, x0, 1, ny, channels)
        act = masked(pre * jax.nn.sigmoid(pre), mask_ref, side).astype(BF)
        store_shifted(sa_ref, x0, act, ny, nz, channels)
    second = conv(sa_ref, v_ref, 0, depth, ny, channels)
    out_ref[...] = masked(second, mask_ref, 1).astype(BF).reshape(out_ref.shape)


def on_ring(features, weight_one, weight_two, cotangent, block_mask):
    depth, ny, nz, channels = features.shape
    area = ny * nz
    rows = weight_one.shape[0]
    chips = len(RING)
    tiles = 2 * chips
    loss_scale = 1.0 / math.sqrt(tiles * depth * area)
    shape = jax.ShapeDtypeStruct
    scratch = pltpu.VMEM
    shards = (shape((chips * rows, channels), BF),) * 2
    weights = scratch((27 * channels, channels), BF)
    flops = 2 * depth * area * 27 * channels * channels

    def permute(pairs):
        return functools.partial(lax.ppermute, axis_name="tiles", perm=pairs)

    def along_ring(core_from, core_to):
        return permute(
            [(2 * RING[i] + core_from, 2 * RING[(i + 1) % chips] + core_to) for i in range(chips)]
            + [
                (2 * RING[i] + 1 - core_from, 2 * RING[i - 1] + 1 - core_to)
                for i in range(chips)
            ]
        )

    onward, gather_across, scatter_across = along_ring(0, 0), along_ring(1, 0), along_ring(0, 1)
    sibling = permute([(i, i ^ 1) for i in range(tiles)])
    up = permute([(i, (i + 1) % tiles) for i in range(tiles)])
    down = permute([(i, (i - 1) % tiles) for i in range(tiles)])

    def after(value, *others):
        return lax.optimization_barrier((value,) + others)[0]

    def kernel(body, name, mib, convs, outs, scratches, *operands, smem=0):
        return pl.pallas_call(
            body,
            name=name,
            out_shape=outs,
            in_specs=[pl.BlockSpec(memory_space=pltpu.SMEM)] * smem
            + [pl.BlockSpec(memory_space=pltpu.VMEM)] * (len(operands) - smem),
            out_specs=jax.tree.map(lambda _: pl.BlockSpec(memory_space=pltpu.VMEM), outs),
            scratch_shapes=scratches,
            compiler_params=pltpu.CompilerParams(vmem_limit_bytes=mib << 20),
            cost_estimate=pl.CostEstimate(
                flops=convs * flops, transcendentals=0, bytes_accessed=4 << 20
            ),
        )(*operands)

    a0 = jnp.concatenate([weight_one, sibling(weight_one)])
    b0 = jnp.concatenate([weight_two, sibling(weight_two)])
    features_late, cot_late, _ = lax.optimization_barrier((features, cotangent, b0))
    low = up(jnp.concatenate([features_late[-2:], cot_late[-1:]]))
    high = down(jnp.concatenate([features_late[:2], cot_late[:1]]))

    a1 = jnp.concatenate([onward(weight_one), gather_across(weight_one)])
    b1 = jnp.concatenate([onward(weight_two), gather_across(weight_two)])
    a2, qa1 = onward(a1), sibling(a1)
    b2, qb1 = onward(after(b1, low, high)), sibling(b1)
    a3, qa2 = onward(after(a2, b1)), sibling(a2)
    sx, sc, in_t, near = kernel(
        prep_kernel,
        "prep",
        8,
        0,
        (
            shape((depth + 4, ny + 2, nz, 3 * channels), BF),
            shape((depth + 2, ny + 2, nz, 3 * channels), BF),
            shape((channels, (depth + 2) * area), BF),
            shape((3, area, channels), BF),
        ),
        [],
        jnp.transpose(block_mask, (1, 2, 0)),
        low,
        features,
        cotangent,
        high,
        smem=1,
    )
    b3, qb2 = onward(b2), sibling(b2)
    a4, qa3 = onward(after(a3[:rows], b2, sx, qa1)), sibling(a3)
    b4, qb3 = onward(after(b3[:rows], qb1)), sibling(b3)
    qa4 = sibling(a4)
    ones = [a0, a1, a2, a3, a4, qa1, qa2, qa3, qa4]
    n = len(ones)

    pre, act, act_t = kernel(
        functools.partial(first_kernel, n),
        "first",
        8,
        1,
        (
            shape((depth * area, channels), F32),
            shape((depth * area, channels), BF),
            shape((channels, depth * area), BF),
        ),
        [weights],
        after(sx, b3),
        near,
        *ones,
    )
    qb4 = sibling(after(b4, act_t))
    twos = [b0, b1, b2, b3, b4, qb1, qb2, qb3, qb4]
    keep_two, send_two = kernel(
        grad_two_kernel, "grad_two", 8, 1, shards, [weights], sc, act_t
    )
    got_two = sibling(send_two)

    def both(keep, got, lo, hi):
        return keep[lo * rows : hi * rows].astype(F32) + got[lo * rows : hi * rows].astype(F32)

    def step(keep, got, moving, k):
        if k == 0:
            return both(keep, got, 0, 1).astype(BF)
        if k == 1:
            moving = jnp.concatenate([moving, jnp.zeros_like(moving)])
        return (both(keep, got, 2 * k - 1, 2 * k + 1) + moving.astype(F32)).astype(BF)

    def finish(keep, got, message):
        total = both(keep, got, 7, 8) + onward(message[:rows]).astype(F32)
        return (total + scatter_across(message[rows:]).astype(F32)) * loss_scale

    delta = kernel(
        functools.partial(back_kernel, n),
        "back",
        8,
        1,
        shape((depth, ny + 2, nz, 3 * channels), BF),
        [weights],
        sc,
        pre,
        near,
        *twos,
    )
    keep_one, send_one = kernel(
        grad_one_kernel, "grad_one", 8, 1, shards, [weights], delta, in_t
    )
    two = onward(step(keep_two, after(got_two, keep_one), None, 0))
    got_one = sibling(send_one)
    one = onward(step(keep_one, got_one, None, 0))
    features_out = kernel(
        functools.partial(third_kernel, n),
        "third",
        14,
        1,
        shape(features.shape, BF),
        [weights, weights, scratch((depth + 2, ny + 2, nz, 3 * channels), BF)],
        sx,
        after(act, two, one),
        near,
        *ones,
        *twos,
    )
    two = onward(step(keep_two, got_two, two, 1))
    one = onward(step(keep_one, got_one, one, 1))
    two = onward(step(keep_two, got_two, two, 2))
    one = onward(step(keep_one, got_one, after(one, features_out), 2))
    grad_two = finish(keep_two, got_two, step(keep_two, got_two, two, 3))
    return (features_out, finish(keep_one, got_one, step(keep_one, got_one, one, 3)), grad_two)


def solution(mesh):
    placed = (
        P(("groups", "tiles"), None, None, None),
        P("tiles", None),
        P("tiles", None),
        P(("groups", "tiles"), None, None, None),
        P("groups", None, None),
    )
    on_device = on_ring if mesh.shape["tiles"] == 2 * len(RING) else on_any
    return jax.shard_map(
        on_device,
        mesh=mesh,
        in_specs=placed,
        out_specs=(
            P(("groups", "tiles"), None, None, None),
            P(("groups", "tiles"), None),
            P(("groups", "tiles"), None),
        ),
        check_vma=False,
    )
```

```python
import functools
import math

import jax
import jax.numpy as jnp
from jax import lax
from jax.experimental import pallas as pl
from jax.experimental.pallas import tpu as pltpu
from jax.sharding import PartitionSpec as P

B = 4
RING = (0, 2, 4, 6, 7, 5, 3, 1)
BF = jnp.bfloat16
F32 = jnp.float32


def with_halo(block, axis, width):
    count = lax.axis_size(axis)
    forward = [(i, i + 1) for i in range(count - 1)]
    backward = [(target, source) for source, target in forward]
    low = lax.ppermute(block[-width:], axis, forward)
    high = lax.ppermute(block[:width], axis, backward)
    return low, high


def tap_columns(padded, flipped):
    extent = [padded.shape[d] - 2 for d in range(3)]
    taps = []
    for a in range(3):
        for b in range(3):
            for c in range(3):
                x, y, z = (2 - a, 2 - b, 2 - c) if flipped else (a, b, c)
                taps.append(padded[x : x + extent[0], y : y + extent[1], z : z + extent[2]])
    stacked = jnp.stack(taps, axis=3)
    return stacked.reshape(extent[0] * extent[1] * extent[2], 27 * padded.shape[3])


def expand_mask(cells, edge):
    planes, rows_y, rows_z = cells.shape
    values = jnp.broadcast_to(
        cells.astype(F32)[:, None, :, None, :, None], (planes, edge, rows_y, edge, rows_z, edge)
    )
    return values.reshape(planes * edge, rows_y * edge, rows_z * edge, 1)


def silu_slope(values):
    logistic = jax.nn.sigmoid(values)
    return logistic * (1.0 + values * (1.0 - logistic))


def near_cells_of(block_mask):
    padded_cells = jnp.pad(block_mask, ((1, 1), (0, 0), (0, 0)))
    return lax.dynamic_slice_in_dim(padded_cells, lax.axis_index("tiles"), 3, 0)


def on_any(features, weight_one, weight_two, cotangent, block_mask):
    depth, width_y, width_z, channels = features.shape
    loss_scale = 1.0 / math.sqrt(lax.axis_size("tiles") * depth * width_y * width_z)
    own_mask = expand_mask(near_cells_of(block_mask), B)[depth : 2 * depth]
    own_flat = own_mask.reshape(-1, 1)

    def cube(field):
        low, high = with_halo(field, "tiles", 1)
        field = jnp.concatenate([low, field, high], axis=0)
        return jnp.pad(field, ((0, 0), (1, 1), (1, 1), (0, 0)))

    def grad_piece(columns_in, rows_in):
        product = lax.dot_general(
            columns_in, rows_in, (((0,), (0,)), ((), ())), preferred_element_type=F32
        )
        return lax.psum_scatter(product * loss_scale, "tiles", scatter_dimension=0, tiled=True)

    full_one = lax.all_gather(weight_one, "tiles", axis=0, tiled=True)
    full_two = lax.all_gather(weight_two, "tiles", axis=0, tiled=True)
    weight_back = jnp.swapaxes(full_two.reshape(27, channels, channels), 1, 2).reshape(
        27 * channels, channels
    )
    inputs = (features * own_mask).astype(BF)
    feature_cols = tap_columns(cube(inputs), False)
    hidden_pre = jnp.dot(feature_cols, full_one, preferred_element_type=F32)
    active = (jax.nn.silu(hidden_pre) * own_flat).astype(BF).reshape(features.shape)
    active_cols = tap_columns(cube(active), False)
    second = jnp.dot(active_cols, full_two, preferred_element_type=F32)
    features_out = (second * own_flat).astype(BF).reshape(features.shape)
    cot = (cotangent * own_mask).astype(BF)
    grad_two = grad_piece(active_cols, cot.reshape(-1, channels))
    upstream = jnp.dot(tap_columns(cube(cot), True), weight_back, preferred_element_type=F32)
    hidden_grad = (upstream * silu_slope(hidden_pre) * own_flat).astype(BF)
    grad_one = grad_piece(feature_cols, hidden_grad)
    return (features_out, grad_one, grad_two)


def chip_at(place):
    return jnp.where(place < 4, 2 * place, 15 - 2 * place)


def place_of(tile):
    chip = tile // 2
    return jnp.where(chip % 2 == 0, chip // 2, 7 - chip // 2)


def shard_rows(tile, core, hop, flip, rows):
    step = jnp.where(core == 0, -hop, hop)
    chip = chip_at((place_of(tile) + step + 8) % 8)
    return pl.multiple_of((2 * chip + (1 - core if flip else core)) * rows, 16)


def store_shifted(out_ref, x0, rows, ny, nz, channels):
    planes = rows.shape[0] // (ny * nz)
    wide = rows.astype(F32)
    z = lax.broadcasted_iota(jnp.int32, wide.shape, 0) % nz
    before = jnp.where(z == 0, 0.0, pltpu.roll(wide, 1, 0)).astype(BF)
    after = jnp.where(z == nz - 1, 0.0, pltpu.roll(wide, wide.shape[0] - 1, 0)).astype(BF)
    for rho, value in enumerate((before, rows.astype(BF), after)):
        out_ref[x0 : x0 + planes, 1 : ny + 1, :, rho * channels : (rho + 1) * channels] = (
            value.reshape(planes, ny, nz, channels)
        )


def clear_edges(out_ref, ny):
    edge = jnp.zeros((out_ref.shape[0], 1) + tuple(out_ref.shape[2:]), BF)
    out_ref[:, 0:1] = edge
    out_ref[:, ny + 1 : ny + 2] = edge


def prep_kernel(cells_ref, low, f_own, c_own, high, sx_ref, sc_ref, int_ref, mask_ref):
    depth, ny, nz, channels = f_own.shape
    area = ny * nz
    tile = lax.axis_index("tiles")
    last = cells_ref.shape[2] - 1
    row = lax.broadcasted_iota(jnp.int32, (area, channels), 0)
    block_y, block_z = row // (B * nz), (row % nz) // B
    m = []
    for i in range(3):
        at = tile + i - 1
        inside = jnp.logical_and(at >= 0, at <= last)
        at = jnp.clip(at, 0, last)
        value = jnp.zeros((area, channels), F32)
        for y in range(ny // B):
            for z in range(nz // B):
                cell = jnp.where(inside, cells_ref[y, z, at], 0).astype(F32)
                here = jnp.logical_and(block_y == y, block_z == z)
                value = jnp.where(here, cell, value)
        value = value.astype(BF)
        mask_ref[i] = value
        m.append(value.reshape(1, area, channels))

    def rows(value, side):
        planes = value.shape[0]
        value = value.reshape(planes, area, channels) * m[side]
        return value.reshape(planes * area, channels)

    clear_edges(sx_ref, ny)
    clear_edges(sc_ref, ny)
    fs = [rows(low[0:2], 0), rows(f_own[...], 1), rows(high[0:2], 2)]
    for x0, value in zip((0, 2, 2 + depth), fs):
        store_shifted(sx_ref, x0, value, ny, nz, channels)
    int_ref[:, 0:area] = fs[0][area:].T
    int_ref[:, area : area + depth * area] = fs[1].T
    int_ref[:, area + depth * area :] = fs[2][:area].T
    for x0, value, side in ((0, low[2:3], 0), (1, c_own[...], 1), (1 + depth, high[2:3], 2)):
        store_shifted(sc_ref, x0, rows(value, side), ny, nz, channels)


PIECES = tuple((hop, False) for hop in range(5)) + tuple((hop, True) for hop in range(1, 5))


def fill_weight(pieces, w_ref):
    tile = lax.axis_index("tiles")
    core = tile % 2
    rows = w_ref.shape[0] // 16
    for piece, (hop, crossed) in zip(pieces, PIECES):
        holder = 1 - core if crossed else core
        for half in range(piece.shape[0] // rows):
            start = shard_rows(tile, holder, hop, half == 1, rows)
            w_ref[pl.ds(start, rows)] = piece[half * rows : (half + 1) * rows]


def split_shards(g_ref, keep_ref, send_ref):
    tile = lax.axis_index("tiles")
    core = tile % 2
    rows = g_ref.shape[0] // 16
    for out_ref, holder in ((send_ref, 1 - core), (keep_ref, core)):
        at = 0
        for hop in (4, 3, 2, 1, 0):
            for flip in (False,) if hop in (0, 4) else (False, True):
                start = shard_rows(tile, holder, -hop, flip, rows)
                out_ref[at : at + rows] = g_ref[pl.ds(start, rows)]
                at += rows


def window(ref, x, y, planes, ny, lo=0, hi=None):
    value = ref[x : x + planes, y : y + ny, :, lo:hi]
    return value.reshape(-1, value.shape[-1])


def conv(s_ref, w_ref, x0, planes, ny, channels):
    acc = None
    for p in range(3):
        for q in range(3):
            t = 9 * p + 3 * q
            part = jnp.dot(
                window(s_ref, x0 + p, q, planes, ny),
                w_ref[t * channels : (t + 3) * channels],
                preferred_element_type=F32,
            )
            acc = part if acc is None else acc + part
    return acc


def store_taps(g_ref, p, q, part, channels):
    for rho in range(3):
        t = 9 * p + 3 * q + 2 - rho
        g_ref[t * channels : (t + 1) * channels] = part[:, rho * channels : (rho + 1) * channels]


def masked(value, mask_ref, side):
    area, channels = mask_ref.shape[1:]
    own = mask_ref[side].reshape(1, area, channels).astype(F32)
    return (value.reshape(-1, area, channels) * own).reshape(-1, channels)


def first_kernel(n, sx_ref, mask_ref, *rest):
    pieces, (pre_ref, act_ref, act_t_ref, w_ref) = rest[:n], rest[n:]
    area, channels = mask_ref.shape[1:]
    ny = sx_ref.shape[1] - 2
    depth = pre_ref.shape[0] // area
    fill_weight(pieces, w_ref)
    pre = conv(sx_ref, w_ref, 1, depth, ny, channels)
    pre_ref[...] = pre
    act = masked(pre * jax.nn.sigmoid(pre), mask_ref, 1).astype(BF)
    act_ref[...] = act
    act_t_ref[...] = act.T


def grad_two_kernel(sc_ref, act_t_ref, keep_ref, send_ref, g_ref):
    depth, ny, nz, channels = sc_ref.shape
    depth, ny, channels = depth - 2, ny - 2, channels // 3
    for p in range(3):
        for q in range(3):
            part = jnp.dot(
                act_t_ref[...],
                window(sc_ref, 2 - p, 2 - q, depth, ny),
                preferred_element_type=F32,
            )
            store_taps(g_ref, p, q, part.astype(BF), channels)
    split_shards(g_ref, keep_ref, send_ref)


def back_kernel(n, sc_ref, pre_ref, mask_ref, *rest):
    pieces, (sd_ref, w_ref) = rest[:n], rest[n:]
    area, channels = mask_ref.shape[1:]
    ny, nz = sc_ref.shape[1] - 2, sc_ref.shape[2]
    depth = pre_ref.shape[0] // area
    fill_weight(pieces, w_ref)
    acc = None
    for p in range(3):
        for q in range(3):
            for r in range(3):
                t = 9 * p + 3 * q + r
                lo = (2 - r) * channels
                part = lax.dot_general(
                    window(sc_ref, 2 - p, 2 - q, depth, ny, lo, lo + channels),
                    w_ref[t * channels : (t + 1) * channels],
                    (((1,), (1,)), ((), ())),
                    preferred_element_type=F32,
                )
                acc = part if acc is None else acc + part
    delta = masked(acc * silu_slope(pre_ref[...]), mask_ref, 1).astype(BF)
    clear_edges(sd_ref, ny)
    store_shifted(sd_ref, 0, delta, ny, nz, channels)


def grad_one_kernel(sd_ref, int_ref, keep_ref, send_ref, g_ref):
    depth, ny, nz, channels = sd_ref.shape
    ny, area, channels = ny - 2, (ny - 2) * nz, channels // 3
    for q in range(3):
        right = window(sd_ref, 0, 2 - q, depth, ny)
        for p in range(3):
            part = jnp.dot(
                int_ref[:, p * area : (p + depth) * area], right, preferred_element_type=F32
            )
            store_taps(g_ref, p, q, part.astype(BF), channels)
    split_shards(g_ref, keep_ref, send_ref)


def third_kernel(n, sx_ref, act_ref, mask_ref, *rest):
    out_ref, w_ref, v_ref, sa_ref = rest[2 * n :]
    area, channels = mask_ref.shape[1:]
    ny, nz = sx_ref.shape[1] - 2, sx_ref.shape[2]
    depth = act_ref.shape[0] // area
    fill_weight(rest[:n], w_ref)
    fill_weight(rest[n : 2 * n], v_ref)
    clear_edges(sa_ref, ny)
    store_shifted(sa_ref, 1, act_ref[...], ny, nz, channels)
    for x0, side in ((0, 0), (1 + depth, 2)):
        pre = conv(sx_ref, w_ref, x0, 1, ny, channels)
        act = masked(pre * jax.nn.sigmoid(pre), mask_ref, side).astype(BF)
        store_shifted(sa_ref, x0, act, ny, nz, channels)
    second = conv(sa_ref, v_ref, 0, depth, ny, channels)
    out_ref[...] = masked(second, mask_ref, 1).astype(BF).reshape(out_ref.shape)


def on_ring(features, weight_one, weight_two, cotangent, block_mask):
    depth, ny, nz, channels = features.shape
    area = ny * nz
    rows = weight_one.shape[0]
    chips = len(RING)
    tiles = 2 * chips
    loss_scale = 1.0 / math.sqrt(tiles * depth * area)
    shape = jax.ShapeDtypeStruct
    scratch = pltpu.VMEM
    shards = (shape((chips * rows, channels), BF),) * 2
    weights = scratch((27 * channels, channels), BF)
    flops = 2 * depth * area * 27 * channels * channels

    def permute(pairs):
        return functools.partial(lax.ppermute, axis_name="tiles", perm=pairs)

    def along_ring(core_from, core_to):
        return permute(
            [(2 * RING[i] + core_from, 2 * RING[(i + 1) % chips] + core_to) for i in range(chips)]
            + [
                (2 * RING[i] + 1 - core_from, 2 * RING[i - 1] + 1 - core_to)
                for i in range(chips)
            ]
        )

    onward, gather_across, scatter_across = along_ring(0, 0), along_ring(1, 0), along_ring(0, 1)
    sibling = permute([(i, i ^ 1) for i in range(tiles)])
    up = permute([(i, (i + 1) % tiles) for i in range(tiles)])
    down = permute([(i, (i - 1) % tiles) for i in range(tiles)])

    def after(value, *others):
        return lax.optimization_barrier((value,) + others)[0]

    def kernel(body, name, mib, convs, outs, scratches, *operands, smem=0):
        return pl.pallas_call(
            body,
            name=name,
            out_shape=outs,
            in_specs=[pl.BlockSpec(memory_space=pltpu.SMEM)] * smem
            + [pl.BlockSpec(memory_space=pltpu.VMEM)] * (len(operands) - smem),
            out_specs=jax.tree.map(lambda _: pl.BlockSpec(memory_space=pltpu.VMEM), outs),
            scratch_shapes=scratches,
            compiler_params=pltpu.CompilerParams(vmem_limit_bytes=mib << 20),
            cost_estimate=pl.CostEstimate(
                flops=convs * flops, transcendentals=0, bytes_accessed=4 << 20
            ),
        )(*operands)

    a0 = jnp.concatenate([weight_one, sibling(weight_one)])
    b0 = jnp.concatenate([weight_two, sibling(weight_two)])
    features_late, cot_late, _ = lax.optimization_barrier((features, cotangent, b0))
    low = up(jnp.concatenate([features_late[-2:], cot_late[-1:]]))
    high = down(jnp.concatenate([features_late[:2], cot_late[:1]]))

    a1 = jnp.concatenate([onward(weight_one), gather_across(weight_one)])
    b1 = jnp.concatenate([onward(weight_two), gather_across(weight_two)])
    a2, qa1 = onward(a1), sibling(a1)
    b2, qb1 = onward(after(b1, low, high)), sibling(b1)
    a3, qa2 = onward(after(a2, b1)), sibling(a2)
    sx, sc, in_t, near = kernel(
        prep_kernel,
        "prep",
        8,
        0,
        (
            shape((depth + 4, ny + 2, nz, 3 * channels), BF),
            shape((depth + 2, ny + 2, nz, 3 * channels), BF),
            shape((channels, (depth + 2) * area), BF),
            shape((3, area, channels), BF),
        ),
        [],
        jnp.transpose(block_mask, (1, 2, 0)),
        low,
        features,
        cotangent,
        high,
        smem=1,
    )
    b3, qb2 = onward(b2), sibling(b2)
    a4, qa3 = onward(after(a3[:rows], b2, qa1)), sibling(a3)
    b4, qb3 = onward(after(b3[:rows], qb1)), sibling(b3)
    qa4 = sibling(a4)
    ones = [a0, a1, a2, a3, a4, qa1, qa2, qa3, qa4]
    n = len(ones)

    pre, act, act_t = kernel(
        functools.partial(first_kernel, n),
        "first",
        8,
        1,
        (
            shape((depth * area, channels), F32),
            shape((depth * area, channels), BF),
            shape((channels, depth * area), BF),
        ),
        [weights],
        after(sx, b3),
        near,
        *ones,
    )
    qb4 = sibling(after(b4, act_t))
    twos = [b0, b1, b2, b3, b4, qb1, qb2, qb3, qb4]
    keep_two, send_two = kernel(
        grad_two_kernel, "grad_two", 8, 1, shards, [weights], sc, act_t
    )
    got_two = sibling(send_two)

    def both(keep, got, lo, hi):
        return keep[lo * rows : hi * rows].astype(F32) + got[lo * rows : hi * rows].astype(F32)

    def step(keep, got, moving, k):
        if k == 0:
            return both(keep, got, 0, 1).astype(BF)
        if k == 1:
            moving = jnp.concatenate([moving, jnp.zeros_like(moving)])
        return (both(keep, got, 2 * k - 1, 2 * k + 1) + moving.astype(F32)).astype(BF)

    def finish(keep, got, message):
        total = both(keep, got, 7, 8) + onward(message[:rows]).astype(F32)
        return (total + scatter_across(message[rows:]).astype(F32)) * loss_scale

    delta = kernel(
        functools.partial(back_kernel, n),
        "back",
        8,
        1,
        shape((depth, ny + 2, nz, 3 * channels), BF),
        [weights],
        sc,
        pre,
        near,
        *twos,
    )
    keep_one, send_one = kernel(
        grad_one_kernel, "grad_one", 8, 1, shards, [weights], delta, in_t
    )
    two = onward(step(keep_two, after(got_two, keep_one), None, 0))
    got_one = sibling(send_one)
    one = onward(step(keep_one, got_one, None, 0))
    features_out = kernel(
        functools.partial(third_kernel, n),
        "third",
        14,
        1,
        shape(features.shape, BF),
        [weights, weights, scratch((depth + 2, ny + 2, nz, 3 * channels), BF)],
        sx,
        after(act, two, one),
        near,
        *ones,
        *twos,
    )
    two = onward(step(keep_two, got_two, two, 1))
    one = onward(step(keep_one, got_one, one, 1))
    two = onward(step(keep_two, got_two, two, 2))
    one = onward(step(keep_one, got_one, after(one, features_out), 2))
    grad_two = finish(keep_two, got_two, step(keep_two, got_two, two, 3))
    return (features_out, finish(keep_one, got_one, step(keep_one, got_one, one, 3)), grad_two)


def solution(mesh):
    placed = (
        P(("groups", "tiles"), None, None, None),
        P("tiles", None),
        P("tiles", None),
        P(("groups", "tiles"), None, None, None),
        P("groups", None, None),
    )
    on_device = on_ring if mesh.shape["tiles"] == 2 * len(RING) else on_any
    return jax.shard_map(
        on_device,
        mesh=mesh,
        in_specs=placed,
        out_specs=(
            P(("groups", "tiles"), None, None, None),
            P(("groups", "tiles"), None),
            P(("groups", "tiles"), None),
        ),
        check_vma=False,
    )
```
